256 devices in a mesh: mem: 64 (over x, z, core), reg: 4 (over y).
Axes of the slice: x: 4, y: 4, z: 8, core: 2. Of those that a mesh axis runs over, the one named last changes fastest.
Arguments:
- background: bfloat16 [256, 4, 512, 128], P('mem', 'reg'), may hold values from -6 to 6
- obs_value: float32 [128, 8, 512], P('mem', 'reg'), may hold values from -6 to 6
- obs_error: float32 [128, 8, 512], P('mem', 'reg'), may hold values from 1 to 4
- obs_patch: int32 [128, 8, 512], P('mem', 'reg'), may hold values from 0 to 7
- obs_variable: int32 [128, 8, 512], P('mem', 'reg'), may hold values from 0 to 127
- obs_count: int32 [128, 8], P('mem', 'reg'), may hold values from 1 to 512
- patch_corners: int32 [4, 512, 4], P('reg', 'mem'), may hold values from 0 to 8, as said below
- interp_weights: float32 [4, 512, 4], P('reg', 'mem'), may hold values from 0 to 1, as said below
Outputs:
- analysis: bfloat16 [256, 4, 512, 128], P('mem', 'reg')
The draws below stay inside these ranges and needn't reach their ends.
Inputs may be any that keep to these rules, and one draw needn't show every extreme that they name: `patch_corners`: each patch's four numbers are base, base + 3, base + 1, base + 4 with base = i * 3 + e, i below 2 and e below 2; in the last region e is below 1. `interp_weights`: the four weights of a patch are non-negative and sum to one.
All inputs are finite; a program needn't handle non-finite values.
Results may differ from the reference program's by a relative error of at most 0.006.
Values may be sent and summed in bfloat16 or wider, within the bound.
No kernel may reach another device: no remote copies, remote signals or barrier semaphores. Data moves between devices by JAX's collectives and lax.ppermute only.
A program may use at most 64 MiB of HBM per device.

```python
import math
import jax
import jax.numpy as jnp
from jax import lax

K = 256
NV = 128
P_DEV = 8
CA = 2
CB = 2
OBS_MAX = 512
NS_ITERS = 4
NREG = 4
NPR = 512
NCA = 128
NCB = 8
N_MEM = 64


def draw_obs_count(key, part):
    level = jax.random.randint(jax.random.fold_in(key, 11), (NCA // CA, NCB // CB), 1, 5)
    ceiling = level * OBS_MAX // 4
    ceiling = jnp.repeat(jnp.repeat(ceiling, CA, axis=0), CB, axis=1)
    lowest = jnp.maximum(ceiling // 2, 1)
    spread = jax.random.randint(jax.random.fold_in(key, 12), (NCA, NCB), 0, OBS_MAX + 1)
    return (lowest + spread % (ceiling - lowest + 1)).astype(jnp.int32)


def draw_patch_corners(key, part):
    row_cell = jax.random.randint(jax.random.fold_in(key, 21), (NREG, NPR), 0, CA)
    raw_cell = jax.random.randint(jax.random.fold_in(key, 22), (NREG, NPR), 0, 64 * CB * CB)
    region = jnp.arange(NREG)[:, None]
    limit = jnp.where(region == NREG - 1, CB - 1, CB)
    col_cell = raw_cell % limit
    base = row_cell * (CB + 1) + col_cell
    return jnp.stack([base, base + CB + 1, base + 1, base + CB + 2], axis=-1).astype(jnp.int32)


def draw_interp_weights(key, part):
    along = jax.random.uniform(jax.random.fold_in(key, 31), (NREG, NPR), jnp.float32)
    across = jax.random.uniform(jax.random.fold_in(key, 32), (NREG, NPR), jnp.float32)
    return jnp.stack([(1.0 - along) * (1.0 - across), along * (1.0 - across), (1.0 - along) * across, along * across], axis=-1).astype(jnp.float32)


def with_ends(drawn, key, smallest, largest):
    index_at = [jax.random.randint(jax.random.fold_in(key, axis), (), 0, length) for axis, length in enumerate(drawn.shape)]
    widest = drawn.shape.index(max(drawn.shape))
    neighbour = index_at[:widest] + [(index_at[widest] + 1) % drawn.shape[widest]] + index_at[widest + 1:]
    return drawn.at[tuple(index_at)].set(smallest).at[tuple(neighbour)].set(largest)


def levels(key, shape, pieces, least, high):
    gain, own = 1.0, jax.random.fold_in(key, 6)
    for position, parts in pieces:
        heights = jnp.exp(jax.random.uniform(jax.random.fold_in(own, position), (parts,), jnp.float32, least / len(pieces), high / len(pieces)))
        gain = gain * jnp.repeat(heights, shape[position] // parts).reshape([-1 if axis == position else 1 for axis in range(len(shape))])
    return gain


def noise(stream_key, shape, width, most, pieces=(), kind=jnp.bfloat16):
    entries = jax.random.normal(stream_key, shape, jnp.float32) * width
    if len(pieces) > 0:
        entries = levels(stream_key, shape, pieces, -0.22, 0.18) * entries
    return jnp.clip(entries, min=-most, max=most).astype(kind)


def setup_inputs(seed: int = 0) -> dict:
    arg_keys = jax.random.split(jax.random.key(seed), 9)
    background = noise(arg_keys[0], (K, NREG, NPR, NV), 1.0, 6.0, ((0, 64), (1, 4)))
    obs_value = noise(arg_keys[1], (NCA, NCB, OBS_MAX), 1.0, 6.0, ((0, 64), (1, 4)), jnp.float32)
    obs_error = jnp.clip(jnp.exp(math.log(4.0) - 1.3862944 * jax.random.uniform(arg_keys[2], (NCA, NCB, OBS_MAX), jnp.float32) ** levels(arg_keys[2], (NCA, NCB, OBS_MAX), ((0, 64), (1, 4)), -0.2, 0.2)), 1.0, 4.0)
    obs_patch = with_ends(jax.random.randint(arg_keys[3], (NCA, NCB, OBS_MAX), 0, P_DEV), jax.random.fold_in(arg_keys[3], 1), 0, P_DEV - 1).astype(jnp.int32)
    obs_variable = with_ends(jax.random.randint(arg_keys[4], (NCA, NCB, OBS_MAX), 0, NV), jax.random.fold_in(arg_keys[4], 1), 0, NV - 1).astype(jnp.int32)
    obs_count = draw_obs_count(jax.random.fold_in(arg_keys[8], 71), 0)
    patch_corners = draw_patch_corners(jax.random.fold_in(arg_keys[8], 71), 0)
    interp_weights = draw_interp_weights(jax.random.fold_in(arg_keys[8], 71), 0)
    return dict(background=background, obs_value=obs_value, obs_error=obs_error, obs_patch=obs_patch, obs_variable=obs_variable, obs_count=obs_count, patch_corners=patch_corners, interp_weights=interp_weights)


def analysis_weights(gram, obs_pert, obs_weight, innovation):
    identity = jnp.eye(K, dtype=jnp.float32)
    system = (K - 1.0) * identity + gram
    scaling = jnp.trace(system, axis1=1, axis2=2) / K
    iterate = system / scaling[:, None, None]
    inverse = jnp.broadcast_to(identity, system.shape)
    for iteration in range(NS_ITERS):
        factor = 1.5 * identity - 0.5 * jnp.einsum('nij,njk->nik', inverse, iterate, precision=lax.Precision.HIGHEST)
        new_iterate = jnp.einsum('nij,njk->nik', iterate, factor, precision=lax.Precision.HIGHEST)
        inverse = jnp.einsum('nij,njk->nik', factor, inverse, precision=lax.Precision.HIGHEST)
        iterate = new_iterate
    projected = jnp.einsum('kns,ns->nk', obs_pert, obs_weight * innovation, precision=lax.Precision.HIGHEST)
    once = jnp.einsum('nij,nj->ni', inverse, projected, precision=lax.Precision.HIGHEST)
    mean_weight = jnp.einsum('nij,nj->ni', inverse, once, precision=lax.Precision.HIGHEST) / scaling[:, None]
    spread = jnp.sqrt((K - 1.0) / scaling)[:, None, None] * inverse
    return (spread + mean_weight[:, :, None]).astype(jnp.bfloat16)

def reference(background, obs_value, obs_error, obs_patch, obs_variable, obs_count, patch_corners, interp_weights):
    column_region = (jnp.arange(NCB) // CB).astype(jnp.int32)

    def row_weights(packed):
        row_index, patch_row, variable_row, value_row, error_row, count_row = packed
        block_index = row_index // CA
        patch_index = (block_index * P_DEV + patch_row).astype(jnp.int32)
        observed = background[:, column_region[:, None], patch_index, variable_row].astype(jnp.float32)
        obs_mean = lax.optimization_barrier(jnp.mean(observed, axis=0))
        obs_pert = observed - obs_mean
        innovation = value_row - obs_mean
        slot_index = jnp.arange(OBS_MAX)
        obs_weight = jnp.where(slot_index[None, :] < count_row[:, None], 1.0 / error_row, 0.0)
        gram = jnp.einsum('kns,jns->nkj', obs_pert * obs_weight[None], obs_pert, precision=lax.Precision.HIGHEST)
        return analysis_weights(gram, obs_pert, obs_weight, innovation)
    weights = lax.map(row_weights, (jnp.arange(NCA).astype(jnp.int32), obs_patch, obs_variable, obs_value, obs_error, obs_count))

    def block_update(block_id):
        region = (block_id // N_MEM).astype(jnp.int32)
        block_index = (block_id % N_MEM).astype(jnp.int32)
        first = (block_index * P_DEV).astype(jnp.int32)
        zero = jnp.zeros((), jnp.int32)
        ensemble = lax.dynamic_slice(background, (zero, region, first, zero), (K, 1, P_DEV, NV))[:, 0]
        corners = lax.dynamic_slice(patch_corners, (region, first, zero), (1, P_DEV, 4))[0]
        coeffs = lax.dynamic_slice(interp_weights, (region, first, zero), (1, P_DEV, 4))[0]
        centre = lax.optimization_barrier(jnp.mean(ensemble.astype(jnp.float32), axis=0))
        perturb = (ensemble.astype(jnp.float32) - centre).astype(jnp.bfloat16)
        coarse_row = ((block_index * CA + corners // (CB + 1)) % NCA).astype(jnp.int32)
        coarse_col = (region * CB + corners % (CB + 1)).astype(jnp.int32)
        chosen = weights[coarse_row, coarse_col].astype(jnp.float32)
        product = jnp.einsum('pcjk,jpv->pckv', chosen, perturb.astype(jnp.float32), precision=lax.Precision.HIGHEST)
        increment = jnp.einsum('pc,pckv->kpv', coeffs, product, precision=lax.Precision.HIGHEST)
        return (centre[None] + increment).astype(jnp.bfloat16)
    blocks = lax.map(block_update, jnp.arange(NREG * N_MEM).astype(jnp.int32))
    blocks = blocks.reshape(NREG, N_MEM, K, P_DEV, NV)
    return jnp.transpose(blocks, (2, 0, 1, 3, 4)).reshape(K, NREG, NPR, NV)
```

```python
import jax
import jax.numpy as jnp
from jax import lax
from jax.experimental import pallas as pl
from jax.experimental.pallas import tpu as pltpu
from jax.sharding import PartitionSpec as P

NS_ITERS = 4
F32 = jnp.float32
BF16 = jnp.bfloat16
VMEM = pl.BlockSpec(memory_space=pltpu.VMEM)
SMEM = pl.BlockSpec(memory_space=pltpu.SMEM)
NN = (((1,), (0,)), ((), ()))
NT = (((1,), (1,)), ((), ()))


def dot(a, b, dims=NN):
    return lax.dot_general(a, b, dims, preferred_element_type=F32)


def split(x):
    high = x.astype(BF16)
    return high, (x - high.astype(F32)).astype(BF16)


def thirds(x):
    high = x.astype(BF16)
    rest = x - high.astype(F32)
    middle = rest.astype(BF16)
    return high, middle, (rest - middle.astype(F32)).astype(BF16)


def product(a, b):
    return dot(a[0], b[0]) + (dot(a[0], b[1]) + dot(a[1], b[0]))


def prepare_kernel(count_ref, value_ref, error_ref, patch_ref, var_ref, corner_ref, coeff_ref, dense_ref, value_out_ref, mix_ref):
    rows, cols, slots = value_ref.shape
    patches, fields = dense_ref.shape[1:]
    slot_index = lax.broadcasted_iota(jnp.int32, (1, slots), 1)
    field_index = lax.broadcasted_iota(jnp.int32, (fields, slots), 0)
    patch_index = lax.broadcasted_iota(jnp.int32, (patches, slots), 0)
    for a in range(rows):
        for b in range(cols):
            weight = jnp.where(slot_index < count_ref[a, b], 1.0 / error_ref[a, b : b + 1, :], 0.0)
            weighted = weight * value_ref[a, b : b + 1, :]
            chosen = (field_index == var_ref[a, b : b + 1, :]).astype(F32).astype(BF16)
            at_patch = patch_index == patch_ref[a, b : b + 1, :]
            left = jnp.concatenate([jnp.where(at_patch, x, 0.0) for x in (weight, weighted)], axis=0)
            high, middle, low = (dot(x, chosen, NT) for x in thirds(left))
            sums = high + (middle + low)
            dense_ref[a * cols + b] = sums[:patches]
            value_out_ref[a * cols + b] = sums[patches:]
    corners, coeffs = corner_ref[...], coeff_ref[...]
    for t in range(mix_ref.shape[0]):
        used = jnp.sum(jnp.where(corners == t, coeffs, 0.0), axis=1, keepdims=True)
        mix_ref[t] = jnp.broadcast_to(used, (patches, fields))


def weights_of(points, high_ref, low_ref, centre, dense_ref, value_ref, out_ref, left_high, left_low):
    members = high_ref.shape[0]
    patches, fields = centre.shape
    row = lax.broadcasted_iota(jnp.int32, (members, members), 0)
    col = lax.broadcasted_iota(jnp.int32, (members, members), 1)
    diagonal = row == col
    identity = diagonal.astype(F32)
    state = []
    for slot, n in enumerate(points):
        dense = dense_ref[n]
        pull = value_ref[n] - dense * centre
        for p in range(patches):
            lanes = slice(p * fields, (p + 1) * fields)
            scaled = (high_ref[:, lanes].astype(F32) + low_ref[:, lanes].astype(F32)) * dense[p : p + 1, :]
            left_high[slot, :members, lanes], left_low[slot, :members, lanes] = split(scaled)
            tail = jnp.broadcast_to(pull[p : p + 1, :], (left_high.shape[1] - members, fields))
            left_high[slot, members:, lanes], left_low[slot, members:, lanes] = split(tail)
    for slot, n in enumerate(points):
        high, low = high_ref[...], low_ref[...]
        both = dot(left_high[slot], high, NT) + (dot(left_high[slot], low, NT) + dot(left_low[slot], high, NT))
        gram, projected = both[:members], both[members : members + 1]
        system = (members - 1.0) * identity + gram
        trace = jnp.sum(jnp.sum(jnp.where(diagonal, system, 0.0), axis=0, keepdims=True), axis=1, keepdims=True)
        scaling = trace / members
        state.append((projected, scaling, system * (1.0 / scaling)))
    iterates, inverses = [], []
    for _, _, start in state:
        parts = split(start)
        iterates.append(1.5 * start - 0.5 * product(parts, parts))
        inverses.append(1.5 * identity - 0.5 * start)
    for step in range(1, NS_ITERS):
        z = [split(x) for x in inverses]
        y = [split(x) for x in iterates]
        factors = [split(1.5 * identity - 0.5 * product(zz, yy)) for zz, yy in zip(z, y)]
        if step < NS_ITERS - 1:
            iterates = [product(yy, ff) for yy, ff in zip(y, factors)]
        inverses = [product(ff, zz) for ff, zz in zip(factors, z)]
    for slot, (projected, scaling, _) in enumerate(state):
        inverse = inverses[slot]
        once = jnp.sum(inverse * projected, axis=1, keepdims=True)
        twice = jnp.sum(inverse * once, axis=0, keepdims=True) / scaling
        out_ref[slot] = (jnp.sqrt((members - 1.0) / scaling) * inverse + twice).astype(BF16)


def first_kernel(ensemble_ref, dense_ref, value_ref, out_ref, high_ref, low_ref, centre_ref, pert_ref, left_high, left_low):
    members, patches, fields = ensemble_ref.shape
    total = jnp.zeros((patches, fields), F32)
    chunk = 32
    for k in range(0, members, chunk):
        total = total + jnp.sum(ensemble_ref[k : k + chunk].astype(F32), axis=0)
    centre = total * (1.0 / members)
    centre_ref[...] = centre
    for k in range(0, members, chunk):
        part = ensemble_ref[k : k + chunk].astype(F32) - centre
        pert_ref[k * patches : (k + chunk) * patches] = part.reshape(chunk * patches, fields)
    for p in range(patches):
        lanes = slice(p * fields, (p + 1) * fields)
        high_ref[:, lanes], low_ref[:, lanes] = split(pert_ref[pl.ds(p, members, stride=patches), :])
    weights_of((0, 2), high_ref, low_ref, centre, dense_ref, value_ref, out_ref, left_high, left_low)


def second_kernel(high_ref, low_ref, centre_ref, dense_ref, value_ref, out_ref, left_high, left_low):
    weights_of((1, 3), high_ref, low_ref, centre_ref[...], dense_ref, value_ref, out_ref, left_high, left_low)


def blend(parts, high_ref, mix_ref, p):
    fields = mix_ref.shape[2]
    lanes = slice(p * fields, (p + 1) * fields)
    total = None
    for t, ref, slot in parts:
        share = mix_ref[t, p : p + 1, :]
        moved = dot(ref[slot], high_ref[:, lanes])
        moved = jnp.where(share != 0.0, share * moved, 0.0)
        total = moved if total is None else total + moved
    return total


def own_kernel(one_ref, two_ref, beside_ref, high_ref, mix_ref, out_ref):
    parts = ((0, one_ref, 0), (3, one_ref, 1), (1, two_ref, 0), (4, two_ref, 1), (2, beside_ref, 0), (5, beside_ref, 1))
    fields = mix_ref.shape[2]
    for p in range(mix_ref.shape[1]):
        out_ref[:, p * fields : (p + 1) * fields] = blend(parts, high_ref, mix_ref, p)


def last_kernel(below_ref, high_ref, mix_ref, partial_ref, centre_ref, out_ref, all_ref):
    parts = ((6, below_ref, 0), (7, below_ref, 1), (8, below_ref, 2))
    members, patches, fields = out_ref.shape
    for p in range(patches):
        lanes = slice(p * fields, (p + 1) * fields)
        total = partial_ref[:, lanes] + blend(parts, high_ref, mix_ref, p)
        all_ref[pl.ds(p, members, stride=patches), :] = total + centre_ref[p : p + 1, :]
    chunk = 32
    for k in range(0, members, chunk):
        part = all_ref[k * patches : (k + chunk) * patches, :]
        out_ref[k : k + chunk] = part.reshape(chunk, patches, fields).astype(BF16)


def call(kernel, outs, specs, scratch=()):
    return pl.pallas_call(
        kernel,
        out_shape=outs,
        in_specs=specs,
        out_specs=jax.tree.map(lambda _: VMEM, outs),
        scratch_shapes=list(scratch),
        compiler_params=pltpu.CompilerParams(vmem_limit_bytes=48 << 20),
    )


def per_device(background, obs_value, obs_error, obs_patch, obs_variable, obs_count, patch_corners, interp_weights):
    shape = jax.ShapeDtypeStruct
    devices = lax.axis_size("mem")
    regions = lax.axis_size("reg")
    own, _, all_patches, fields = background.shape
    patches = all_patches // devices
    members = own * devices
    points = obs_value.shape[0] * obs_value.shape[1]
    columns = patches * fields

    outgoing = jnp.transpose(background.reshape(own, devices, patches, fields), (1, 0, 2, 3))
    ensemble = lax.all_to_all(outgoing, "mem", split_axis=0, concat_axis=0, tiled=True).reshape(members, patches, fields)
    dense, values, mix = call(
        prepare_kernel,
        (shape((points, patches, fields), F32), shape((points, patches, fields), F32), shape((9, patches, fields), F32)),
        [SMEM] + [VMEM] * 6,
    )(obs_count, obs_value, obs_error, obs_patch, obs_variable, patch_corners[0], interp_weights[0])

    pair = shape((2, members, members), BF16)
    lefts = [pltpu.VMEM((2, members + 16, columns), BF16)] * 2
    one, high, low, centre = call(
        first_kernel,
        (pair, shape((members, columns), BF16), shape((members, columns), BF16), shape((patches, fields), F32)),
        [VMEM] * 3,
        [pltpu.VMEM((members * patches, fields), F32)] + lefts,
    )(ensemble, dense, values)
    beside = lax.ppermute(one, "reg", [(r + 1, r) for r in range(regions - 1)])
    two = call(second_kernel, pair, [VMEM] * 5, lefts)(high, low, centre, dense, values)
    top = jnp.stack([one[0], two[0], beside[0]])
    below = lax.ppermute(top, "mem", [((d + 1) % devices, d) for d in range(devices)])
    partial = call(own_kernel, shape((members, columns), F32), [VMEM] * 5)(one, two, beside, high, mix)
    analysis = call(
        last_kernel,
        shape((members, patches, fields), BF16),
        [VMEM] * 5,
        [pltpu.VMEM((members * patches, fields), F32)],
    )(below, high, mix, partial, centre)
    returned = lax.all_to_all(analysis.reshape(devices, own, patches, fields), "mem", split_axis=0, concat_axis=0, tiled=True)
    return jnp.transpose(returned, (1, 0, 2, 3)).reshape(own, 1, all_patches, fields)


def solution(mesh):
    placed = (
        P("mem", "reg", None, None),
        P("mem", "reg", None),
        P("mem", "reg", None),
        P("mem", "reg", None),
        P("mem", "reg", None),
        P("mem", "reg"),
        P("reg", "mem", None),
        P("reg", "mem", None),
    )
    return jax.shard_map(
        per_device,
        mesh=mesh,
        in_specs=placed,
        out_specs=P("mem", "reg", None, None),
        check_vma=False,
    )
```

```python
import jax
import jax.numpy as jnp
from jax import lax
from jax.experimental import pallas as pl
from jax.experimental.pallas import tpu as pltpu
from jax.sharding import PartitionSpec as P

F32 = jnp.float32
BF16 = jnp.bfloat16
VMEM = pl.BlockSpec(memory_space=pltpu.VMEM)
SMEM = pl.BlockSpec(memory_space=pltpu.SMEM)
HBM = pl.BlockSpec(memory_space=pltpu.HBM)
NN = (((1,), (0,)), ((), ()))
NT = (((1,), (1,)), ((), ()))


def dot(a, b, dims=NN):
    return lax.dot_general(a, b, dims, preferred_element_type=F32)


def split(x):
    high = x.astype(BF16)
    return high, (x - high.astype(F32)).astype(BF16)


def thirds(x):
    high = x.astype(BF16)
    rest = x - high.astype(F32)
    middle = rest.astype(BF16)
    return high, middle, (rest - middle.astype(F32)).astype(BF16)


def product(a, b):
    return dot(a[0], b[0]) + (dot(a[0], b[1]) + dot(a[1], b[0]))


def prepare_kernel(count_ref, value_ref, error_ref, patch_ref, var_ref, corner_ref, coeff_ref, dense_ref, value_out_ref, mix_ref):
    rows, cols, slots = value_ref.shape
    patches, fields = dense_ref.shape[1:]
    slot_index = lax.broadcasted_iota(jnp.int32, (1, slots), 1)
    field_index = lax.broadcasted_iota(jnp.int32, (fields, slots), 0)
    patch_index = lax.broadcasted_iota(jnp.int32, (patches, slots), 0)
    for a in range(rows):
        for b in range(cols):
            weight = jnp.where(slot_index < count_ref[a, b], 1.0 / error_ref[a, b : b + 1, :], 0.0)
            weighted = weight * value_ref[a, b : b + 1, :]
            chosen = (field_index == var_ref[a, b : b + 1, :]).astype(F32).astype(BF16)
            at_patch = patch_index == patch_ref[a, b : b + 1, :]
            left = jnp.concatenate([jnp.where(at_patch, x, 0.0) for x in (weight, weighted)], axis=0)
            high, middle, low = (dot(x, chosen, NT) for x in thirds(left))
            sums = high + (middle + low)
            dense_ref[a * cols + b] = sums[:patches]
            value_out_ref[a * cols + b] = sums[patches:]
    corners, coeffs = corner_ref[...], coeff_ref[...]
    for t in range(mix_ref.shape[0]):
        used = jnp.sum(jnp.where(corners == t, coeffs, 0.0), axis=1, keepdims=True)
        mix_ref[t] = jnp.broadcast_to(used, (patches, fields))


def shares(points, x_ref, centre, dense_ref, value_ref, left_high, left_low):
    members = x_ref.shape[0]
    patches, fields = centre.shape
    for slot, n in enumerate(points):
        dense = dense_ref[n]
        pull = value_ref[n] - dense * centre
        for p in range(patches):
            lanes = slice(p * fields, (p + 1) * fields)
            scaled = (x_ref[:, lanes].astype(F32) - centre[p : p + 1, :]) * dense[p : p + 1, :]
            left_high[slot, :members, lanes], left_low[slot, :members, lanes] = split(scaled)
            tail = jnp.broadcast_to(pull[p : p + 1, :], (left_high.shape[1] - members, fields))
            left_high[slot, members:, lanes], left_low[slot, members:, lanes] = split(tail)


def two_factors(x, square):
    return 0.375 * square - 0.5 * x + product(split(square), split(0.0625 * square - 0.3125 * x))


def weights_of(count, x_ref, left_high, left_low, out_ref):
    members = x_ref.shape[0]
    row = lax.broadcasted_iota(jnp.int32, (members, members), 0)
    col = lax.broadcasted_iota(jnp.int32, (members, members), 1)
    diagonal = row == col
    slots = range(count)
    state = []
    for slot in slots:
        columns = x_ref[...]
        both = dot(left_high[slot], columns, NT) + dot(left_low[slot], columns, NT)
        both = both - jnp.sum(both, axis=1, keepdims=True) * (1.0 / members)
        gram, projected = both[:members], both[members : members + 1]
        trace = jnp.sum(jnp.sum(jnp.where(diagonal, gram, 0.0), axis=0, keepdims=True), axis=1, keepdims=True)
        scaling = (members - 1.0) + trace / members
        inverse_scaling = 1.0 / scaling
        state.append((projected, scaling, gram * inverse_scaling + jnp.where(diagonal, (members - 1.0) * inverse_scaling - 1.0, 0.0)))
    r = [split(x) for _, _, x in state]
    squares = [product(x, x) for x in r]
    w = [two_factors(state[s][2], squares[s]) for s in slots]
    w_parts = [split(x) for x in w]
    v = [state[s][2] + w[s] + product(r[s], w_parts[s]) for s in slots]
    e = [v[s] + w[s] + product(split(v[s]), w_parts[s]) for s in slots]
    e_parts = [split(x) for x in e]
    squares = [product(x, x) for x in e_parts]
    h = [two_factors(e[s], squares[s]) for s in slots]
    inverses = [w[s] + h[s] + product(w_parts[s], split(h[s])) for s in slots]
    half = members // 2
    small_row, small_col = row[:half, :half], col[:half, :half]
    tail_row = lax.broadcasted_iota(jnp.int32, (16, members), 0)
    for slot in slots:
        projected, scaling, _ = state[slot]
        inverse = inverses[slot] + jnp.where(diagonal, 1.0, 0.0)
        once = jnp.sum(inverse * projected, axis=1, keepdims=True)
        twice = jnp.sum(inverse * once, axis=0, keepdims=True) / scaling
        spread = jnp.sqrt((members - 1.0) / scaling) * inverse
        out_ref[slot] = (spread + twice).astype(BF16)
        yield slot, spread, twice, half, small_row, small_col, tail_row


def pack(target, slot, spread, twice, half, small_row, small_col, tail_row):
    corner = spread[half:, half:]
    target[slot, :half, :half] = jnp.where(small_row >= small_col, spread[:half, :half], corner).astype(BF16)
    target[slot, :half, half:] = spread[:half, half:].astype(BF16)
    on_diagonal = jnp.sum(jnp.where(small_row == small_col, corner, 0.0), axis=0, keepdims=True)
    high, low = split(twice)
    rows = jnp.where(tail_row == 1, high.astype(F32), jnp.where(tail_row == 2, low.astype(F32), 0.0))
    first = jnp.concatenate([on_diagonal, jnp.zeros_like(on_diagonal)], axis=1)
    target[slot, half:, :] = jnp.where(tail_row == 0, first, rows).astype(BF16)


def unpack(source, slot, target, place):
    half = source.shape[1] - 16
    row = lax.broadcasted_iota(jnp.int32, (half, half), 0)
    col = lax.broadcasted_iota(jnp.int32, (half, half), 1)
    mixed = source[slot, :half, :half].astype(F32)
    across = source[slot, :half, half:].astype(F32)
    tail = source[slot, half:, :].astype(F32)
    mean = tail[1:2] + tail[2:3]
    left, right = mean[:, :half], mean[:, half:]
    turned = mixed.T
    target[place, :half, :half] = (jnp.where(row >= col, mixed, turned) + left).astype(BF16)
    target[place, :half, half:] = (across + right).astype(BF16)
    target[place, half:, :half] = (across.T + left).astype(BF16)
    corner = jnp.where(row < col, mixed, jnp.where(row == col, tail[0:1, :half], turned))
    target[place, half:, half:] = (corner + right).astype(BF16)


def first_kernel(ensemble_ref, dense_ref, value_ref, out_ref, pack_ref, x_ref, high_ref, centre_ref, wide_ref, left_high, left_low):
    members, patches, fields = ensemble_ref.shape
    total = jnp.zeros((patches, fields), F32)
    chunk = 32
    for k in range(0, members, chunk):
        part = ensemble_ref[k : k + chunk].astype(F32)
        total = total + jnp.sum(part, axis=0)
        wide_ref[k * patches : (k + chunk) * patches] = part.reshape(chunk * patches, fields)
    centre = total * (1.0 / members)
    centre_ref[...] = centre
    for p in range(patches):
        lanes = slice(p * fields, (p + 1) * fields)
        part = wide_ref[pl.ds(p, members, stride=patches), :]
        x_ref[:, lanes] = part.astype(BF16)
        high_ref[:, lanes] = (part - centre[p : p + 1, :]).astype(BF16)
    shares((0, 2), x_ref, centre, dense_ref, value_ref, left_high, left_low)
    for slot, *rest in weights_of(2, x_ref, left_high, left_low, out_ref):
        pack(pack_ref, slot, *rest)


def second_kernel(x_ref, centre_ref, dense_ref, value_ref, sent_ref, out_ref, pack_ref, left_high, left_low):
    shares((1, 3), x_ref, centre_ref[...], dense_ref, value_ref, left_high, left_low)
    pack_ref[0] = sent_ref[0]
    for slot, *rest in weights_of(2, x_ref, left_high, left_low, out_ref):
        if slot == 0:
            pack(pack_ref, 1, *rest)
    pack_ref[2] = jnp.zeros(pack_ref.shape[1:], BF16)


def blend(parts, high_ref, mix_ref, p):
    fields = mix_ref.shape[2]
    lanes = slice(p * fields, (p + 2) * fields)
    total = None
    for t, ref, slot in parts:
        share = jnp.concatenate([mix_ref[t, p : p + 1, :], mix_ref[t, p + 1 : p + 2, :]], axis=1)
        moved = dot(ref[slot], high_ref[:, lanes])
        moved = jnp.where(share != 0.0, share * moved, 0.0)
        total = moved if total is None else total + moved
    return total


def own_kernel(one_ref, two_ref, beside_ref, high_ref, mix_ref, out_ref, whole_ref):
    unpack(beside_ref, 0, whole_ref, 0)
    unpack(beside_ref, 1, whole_ref, 1)
    parts = ((0, one_ref, 0), (3, one_ref, 1), (1, two_ref, 0), (4, two_ref, 1), (2, whole_ref, 0), (5, whole_ref, 1))
    fields = mix_ref.shape[2]
    for p in range(0, mix_ref.shape[1], 2):
        out_ref[:, p * fields : (p + 2) * fields] = blend(parts, high_ref, mix_ref, p)


def last_kernel(below_ref, high_ref, mix_ref, partial_ref, centre_ref, out_ref, all_ref, whole_ref):
    for slot in range(3):
        unpack(below_ref, slot, whole_ref, slot)
    parts = ((6, whole_ref, 0), (7, whole_ref, 1), (8, whole_ref, 2))
    members, patches, fields = out_ref.shape
    for p in range(0, patches, 2):
        lanes = slice(p * fields, (p + 2) * fields)
        total = partial_ref[:, lanes] + blend(parts, high_ref, mix_ref, p)
        for q in range(2):
            part = total[:, q * fields : (q + 1) * fields] + centre_ref[p + q : p + q + 1, :]
            all_ref[pl.ds(p + q, members, stride=patches), :] = part
    chunk = 32
    for k in range(0, members, chunk):
        part = all_ref[k * patches : (k + chunk) * patches, :]
        out_ref[k : k + chunk] = part.reshape(chunk, patches, fields).astype(BF16)


def outgoing_kernel(source_ref, target_ref, done):
    copies = [pltpu.make_async_copy(source_ref.at[m], target_ref.at[:, m], done.at[m]) for m in range(source_ref.shape[0])]
    for copy in copies:
        copy.start()
    for copy in copies:
        copy.wait()


def returned_kernel(source_ref, target_ref, done):
    copies = [pltpu.make_async_copy(source_ref.at[:, m], target_ref.at[m], done.at[m]) for m in range(target_ref.shape[0])]
    for copy in copies:
        copy.start()
    for copy in copies:
        copy.wait()


def call(kernel, outs, specs, scratch=(), to=VMEM):
    return pl.pallas_call(
        kernel,
        out_shape=outs,
        in_specs=specs,
        out_specs=jax.tree.map(lambda _: to, outs),
        scratch_shapes=list(scratch),
        compiler_params=pltpu.CompilerParams(vmem_limit_bytes=48 << 20),
    )


def per_device(background, obs_value, obs_error, obs_patch, obs_variable, obs_count, patch_corners, interp_weights):
    shape = jax.ShapeDtypeStruct
    devices = lax.axis_size("mem")
    regions = lax.axis_size("reg")
    own, _, all_patches, fields = background.shape
    patches = all_patches // devices
    members = own * devices
    points = obs_value.shape[0] * obs_value.shape[1]
    columns = patches * fields
    copies = [pltpu.SemaphoreType.DMA((own,))]

    outgoing = call(outgoing_kernel, shape((devices, own, patches, fields), BF16), [HBM], copies, HBM)(
        pltpu.with_memory_space_constraint(background.reshape(own, devices, patches, fields), pltpu.HBM)
    )
    ensemble = lax.all_to_all(outgoing, "mem", split_axis=0, concat_axis=0, tiled=True).reshape(members, patches, fields)
    dense, values, mix = call(
        prepare_kernel,
        (shape((points, patches, fields), F32), shape((points, patches, fields), F32), shape((9, patches, fields), F32)),
        [SMEM] + [VMEM] * 6,
    )(obs_count, obs_value, obs_error, obs_patch, obs_variable, patch_corners[0], interp_weights[0])

    pair = shape((2, members, members), BF16)
    packed = (members // 2 + 16, members)
    lefts = [pltpu.VMEM((2, members + 16, columns), BF16)] * 2
    wide = pltpu.VMEM((members * patches, fields), F32)
    one, sent, x, high, centre = call(
        first_kernel,
        (pair, shape((2,) + packed, BF16), shape((members, columns), BF16), shape((members, columns), BF16), shape((patches, fields), F32)),
        [VMEM] * 3,
        [wide] + lefts,
    )(ensemble, dense, values)
    beside = lax.ppermute(sent, "reg", [(r + 1, r) for r in range(regions - 1)])
    two, top = call(second_kernel, (pair, shape((3,) + packed, BF16)), [VMEM] * 5, lefts)(x, centre, dense, values, sent)
    top = lax.dynamic_update_slice(top, beside[:1], (2, 0, 0))
    below = lax.ppermute(top, "mem", [((d + 1) % devices, d) for d in range(devices)])
    whole = pltpu.VMEM((3, members, members), BF16)
    partial = call(own_kernel, shape((members, columns), F32), [VMEM] * 5, [whole])(one, two, beside, high, mix)
    analysis = call(last_kernel, shape((members, patches, fields), BF16), [VMEM] * 5, [wide, whole])(below, high, mix, partial, centre)
    returned = lax.all_to_all(analysis.reshape(devices, own, patches, fields), "mem", split_axis=0, concat_axis=0, tiled=True)
    result = call(returned_kernel, shape((own, devices, patches, fields), BF16), [VMEM], copies, HBM)(returned)
    return result.reshape(own, 1, all_patches, fields)


def solution(mesh):
    placed = (
        P("mem", "reg", None, None),
        P("mem", "reg", None),
        P("mem", "reg", None),
        P("mem", "reg", None),
        P("mem", "reg", None),
        P("mem", "reg"),
        P("reg", "mem", None),
        P("reg", "mem", None),
    )
    return jax.shard_map(
        per_device,
        mesh=mesh,
        in_specs=placed,
        out_specs=P("mem", "reg", None, None),
        check_vma=False,
    )
```

```python
import jax
import jax.numpy as jnp
from jax import lax
from jax.experimental import pallas as pl
from jax.experimental.pallas import tpu as pltpu
from jax.sharding import PartitionSpec as P


F32 = jnp.float32
BF16 = jnp.bfloat16
VMEM = pl.BlockSpec(memory_space=pltpu.VMEM)
SMEM = pl.BlockSpec(memory_space=pltpu.SMEM)
HBM = pl.BlockSpec(memory_space=pltpu.HBM)
NN = (((1,), (0,)), ((), ()))
NT = (((1,), (1,)), ((), ()))


def dot(a, b, dims=NN):
    return lax.dot_general(a, b, dims, preferred_element_type=F32)


def split(x):
    high = x.astype(BF16)
    return high, (x - high.astype(F32)).astype(BF16)


def thirds(x):
    high = x.astype(BF16)
    rest = x - high.astype(F32)
    middle = rest.astype(BF16)
    return high, middle, (rest - middle.astype(F32)).astype(BF16)


def product(a, b):
    return dot(a[0], b[0]) + (dot(a[0], b[1]) + dot(a[1], b[0]))


def prepare_kernel(count_ref, value_ref, error_ref, patch_ref, var_ref, corner_ref, coeff_ref, dense_ref, value_out_ref, mix_ref):
    rows, cols, slots = value_ref.shape
    patches, fields = dense_ref.shape[1:]
    slot_index = lax.broadcasted_iota(jnp.int32, (1, slots), 1)
    field_index = lax.broadcasted_iota(jnp.int32, (fields, slots), 0)
    patch_index = lax.broadcasted_iota(jnp.int32, (patches, slots), 0)
    for a in range(rows):
        for b in range(cols):
            weight = jnp.where(slot_index < count_ref[a, b], 1.0 / error_ref[a, b : b + 1, :], 0.0)
            weighted = weight * value_ref[a, b : b + 1, :]
            chosen = (field_index == var_ref[a, b : b + 1, :]).astype(F32).astype(BF16)
            at_patch = patch_index == patch_ref[a, b : b + 1, :]
            left = jnp.concatenate([jnp.where(at_patch, x, 0.0) for x in (weight, weighted)], axis=0)
            high, middle, low = (dot(x, chosen, NT) for x in thirds(left))
            sums = high + (middle + low)
            dense_ref[a * cols + b] = sums[:patches]
            value_out_ref[a * cols + b] = sums[patches:]
    corners, coeffs = corner_ref[...], coeff_ref[...]
    for t in range(mix_ref.shape[0]):
        used = jnp.sum(jnp.where(corners == t, coeffs, 0.0), axis=1, keepdims=True)
        mix_ref[t] = jnp.broadcast_to(used, (patches, fields))


def shares(points, pert_ref, centre, dense_ref, value_ref, left_high, left_low):
    members = pert_ref.shape[0]
    patches, fields = centre.shape
    pulls = [value_ref[n] - dense_ref[n] * centre for n in points]
    for p in range(patches):
        lanes = slice(p * fields, (p + 1) * fields)
        pert = pert_ref[:, lanes]
        for slot, n in enumerate(points):
            left_high[slot, :members, lanes], left_low[slot, :members, lanes] = split(pert * dense_ref[n, p : p + 1, :])
            tail = jnp.broadcast_to(pulls[slot][p : p + 1, :], (left_high.shape[1] - members, fields))
            left_high[slot, members:, lanes], left_low[slot, members:, lanes] = split(tail)


def add_diagonal(x, value, diagonal):
    half = diagonal.shape[0]
    step = jnp.where(diagonal, value, 0.0)
    top = jnp.concatenate([x[:half, :half] + step, x[:half, half:]], axis=1)
    bottom = jnp.concatenate([x[half:, :half], x[half:, half:] + step], axis=1)
    return jnp.concatenate([top, bottom], axis=0)


def two_factors(x, parts, diagonal):
    square = product(parts, parts)
    inner = add_diagonal(square - 4.5 * x, 6.75, diagonal)
    return add_diagonal(product(split(square), split(inner)) - 4.875 * x, 2.25, diagonal)


def weights_of(count, x_ref, left_high, left_low, out_ref):
    members = x_ref.shape[0]
    half = members // 2
    row = lax.broadcasted_iota(jnp.int32, (half, half), 0)
    col = lax.broadcasted_iota(jnp.int32, (half, half), 1)
    diagonal = row == col
    slots = range(count)
    state = []
    for slot in slots:
        columns = x_ref[...]
        both = dot(left_high[slot], columns, NT) + dot(left_low[slot], columns, NT)
        both = both - jnp.sum(both, axis=1, keepdims=True) * (1.0 / members)
        gram, projected = both[:members], both[members : members + 1]
        on_diagonal = jnp.where(diagonal, gram[:half, :half] + gram[half:, half:], 0.0)
        trace = jnp.sum(jnp.sum(on_diagonal, axis=0, keepdims=True), axis=1, keepdims=True)
        scaling = (members - 1.0) + trace / members
        half_inverse = 0.5 / scaling
        state.append((projected, scaling, add_diagonal(gram * half_inverse, (members - 1.0) * half_inverse, diagonal)))
    parts = [split(x) for _, _, x in state]
    z = [split(two_factors(state[s][2], parts[s], diagonal)) for s in slots]
    y = [split(product(parts[s], z[s])) for s in slots]
    c = [product(y[s], z[s]) for s in slots]
    f = [split(two_factors(c[s], split(c[s]), diagonal)) for s in slots]
    inverses = [product(f[s], z[s]) for s in slots]
    for slot in slots:
        projected, scaling, _ = state[slot]
        inverse = inverses[slot]
        once = jnp.sum(inverse * projected, axis=1, keepdims=True)
        twice = jnp.sum(inverse * once, axis=0, keepdims=True) / scaling
        spread = jnp.sqrt((members - 1.0) / scaling) * inverse
        out_ref[slot] = (spread + twice).astype(BF16)
        yield slot, spread, twice


def pack(target, slot, spread, twice):
    members = spread.shape[0]
    half = members // 2
    small_row = lax.broadcasted_iota(jnp.int32, (half, half), 0)
    small_col = lax.broadcasted_iota(jnp.int32, (half, half), 1)
    tail_row = lax.broadcasted_iota(jnp.int32, (16, members), 0)
    corner = spread[half:, half:]
    target[slot, :half, :half] = jnp.where(small_row >= small_col, spread[:half, :half], corner).astype(BF16)
    target[slot, :half, half:] = spread[:half, half:].astype(BF16)
    on_diagonal = jnp.sum(jnp.where(small_row == small_col, corner, 0.0), axis=0, keepdims=True)
    high, low = split(twice)
    rows = jnp.where(tail_row == 1, high.astype(F32), jnp.where(tail_row == 2, low.astype(F32), 0.0))
    first = jnp.concatenate([on_diagonal, jnp.zeros_like(on_diagonal)], axis=1)
    target[slot, half:, :] = jnp.where(tail_row == 0, first, rows).astype(BF16)


def unpack(source, slot, target, place):
    half = source.shape[1] - 16
    row = lax.broadcasted_iota(jnp.int32, (half, half), 0)
    col = lax.broadcasted_iota(jnp.int32, (half, half), 1)
    mixed = source[slot, :half, :half].astype(F32)
    across = source[slot, :half, half:].astype(F32)
    tail = source[slot, half:, :].astype(F32)
    mean = tail[1:2] + tail[2:3]
    left, right = mean[:, :half], mean[:, half:]
    turned = mixed.T
    target[place, :half, :half] = (jnp.where(row >= col, mixed, turned) + left).astype(BF16)
    target[place, :half, half:] = (across + right).astype(BF16)
    target[place, half:, :half] = (across.T + left).astype(BF16)
    corner = jnp.where(row < col, mixed, jnp.where(row == col, tail[0:1, :half], turned))
    target[place, half:, half:] = (corner + right).astype(BF16)


def first_kernel(ensemble_ref, dense_ref, value_ref, out_ref, pack_ref, corner_ref, x_ref, pert_ref, high_ref, centre_ref, wide_ref, left_high, left_low):
    members, patches, fields = ensemble_ref.shape
    total = jnp.zeros((patches, fields), F32)
    chunk = 32
    for k in range(0, members, chunk):
        part = ensemble_ref[k : k + chunk].astype(F32)
        total = total + jnp.sum(part, axis=0)
        wide_ref[k * patches : (k + chunk) * patches] = part.reshape(chunk * patches, fields)
    centre = total * (1.0 / members)
    centre_ref[...] = centre
    for p in range(patches):
        lanes = slice(p * fields, (p + 1) * fields)
        part = wide_ref[pl.ds(p, members, stride=patches), :]
        x_ref[:, lanes] = part.astype(BF16)
        pert = part - centre[p : p + 1, :]
        pert_ref[:, lanes] = pert
        high_ref[:, lanes] = pert.astype(BF16)
    shares((0, 2), pert_ref, centre, dense_ref, value_ref, left_high, left_low)
    for slot, spread, twice in weights_of(2, x_ref, left_high, left_low, out_ref):
        pack(pack_ref, slot, spread, twice)
        if slot == 0:
            corner_ref[0] = pack_ref[0]


def second_kernel(x_ref, pert_ref, centre_ref, dense_ref, value_ref, sent_ref, out_ref, pack_ref, left_high, left_low):
    pack_ref[0] = sent_ref[0]
    shares((1, 3), pert_ref, centre_ref[...], dense_ref, value_ref, left_high, left_low)
    for slot, spread, twice in weights_of(2, x_ref, left_high, left_low, out_ref):
        if slot == 0:
            pack(pack_ref, 1, spread, twice)


def blend(parts, high_ref, mix_ref, p):
    fields = mix_ref.shape[2]
    lanes = slice(p * fields, (p + 2) * fields)
    total = None
    for t, ref, slot in parts:
        share = jnp.concatenate([mix_ref[t, p : p + 1, :], mix_ref[t, p + 1 : p + 2, :]], axis=1)
        moved = dot(ref[slot], high_ref[:, lanes])
        moved = jnp.where(share != 0.0, share * moved, 0.0)
        total = moved if total is None else total + moved
    return total


def own_kernel(one_ref, two_ref, beside_ref, high_ref, mix_ref, out_ref, whole_ref):
    unpack(beside_ref, 0, whole_ref, 0)
    unpack(beside_ref, 1, whole_ref, 1)
    parts = ((0, one_ref, 0), (3, one_ref, 1), (1, two_ref, 0), (4, two_ref, 1), (2, whole_ref, 0), (5, whole_ref, 1))
    fields = mix_ref.shape[2]
    for p in range(0, mix_ref.shape[1], 2):
        out_ref[:, p * fields : (p + 2) * fields] = blend(parts, high_ref, mix_ref, p)


def last_kernel(below_ref, diagonal_ref, high_ref, mix_ref, partial_ref, centre_ref, out_ref, all_ref, whole_ref):
    unpack(below_ref, 0, whole_ref, 0)
    unpack(below_ref, 1, whole_ref, 1)
    unpack(diagonal_ref, 0, whole_ref, 2)
    parts = ((6, whole_ref, 0), (7, whole_ref, 1), (8, whole_ref, 2))
    members, patches, fields = out_ref.shape
    for p in range(0, patches, 2):
        lanes = slice(p * fields, (p + 2) * fields)
        total = partial_ref[:, lanes] + blend(parts, high_ref, mix_ref, p)
        for q in range(2):
            part = total[:, q * fields : (q + 1) * fields] + centre_ref[p + q : p + q + 1, :]
            all_ref[pl.ds(p + q, members, stride=patches), :] = part
    chunk = 32
    for k in range(0, members, chunk):
        part = all_ref[k * patches : (k + chunk) * patches, :]
        out_ref[k : k + chunk] = part.reshape(chunk, patches, fields).astype(BF16)


def returned_kernel(source_ref, target_ref, done):
    copies = [pltpu.make_async_copy(source_ref.at[:, m], target_ref.at[m], done.at[m]) for m in range(target_ref.shape[0])]
    for copy in copies:
        copy.start()
    for copy in copies:
        copy.wait()


def call(kernel, outs, specs, scratch=(), to=VMEM):
    return pl.pallas_call(
        kernel,
        out_shape=outs,
        in_specs=specs,
        out_specs=jax.tree.map(lambda _: to, outs),
        scratch_shapes=list(scratch),
        compiler_params=pltpu.CompilerParams(vmem_limit_bytes=48 << 20),
    )


def per_device(background, obs_value, obs_error, obs_patch, obs_variable, obs_count, patch_corners, interp_weights):
    shape = jax.ShapeDtypeStruct
    devices = lax.axis_size("mem")
    regions = lax.axis_size("reg")
    own, _, all_patches, fields = background.shape
    patches = all_patches // devices
    members = own * devices
    points = obs_value.shape[0] * obs_value.shape[1]
    columns = patches * fields
    copies = [pltpu.SemaphoreType.DMA((own,))]

    outgoing = jnp.transpose(background.reshape(own, devices, patches, fields), (1, 0, 2, 3))
    ensemble = lax.all_to_all(outgoing, "mem", split_axis=0, concat_axis=0, tiled=True).reshape(members, patches, fields)
    dense, values, mix = call(
        prepare_kernel,
        (shape((points, patches, fields), F32), shape((points, patches, fields), F32), shape((9, patches, fields), F32)),
        [SMEM] + [VMEM] * 6,
    )(obs_count, obs_value, obs_error, obs_patch, obs_variable, patch_corners[0], interp_weights[0])

    pair = shape((2, members, members), BF16)
    packed = (members // 2 + 16, members)
    lefts = [pltpu.VMEM((2, members + 16, columns), BF16)] * 2
    wide = pltpu.VMEM((members * patches, fields), F32)
    flat = (members, columns)
    one, sent, corner, x, pert, high, centre = call(
        first_kernel,
        (pair, shape((2,) + packed, BF16), shape((1,) + packed, BF16), shape(flat, BF16), shape(flat, F32), shape(flat, BF16), shape((patches, fields), F32)),
        [VMEM] * 3,
        [wide] + lefts,
    )(ensemble, dense, values)
    down = [((d + 1) % devices, d) for d in range(devices)]
    across = [(r + 1, r) for r in range(regions - 1)]
    both = [(d * regions + r, e * regions + t) for d, e in down for r, t in across]
    beside = lax.ppermute(sent, "reg", across)
    diagonal = lax.ppermute(corner, ("mem", "reg"), both)
    two, top = call(second_kernel, (pair, shape((2,) + packed, BF16)), [VMEM] * 6, lefts)(x, pert, centre, dense, values, sent)
    below = lax.ppermute(top, "mem", down)
    whole = pltpu.VMEM((3, members, members), BF16)
    partial = call(own_kernel, shape(flat, F32), [VMEM] * 5, [whole])(one, two, beside, high, mix)
    analysis = call(last_kernel, shape((members, patches, fields), BF16), [VMEM] * 6, [wide, whole])(below, diagonal, high, mix, partial, centre)
    returned = lax.all_to_all(analysis.reshape(devices, own, patches, fields), "mem", split_axis=0, concat_axis=0, tiled=True)
    result = call(returned_kernel, shape((own, devices, patches, fields), BF16), [VMEM], copies, HBM)(returned)
    return result.reshape(own, 1, all_patches, fields)


def solution(mesh):
    placed = (
        P("mem", "reg", None, None),
        P("mem", "reg", None),
        P("mem", "reg", None),
        P("mem", "reg", None),
        P("mem", "reg", None),
        P("mem", "reg"),
        P("reg", "mem", None),
        P("reg", "mem", None),
    )
    return jax.shard_map(
        per_device,
        mesh=mesh,
        in_specs=placed,
        out_specs=P("mem", "reg", None, None),
        check_vma=False,
    )
```

```python
import jax
import jax.numpy as jnp
from jax import lax
from jax.experimental import pallas as pl
from jax.experimental.pallas import tpu as pltpu
from jax.sharding import PartitionSpec as P


F32 = jnp.float32
BF16 = jnp.bfloat16
VMEM = pl.BlockSpec(memory_space=pltpu.VMEM)
SMEM = pl.BlockSpec(memory_space=pltpu.SMEM)
HBM = pl.BlockSpec(memory_space=pltpu.HBM)
NN = (((1,), (0,)), ((), ()))
NT = (((1,), (1,)), ((), ()))


def dot(a, b, dims=NN):
    return lax.dot_general(a, b, dims, preferred_element_type=F32)


def split(x):
    high = x.astype(BF16)
    return high, (x - high.astype(F32)).astype(BF16)


def thirds(x):
    high = x.astype(BF16)
    rest = x - high.astype(F32)
    middle = rest.astype(BF16)
    return high, middle, (rest - middle.astype(F32)).astype(BF16)


def product(a, b):
    return dot(a[0], b[0]) + (dot(a[0], b[1]) + dot(a[1], b[0]))


def prepare_kernel(count_ref, value_ref, error_ref, patch_ref, var_ref, corner_ref, coeff_ref, dense_ref, value_out_ref, mix_ref):
    rows, cols, slots = value_ref.shape
    patches, fields = dense_ref.shape[1:]
    slot_index = lax.broadcasted_iota(jnp.int32, (1, slots), 1)
    field_index = lax.broadcasted_iota(jnp.int32, (fields, slots), 0)
    patch_index = lax.broadcasted_iota(jnp.int32, (patches, slots), 0)
    for a in range(rows):
        for b in range(cols):
            weight = jnp.where(slot_index < count_ref[a, b], 1.0 / error_ref[a, b : b + 1, :], 0.0)
            weighted = weight * value_ref[a, b : b + 1, :]
            chosen = (field_index == var_ref[a, b : b + 1, :]).astype(F32).astype(BF16)
            at_patch = patch_index == patch_ref[a, b : b + 1, :]
            left = jnp.concatenate([jnp.where(at_patch, x, 0.0) for x in (weight, weighted)], axis=0)
            high, middle, low = (dot(x, chosen, NT) for x in thirds(left))
            sums = high + (middle + low)
            dense_ref[a * cols + b] = sums[:patches]
            value_out_ref[a * cols + b] = sums[patches:]
    corners, coeffs = corner_ref[...], coeff_ref[...]
    for t in range(mix_ref.shape[0]):
        used = jnp.sum(jnp.where(corners == t, coeffs, 0.0), axis=1, keepdims=True)
        mix_ref[t] = jnp.broadcast_to(used, (patches, fields))


def shares(points, pert_ref, centre, dense_ref, value_ref, left_high, left_low):
    members = pert_ref.shape[0]
    patches, fields = centre.shape
    pulls = [value_ref[n] - dense_ref[n] * centre for n in points]
    for p in range(patches):
        lanes = slice(p * fields, (p + 1) * fields)
        pert = pert_ref[:, lanes]
        for slot, n in enumerate(points):
            left_high[slot, :members, lanes], left_low[slot, :members, lanes] = split(pert * dense_ref[n, p : p + 1, :])
            tail = jnp.broadcast_to(pulls[slot][p : p + 1, :], (left_high.shape[1] - members, fields))
            left_high[slot, members:, lanes], left_low[slot, members:, lanes] = split(tail)


def add_diagonal(x, value, diagonal):
    half = diagonal.shape[0]
    step = jnp.where(diagonal, value, 0.0)
    top = jnp.concatenate([x[:half, :half] + step, x[:half, half:]], axis=1)
    bottom = jnp.concatenate([x[half:, :half], x[half:, half:] + step], axis=1)
    return jnp.concatenate([top, bottom], axis=0)


def two_factors(x, parts, diagonal):
    square = product(parts, parts)
    inner = add_diagonal(square - 4.5 * x, 6.75, diagonal)
    return add_diagonal(product(split(square), split(inner)) - 4.875 * x, 2.25, diagonal)


def weights_of(count, x_ref, left_high, left_low, out_ref):
    members = x_ref.shape[0]
    half = members // 2
    row = lax.broadcasted_iota(jnp.int32, (half, half), 0)
    col = lax.broadcasted_iota(jnp.int32, (half, half), 1)
    diagonal = row == col
    slots = range(count)
    state = []
    for slot in slots:
        columns = x_ref[...]
        both = dot(left_high[slot], columns, NT) + dot(left_low[slot], columns, NT)
        both = both - jnp.sum(both, axis=1, keepdims=True) * (1.0 / members)
        gram, projected = both[:members], both[members : members + 1]
        on_diagonal = jnp.where(diagonal, gram[:half, :half] + gram[half:, half:], 0.0)
        trace = jnp.sum(jnp.sum(on_diagonal, axis=0, keepdims=True), axis=1, keepdims=True)
        scaling = (members - 1.0) + trace / members
        half_inverse = 0.5 / scaling
        state.append((projected, scaling, add_diagonal(gram * half_inverse, (members - 1.0) * half_inverse, diagonal)))
    parts = [split(x) for _, _, x in state]
    z = [split(two_factors(state[s][2], parts[s], diagonal)) for s in slots]
    y = [split(product(parts[s], z[s])) for s in slots]
    c = [product(y[s], z[s]) for s in slots]
    f = [split(two_factors(c[s], split(c[s]), diagonal)) for s in slots]
    inverses = [product(f[s], z[s]) for s in slots]
    for slot in slots:
        projected, scaling, _ = state[slot]
        inverse = inverses[slot]
        once = jnp.sum(inverse * projected, axis=1, keepdims=True)
        twice = jnp.sum(inverse * once, axis=0, keepdims=True) / scaling
        spread = jnp.sqrt((members - 1.0) / scaling) * inverse
        out_ref[slot] = (spread + twice).astype(BF16)
        yield slot, spread, twice


def pack(target, slot, spread, twice):
    members = spread.shape[0]
    half = members // 2
    small_row = lax.broadcasted_iota(jnp.int32, (half, half), 0)
    small_col = lax.broadcasted_iota(jnp.int32, (half, half), 1)
    tail_row = lax.broadcasted_iota(jnp.int32, (16, members), 0)
    corner = spread[half:, half:]
    target[slot, :half, :half] = jnp.where(small_row >= small_col, spread[:half, :half], corner).astype(BF16)
    target[slot, :half, half:] = spread[:half, half:].astype(BF16)
    on_diagonal = jnp.sum(jnp.where(small_row == small_col, corner, 0.0), axis=0, keepdims=True)
    high, low = split(twice)
    rows = jnp.where(tail_row == 1, high.astype(F32), jnp.where(tail_row == 2, low.astype(F32), 0.0))
    first = jnp.concatenate([on_diagonal, jnp.zeros_like(on_diagonal)], axis=1)
    target[slot, half:, :] = jnp.where(tail_row == 0, first, rows).astype(BF16)


def unpack(source, slot, target, place):
    half = source.shape[1] - 16
    row = lax.broadcasted_iota(jnp.int32, (half, half), 0)
    col = lax.broadcasted_iota(jnp.int32, (half, half), 1)
    mixed = source[slot, :half, :half].astype(F32)
    across = source[slot, :half, half:].astype(F32)
    tail = source[slot, half:, :].astype(F32)
    mean = tail[1:2] + tail[2:3]
    left, right = mean[:, :half], mean[:, half:]
    turned = mixed.T
    target[place, :half, :half] = (jnp.where(row >= col, mixed, turned) + left).astype(BF16)
    target[place, :half, half:] = (across + right).astype(BF16)
    target[place, half:, :half] = (across.T + left).astype(BF16)
    corner = jnp.where(row < col, mixed, jnp.where(row == col, tail[0:1, :half], turned))
    target[place, half:, half:] = (corner + right).astype(BF16)


def first_kernel(
    ensemble_ref, dense_ref, value_ref, out_ref, beside_ref, corner_ref, below_ref, x_ref, pert_ref, high_ref, centre_ref, wide_ref, left_high, left_low
):
    members, patches, fields = ensemble_ref.shape
    total = jnp.zeros((patches, fields), F32)
    chunk = 32
    for k in range(0, members, chunk):
        part = ensemble_ref[k : k + chunk].astype(F32)
        total = total + jnp.sum(part, axis=0)
        wide_ref[k * patches : (k + chunk) * patches] = part.reshape(chunk * patches, fields)
    centre = total * (1.0 / members)
    centre_ref[...] = centre
    for p in range(patches):
        lanes = slice(p * fields, (p + 1) * fields)
        part = wide_ref[pl.ds(p, members, stride=patches), :]
        x_ref[:, lanes] = part.astype(BF16)
        pert = part - centre[p : p + 1, :]
        pert_ref[:, lanes] = pert
        high_ref[:, lanes] = pert.astype(BF16)
    shares((0, 1, 2), pert_ref, centre, dense_ref, value_ref, left_high, left_low)
    for slot, spread, twice in weights_of(3, x_ref, left_high, left_low, out_ref):
        if slot == 0:
            pack(corner_ref, 0, spread, twice)
            beside_ref[0] = corner_ref[0]
            below_ref[0] = corner_ref[0]
        else:
            pack(below_ref if slot == 1 else beside_ref, 1, spread, twice)


def second_kernel(x_ref, pert_ref, centre_ref, dense_ref, value_ref, one_ref, high_ref, mix_ref, out_ref, left_high, left_low, two_ref):
    patches, fields = centre_ref.shape
    shares((3,), pert_ref, centre_ref[...], dense_ref, value_ref, left_high, left_low)
    parts = ((0, one_ref, 0), (1, one_ref, 1), (3, one_ref, 2))
    for p in range(0, patches, 2):
        out_ref[:, p * fields : (p + 2) * fields] = blend(parts, high_ref, mix_ref, p)
    for _ in weights_of(1, x_ref, left_high, left_low, two_ref):
        pass
    for p in range(0, patches, 2):
        lanes = slice(p * fields, (p + 2) * fields)
        out_ref[:, lanes] = out_ref[:, lanes] + blend(((4, two_ref, 0),), high_ref, mix_ref, p)


def blend(parts, high_ref, mix_ref, p):
    fields = mix_ref.shape[2]
    lanes = slice(p * fields, (p + 2) * fields)
    total = None
    for t, ref, slot in parts:
        share = jnp.concatenate([mix_ref[t, p : p + 1, :], mix_ref[t, p + 1 : p + 2, :]], axis=1)
        moved = dot(ref[slot], high_ref[:, lanes])
        moved = jnp.where(share != 0.0, share * moved, 0.0)
        total = moved if total is None else total + moved
    return total


def last_kernel(beside_ref, below_ref, diagonal_ref, high_ref, mix_ref, partial_ref, centre_ref, out_ref, all_ref, whole_ref):
    arrived = ((2, beside_ref, 0), (5, beside_ref, 1), (6, below_ref, 0), (7, below_ref, 1), (8, diagonal_ref, 0))
    for place, (_, ref, slot) in enumerate(arrived):
        unpack(ref, slot, whole_ref, place)
    parts = [(t, whole_ref, place) for place, (t, _, _) in enumerate(arrived)]
    members, patches, fields = out_ref.shape
    for p in range(0, patches, 2):
        lanes = slice(p * fields, (p + 2) * fields)
        total = partial_ref[:, lanes] + blend(parts, high_ref, mix_ref, p)
        for q in range(2):
            part = total[:, q * fields : (q + 1) * fields] + centre_ref[p + q : p + q + 1, :]
            all_ref[pl.ds(p + q, members, stride=patches), :] = part
    chunk = 32
    for k in range(0, members, chunk):
        part = all_ref[k * patches : (k + chunk) * patches, :]
        out_ref[k : k + chunk] = part.reshape(chunk, patches, fields).astype(BF16)


def returned_kernel(source_ref, target_ref, done):
    copies = [pltpu.make_async_copy(source_ref.at[:, m], target_ref.at[m], done.at[m]) for m in range(target_ref.shape[0])]
    for copy in copies:
        copy.start()
    for copy in copies:
        copy.wait()


def call(kernel, outs, specs, scratch=(), to=VMEM):
    return pl.pallas_call(
        kernel,
        out_shape=outs,
        in_specs=specs,
        out_specs=jax.tree.map(lambda _: to, outs),
        scratch_shapes=list(scratch),
        compiler_params=pltpu.CompilerParams(vmem_limit_bytes=48 << 20),
    )


def per_device(background, obs_value, obs_error, obs_patch, obs_variable, obs_count, patch_corners, interp_weights):
    shape = jax.ShapeDtypeStruct
    devices = lax.axis_size("mem")
    regions = lax.axis_size("reg")
    own, _, all_patches, fields = background.shape
    patches = all_patches // devices
    members = own * devices
    points = obs_value.shape[0] * obs_value.shape[1]
    columns = patches * fields
    copies = [pltpu.SemaphoreType.DMA((own,))]

    outgoing = jnp.transpose(background.reshape(own, devices, patches, fields), (1, 0, 2, 3))
    ensemble = lax.all_to_all(outgoing, "mem", split_axis=0, concat_axis=0, tiled=True).reshape(members, patches, fields)
    dense, values, mix = call(
        prepare_kernel,
        (shape((points, patches, fields), F32), shape((points, patches, fields), F32), shape((9, patches, fields), F32)),
        [SMEM] + [VMEM] * 6,
    )(obs_count, obs_value, obs_error, obs_patch, obs_variable, patch_corners[0], interp_weights[0])

    packed = (members // 2 + 16, members)
    left = (members + 16, columns)
    flat = (members, columns)
    wide = pltpu.VMEM((members * patches, fields), F32)
    down = [((d + 1) % devices, d) for d in range(devices)]
    across = [(r + 1, r) for r in range(regions - 1)]
    both = [(d * regions + r, e * regions + t) for d, e in down for r, t in across]
    one, to_beside, to_corner, to_below, x, pert, high, centre = call(
        first_kernel,
        (
            shape((3, members, members), BF16),
            shape((2,) + packed, BF16),
            shape((1,) + packed, BF16),
            shape((2,) + packed, BF16),
            shape(flat, BF16),
            shape(flat, F32),
            shape(flat, BF16),
            shape((patches, fields), F32),
        ),
        [VMEM] * 3,
        [wide] + [pltpu.VMEM((3,) + left, BF16)] * 2,
    )(ensemble, dense, values)
    beside = lax.ppermute(to_beside, "reg", across)
    diagonal = lax.ppermute(to_corner, ("mem", "reg"), both)
    below = lax.ppermute(to_below, "mem", down)
    partial = call(
        second_kernel,
        shape(flat, F32),
        [VMEM] * 8,
        [pltpu.VMEM((1,) + left, BF16)] * 2 + [pltpu.VMEM((1, members, members), BF16)],
    )(x, pert, centre, dense, values, one, high, mix)
    analysis = call(
        last_kernel,
        shape((members, patches, fields), BF16),
        [VMEM] * 7,
        [wide, pltpu.VMEM((5, members, members), BF16)],
    )(beside, below, diagonal, high, mix, partial, centre)
    returned = lax.all_to_all(analysis.reshape(devices, own, patches, fields), "mem", split_axis=0, concat_axis=0, tiled=True)
    result = call(returned_kernel, shape((own, devices, patches, fields), BF16), [VMEM], copies, HBM)(returned)
    return result.reshape(own, 1, all_patches, fields)


def solution(mesh):
    placed = (
        P("mem", "reg", None, None),
        P("mem", "reg", None),
        P("mem", "reg", None),
        P("mem", "reg", None),
        P("mem", "reg", None),
        P("mem", "reg"),
        P("reg", "mem", None),
        P("reg", "mem", None),
    )
    return jax.shard_map(
        per_device,
        mesh=mesh,
        in_specs=placed,
        out_specs=P("mem", "reg", None, None),
        check_vma=False,
    )
```

```python
import jax
import jax.numpy as jnp
from jax import lax
from jax.experimental import pallas as pl
from jax.experimental.pallas import tpu as pltpu
from jax.sharding import PartitionSpec as P


F32 = jnp.float32
BF16 = jnp.bfloat16
VMEM = pl.BlockSpec(memory_space=pltpu.VMEM)
SMEM = pl.BlockSpec(memory_space=pltpu.SMEM)
HBM = pl.BlockSpec(memory_space=pltpu.HBM)
NN = (((1,), (0,)), ((), ()))
NT = (((1,), (1,)), ((), ()))


def dot(a, b, dims=NN):
    return lax.dot_general(a, b, dims, preferred_element_type=F32)


def split(x):
    high = x.astype(BF16)
    return high, (x - high.astype(F32)).astype(BF16)


def thirds(x):
    high = x.astype(BF16)
    rest = x - high.astype(F32)
    middle = rest.astype(BF16)
    return high, middle, (rest - middle.astype(F32)).astype(BF16)


def product(a, b):
    return dot(a[0], b[0]) + (dot(a[0], b[1]) + dot(a[1], b[0]))


def prepare_kernel(count_ref, value_ref, error_ref, patch_ref, var_ref, corner_ref, coeff_ref, dense_ref, value_out_ref, mix_ref):
    rows, cols, slots = value_ref.shape
    patches, fields = dense_ref.shape[1:]
    slot_index = lax.broadcasted_iota(jnp.int32, (1, slots), 1)
    field_index = lax.broadcasted_iota(jnp.int32, (fields, slots), 0)
    patch_index = lax.broadcasted_iota(jnp.int32, (patches, slots), 0)
    for a in range(rows):
        for b in range(cols):
            weight = jnp.where(slot_index < count_ref[a, b], 1.0 / error_ref[a, b : b + 1, :], 0.0)
            weighted = weight * value_ref[a, b : b + 1, :]
            chosen = (field_index == var_ref[a, b : b + 1, :]).astype(F32).astype(BF16)
            at_patch = patch_index == patch_ref[a, b : b + 1, :]
            left = jnp.concatenate([jnp.where(at_patch, x, 0.0) for x in (weight, weighted)], axis=0)
            high, middle, low = (dot(x, chosen, NT) for x in thirds(left))
            sums = high + (middle + low)
            dense_ref[a * cols + b] = sums[:patches]
            value_out_ref[a * cols + b] = sums[patches:]
    corners, coeffs = corner_ref[...], coeff_ref[...]
    for t in range(mix_ref.shape[0]):
        used = jnp.sum(jnp.where(corners == t, coeffs, 0.0), axis=1, keepdims=True)
        mix_ref[t] = jnp.broadcast_to(used, (patches, fields))


def shares(points, pert_ref, centre, dense_ref, value_ref, left_high, left_low):
    members = pert_ref.shape[0]
    patches, fields = centre.shape
    pulls = [value_ref[n] - dense_ref[n] * centre for n in points]
    for p in range(patches):
        lanes = slice(p * fields, (p + 1) * fields)
        pert = pert_ref[:, lanes]
        for slot, n in enumerate(points):
            left_high[slot, :members, lanes], left_low[slot, :members, lanes] = split(pert * dense_ref[n, p : p + 1, :])
            tail = jnp.broadcast_to(pulls[slot][p : p + 1, :], (left_high.shape[1] - members, fields))
            left_high[slot, members:, lanes], left_low[slot, members:, lanes] = split(tail)


def add_diagonal(x, value, diagonal):
    half = diagonal.shape[0]
    step = jnp.where(diagonal, value, 0.0)
    top = jnp.concatenate([x[:half, :half] + step, x[:half, half:]], axis=1)
    bottom = jnp.concatenate([x[half:, :half], x[half:, half:] + step], axis=1)
    return jnp.concatenate([top, bottom], axis=0)


def two_factors(x, parts, diagonal):
    square = product(parts, parts)
    inner = add_diagonal(square - 4.5 * x, 6.75, diagonal)
    return add_diagonal(product(split(square), split(inner)) - 4.875 * x, 2.25, diagonal)


def later_factors(x):
    rounded = x.astype(BF16)
    square = dot(rounded, rounded)
    return 1.5 * square - x + dot(square.astype(BF16), (square - 2.5 * x).astype(BF16))


def weights_of(count, x_ref, left_high, left_low, out_ref):
    members = x_ref.shape[0]
    half = members // 2
    row = lax.broadcasted_iota(jnp.int32, (half, half), 0)
    col = lax.broadcasted_iota(jnp.int32, (half, half), 1)
    diagonal = row == col
    slots = range(count)
    state = []
    for slot in slots:
        columns = x_ref[...]
        both = dot(left_high[slot], columns, NT) + dot(left_low[slot], columns, NT)
        both = both - jnp.sum(both, axis=1, keepdims=True) * (1.0 / members)
        gram, projected = both[:members], both[members : members + 1]
        on_diagonal = jnp.where(diagonal, gram[:half, :half] + gram[half:, half:], 0.0)
        trace = jnp.sum(jnp.sum(on_diagonal, axis=0, keepdims=True), axis=1, keepdims=True)
        scaling = (members - 1.0) + trace / members
        half_inverse = 0.5 / scaling
        state.append((projected, scaling, add_diagonal(gram * half_inverse, (members - 1.0) * half_inverse, diagonal)))
    parts = [split(x) for _, _, x in state]
    roots = [two_factors(state[s][2], parts[s], diagonal) for s in slots]
    z = [split(x) for x in roots]
    y = [split(product(parts[s], z[s])) for s in slots]
    excess = [add_diagonal(product(y[s], z[s]), -0.5, diagonal) for s in slots]
    rest = [later_factors(x) for x in excess]
    inverses = [roots[s] + rest[s] + dot(rest[s].astype(BF16), add_diagonal(roots[s], -1.0, diagonal).astype(BF16)) for s in slots]
    for slot in slots:
        projected, scaling, _ = state[slot]
        inverse = inverses[slot]
        once = jnp.sum(inverse * projected, axis=1, keepdims=True)
        twice = jnp.sum(inverse * once, axis=0, keepdims=True) / scaling
        spread = jnp.sqrt((members - 1.0) / scaling) * inverse
        out_ref[slot] = (spread + twice).astype(BF16)
        yield slot, spread, twice


def pack(target, slot, spread, twice):
    members = spread.shape[0]
    half = members // 2
    small_row = lax.broadcasted_iota(jnp.int32, (half, half), 0)
    small_col = lax.broadcasted_iota(jnp.int32, (half, half), 1)
    tail_row = lax.broadcasted_iota(jnp.int32, (16, members), 0)
    corner = spread[half:, half:]
    target[slot, :half, :half] = jnp.where(small_row >= small_col, spread[:half, :half], corner).astype(BF16)
    target[slot, :half, half:] = spread[:half, half:].astype(BF16)
    on_diagonal = jnp.sum(jnp.where(small_row == small_col, corner, 0.0), axis=0, keepdims=True)
    high, low = split(twice)
    rows = jnp.where(tail_row == 1, high.astype(F32), jnp.where(tail_row == 2, low.astype(F32), 0.0))
    first = jnp.concatenate([on_diagonal, jnp.zeros_like(on_diagonal)], axis=1)
    target[slot, half:, :] = jnp.where(tail_row == 0, first, rows).astype(BF16)


def unpack(source, slot, target, place):
    half = source.shape[1] - 16
    row = lax.broadcasted_iota(jnp.int32, (half, half), 0)
    col = lax.broadcasted_iota(jnp.int32, (half, half), 1)
    mixed = source[slot, :half, :half].astype(F32)
    across = source[slot, :half, half:].astype(F32)
    tail = source[slot, half:, :].astype(F32)
    mean = tail[1:2] + tail[2:3]
    left, right = mean[:, :half], mean[:, half:]
    turned = mixed.T
    target[place, :half, :half] = (jnp.where(row >= col, mixed, turned) + left).astype(BF16)
    target[place, :half, half:] = (across + right).astype(BF16)
    target[place, half:, :half] = (across.T + left).astype(BF16)
    corner = jnp.where(row < col, mixed, jnp.where(row == col, tail[0:1, :half], turned))
    target[place, half:, half:] = (corner + right).astype(BF16)


def first_kernel(
    ensemble_ref, dense_ref, value_ref, out_ref, beside_ref, corner_ref, below_ref, x_ref, pert_ref, high_ref, centre_ref, wide_ref, left_high, left_low
):
    members, patches, fields = ensemble_ref.shape
    total = jnp.zeros((patches, fields), F32)
    chunk = 32
    for k in range(0, members, chunk):
        part = ensemble_ref[k : k + chunk].astype(F32)
        total = total + jnp.sum(part, axis=0)
        wide_ref[k * patches : (k + chunk) * patches] = part.reshape(chunk * patches, fields)
    centre = total * (1.0 / members)
    centre_ref[...] = centre
    for p in range(patches):
        lanes = slice(p * fields, (p + 1) * fields)
        part = wide_ref[pl.ds(p, members, stride=patches), :]
        x_ref[:, lanes] = part.astype(BF16)
        pert = part - centre[p : p + 1, :]
        pert_ref[:, lanes] = pert
        high_ref[:, lanes] = pert.astype(BF16)
    shares((0, 1, 2), pert_ref, centre, dense_ref, value_ref, left_high, left_low)
    for slot, spread, twice in weights_of(3, x_ref, left_high, left_low, out_ref):
        if slot == 0:
            pack(corner_ref, 0, spread, twice)
            beside_ref[0] = corner_ref[0]
            below_ref[0] = corner_ref[0]
        else:
            pack(below_ref if slot == 1 else beside_ref, 1, spread, twice)


def second_kernel(x_ref, pert_ref, centre_ref, dense_ref, value_ref, one_ref, high_ref, mix_ref, out_ref, left_high, left_low, two_ref):
    patches, fields = centre_ref.shape
    shares((3,), pert_ref, centre_ref[...], dense_ref, value_ref, left_high, left_low)
    parts = ((0, one_ref, 0), (1, one_ref, 1), (3, one_ref, 2), (4, two_ref, 0))
    for _ in weights_of(1, x_ref, left_high, left_low, two_ref):
        pass
    for p in range(0, patches, 2):
        out_ref[:, p * fields : (p + 2) * fields] = blend(parts, high_ref, mix_ref, p)


def blend(parts, high_ref, mix_ref, p):
    fields = mix_ref.shape[2]
    lanes = slice(p * fields, (p + 2) * fields)
    total = None
    for t, ref, slot in parts:
        share = jnp.concatenate([mix_ref[t, p : p + 1, :], mix_ref[t, p + 1 : p + 2, :]], axis=1)
        moved = dot(ref[slot], high_ref[:, lanes])
        moved = jnp.where(share != 0.0, share * moved, 0.0)
        total = moved if total is None else total + moved
    return total


def last_kernel(beside_ref, below_ref, diagonal_ref, high_ref, mix_ref, partial_ref, centre_ref, out_ref, all_ref, whole_ref):
    arrived = ((2, beside_ref, 0), (5, beside_ref, 1), (6, below_ref, 0), (7, below_ref, 1), (8, diagonal_ref, 0))
    for place, (_, ref, slot) in enumerate(arrived):
        unpack(ref, slot, whole_ref, place)
    parts = [(t, whole_ref, place) for place, (t, _, _) in enumerate(arrived)]
    members, patches, fields = out_ref.shape
    for p in range(0, patches, 2):
        lanes = slice(p * fields, (p + 2) * fields)
        total = partial_ref[:, lanes] + blend(parts, high_ref, mix_ref, p)
        for q in range(2):
            part = total[:, q * fields : (q + 1) * fields] + centre_ref[p + q : p + q + 1, :]
            all_ref[pl.ds(p + q, members, stride=patches), :] = part
    chunk = 32
    for k in range(0, members, chunk):
        part = all_ref[k * patches : (k + chunk) * patches, :]
        out_ref[k : k + chunk] = part.reshape(chunk, patches, fields).astype(BF16)


def outgoing_kernel(source_ref, target_ref, held_ref, turned_ref, read, written):
    own, devices = source_ref.shape[:2]
    half = devices // 2
    spans = [slice(h * half, (h + 1) * half) for h in range(2)]
    inward = [pltpu.make_async_copy(source_ref.at[:, s], held_ref.at[:, s], read.at[h]) for h, s in enumerate(spans)]
    outward = [pltpu.make_async_copy(turned_ref.at[s], target_ref.at[s], written.at[h]) for h, s in enumerate(spans)]
    for copy in inward:
        copy.start()
    for copy, out, s in zip(inward, outward, spans):
        copy.wait()
        for m in range(own):
            turned_ref[s, m] = held_ref[m, s]
        out.start()
    for out in outward:
        out.wait()


def returned_kernel(source_ref, target_ref, done):
    copies = [pltpu.make_async_copy(source_ref.at[:, m], target_ref.at[m], done.at[m]) for m in range(target_ref.shape[0])]
    for copy in copies:
        copy.start()
    for copy in copies:
        copy.wait()


def call(kernel, outs, specs, scratch=(), to=VMEM):
    return pl.pallas_call(
        kernel,
        out_shape=outs,
        in_specs=specs,
        out_specs=jax.tree.map(lambda _: to, outs),
        scratch_shapes=list(scratch),
        compiler_params=pltpu.CompilerParams(vmem_limit_bytes=48 << 20),
    )


def per_device(background, obs_value, obs_error, obs_patch, obs_variable, obs_count, patch_corners, interp_weights):
    shape = jax.ShapeDtypeStruct
    devices = lax.axis_size("mem")
    regions = lax.axis_size("reg")
    own, _, all_patches, fields = background.shape
    patches = all_patches // devices
    members = own * devices
    points = obs_value.shape[0] * obs_value.shape[1]
    columns = patches * fields
    copies = [pltpu.SemaphoreType.DMA((own,))]

    blocks = (devices, own, patches, fields)
    outgoing = call(
        outgoing_kernel,
        shape(blocks, BF16),
        [HBM],
        [pltpu.VMEM((own,) + (devices,) + blocks[2:], BF16), pltpu.VMEM(blocks, BF16)] + [pltpu.SemaphoreType.DMA((2,))] * 2,
        HBM,
    )(pltpu.with_memory_space_constraint(background.reshape(own, devices, patches, fields), pltpu.HBM))
    ensemble = lax.all_to_all(outgoing, "mem", split_axis=0, concat_axis=0, tiled=True).reshape(members, patches, fields)
    dense, values, mix = call(
        prepare_kernel,
        (shape((points, patches, fields), F32), shape((points, patches, fields), F32), shape((9, patches, fields), F32)),
        [SMEM] + [VMEM] * 6,
    )(obs_count, obs_value, obs_error, obs_patch, obs_variable, patch_corners[0], interp_weights[0])

    packed = (members // 2 + 16, members)
    left = (members + 16, columns)
    flat = (members, columns)
    wide = pltpu.VMEM((members * patches, fields), F32)
    down = [((d + 1) % devices, d) for d in range(devices)]
    across = [(r + 1, r) for r in range(regions - 1)]
    both = [(d * regions + r, e * regions + t) for d, e in down for r, t in across]
    one, to_beside, to_corner, to_below, x, pert, high, centre = call(
        first_kernel,
        (
            shape((3, members, members), BF16),
            shape((2,) + packed, BF16),
            shape((1,) + packed, BF16),
            shape((2,) + packed, BF16),
            shape(flat, BF16),
            shape(flat, F32),
            shape(flat, BF16),
            shape((patches, fields), F32),
        ),
        [VMEM] * 3,
        [wide] + [pltpu.VMEM((3,) + left, BF16)] * 2,
    )(ensemble, dense, values)
    beside = lax.ppermute(to_beside, "reg", across)
    diagonal = lax.ppermute(to_corner, ("mem", "reg"), both)
    below = lax.ppermute(to_below, "mem", down)
    partial = call(
        second_kernel,
        shape(flat, F32),
        [VMEM] * 8,
        [pltpu.VMEM((1,) + left, BF16)] * 2 + [pltpu.VMEM((1, members, members), BF16)],
    )(x, pert, centre, dense, values, one, high, mix)
    analysis = call(
        last_kernel,
        shape((members, patches, fields), BF16),
        [VMEM] * 7,
        [wide, pltpu.VMEM((5, members, members), BF16)],
    )(beside, below, diagonal, high, mix, partial, centre)
    returned = lax.all_to_all(analysis.reshape(devices, own, patches, fields), "mem", split_axis=0, concat_axis=0, tiled=True)
    result = call(returned_kernel, shape((own, devices, patches, fields), BF16), [VMEM], copies, HBM)(returned)
    return result.reshape(own, 1, all_patches, fields)


def solution(mesh):
    placed = (
        P("mem", "reg", None, None),
        P("mem", "reg", None),
        P("mem", "reg", None),
        P("mem", "reg", None),
        P("mem", "reg", None),
        P("mem", "reg"),
        P("reg", "mem", None),
        P("reg", "mem", None),
    )
    return jax.shard_map(
        per_device,
        mesh=mesh,
        in_specs=placed,
        out_specs=P("mem", "reg", None, None),
        check_vma=False,
    )
```

```python
import jax
import jax.numpy as jnp
from jax import lax
from jax.experimental import pallas as pl
from jax.experimental.pallas import tpu as pltpu
from jax.sharding import PartitionSpec as P


F32 = jnp.float32
BF16 = jnp.bfloat16
VMEM = pl.BlockSpec(memory_space=pltpu.VMEM)
SMEM = pl.BlockSpec(memory_space=pltpu.SMEM)
HBM = pl.BlockSpec(memory_space=pltpu.HBM)
NN = (((1,), (0,)), ((), ()))
NT = (((1,), (1,)), ((), ()))


def dot(a, b, dims=NN):
    return lax.dot_general(a, b, dims, preferred_element_type=F32)


def split(x):
    high = x.astype(BF16)
    return high, (x - high.astype(F32)).astype(BF16)


def thirds(x):
    high = x.astype(BF16)
    rest = x - high.astype(F32)
    middle = rest.astype(BF16)
    return high, middle, (rest - middle.astype(F32)).astype(BF16)


def product(a, b):
    return dot(a[0], b[0]) + (dot(a[0], b[1]) + dot(a[1], b[0]))


def prepare_kernel(count_ref, value_ref, error_ref, patch_ref, var_ref, corner_ref, coeff_ref, dense_ref, value_out_ref, mix_ref):
    rows, cols, slots = value_ref.shape
    patches, fields = dense_ref.shape[1:]
    slot_index = lax.broadcasted_iota(jnp.int32, (1, slots), 1)
    field_index = lax.broadcasted_iota(jnp.int32, (fields, slots), 0)
    patch_index = lax.broadcasted_iota(jnp.int32, (patches, slots), 0)
    for a in range(rows):
        for b in range(cols):
            weight = jnp.where(slot_index < count_ref[a, b], 1.0 / error_ref[a, b : b + 1, :], 0.0)
            weighted = weight * value_ref[a, b : b + 1, :]
            chosen = (field_index == var_ref[a, b : b + 1, :]).astype(F32).astype(BF16)
            at_patch = patch_index == patch_ref[a, b : b + 1, :]
            left = jnp.concatenate([jnp.where(at_patch, x, 0.0) for x in (weight, weighted)], axis=0)
            high, middle, low = (dot(x, chosen, NT) for x in thirds(left))
            sums = high + (middle + low)
            dense_ref[a * cols + b] = sums[:patches]
            value_out_ref[a * cols + b] = sums[patches:]
    corners, coeffs = corner_ref[...], coeff_ref[...]
    for t in range(mix_ref.shape[0]):
        used = jnp.sum(jnp.where(corners == t, coeffs, 0.0), axis=1, keepdims=True)
        mix_ref[t] = jnp.broadcast_to(used, (patches, fields))


def shares(points, pert_ref, centre, dense_ref, value_ref, left_high, left_low):
    members = pert_ref.shape[0]
    patches, fields = centre.shape
    pulls = [value_ref[n] - dense_ref[n] * centre for n in points]
    for p in range(patches):
        lanes = slice(p * fields, (p + 1) * fields)
        pert = pert_ref[:, lanes]
        for slot, n in enumerate(points):
            left_high[slot, :members, lanes], left_low[slot, :members, lanes] = split(pert * dense_ref[n, p : p + 1, :])
            tail = jnp.broadcast_to(pulls[slot][p : p + 1, :], (left_high.shape[1] - members, fields))
            left_high[slot, members:, lanes], left_low[slot, members:, lanes] = split(tail)


def add_diagonal(x, value, diagonal):
    half = diagonal.shape[0]
    step = jnp.where(diagonal, value, 0.0)
    top = jnp.concatenate([x[:half, :half] + step, x[:half, half:]], axis=1)
    bottom = jnp.concatenate([x[half:, :half], x[half:, half:] + step], axis=1)
    return jnp.concatenate([top, bottom], axis=0)


def two_factors(x, parts, diagonal):
    square = product(parts, parts)
    inner = add_diagonal(square - 4.5 * x, 6.75, diagonal)
    return add_diagonal(product(split(square), split(inner)) - 4.875 * x, 2.25, diagonal)


def later_factors(x):
    rounded = x.astype(BF16)
    square = dot(rounded, rounded)
    return 1.5 * square - x + dot(square.astype(BF16), (square - 2.5 * x).astype(BF16))


def weights_of(count, x_ref, left_high, left_low, out_ref):
    members = x_ref.shape[0]
    half = members // 2
    row = lax.broadcasted_iota(jnp.int32, (half, half), 0)
    col = lax.broadcasted_iota(jnp.int32, (half, half), 1)
    diagonal = row == col
    slots = range(count)
    state = []
    for slot in slots:
        columns = x_ref[...]
        both = dot(left_high[slot], columns, NT) + dot(left_low[slot], columns, NT)
        both = both - jnp.sum(both, axis=1, keepdims=True) * (1.0 / members)
        gram, projected = both[:members], both[members : members + 1]
        on_diagonal = jnp.where(diagonal, gram[:half, :half] + gram[half:, half:], 0.0)
        trace = jnp.sum(jnp.sum(on_diagonal, axis=0, keepdims=True), axis=1, keepdims=True)
        scaling = (members - 1.0) + trace / members
        half_inverse = 0.5 / scaling
        state.append((projected, scaling, add_diagonal(gram * half_inverse, (members - 1.0) * half_inverse, diagonal)))
    parts = [split(x) for _, _, x in state]
    roots = [two_factors(state[s][2], parts[s], diagonal) for s in slots]
    z = [split(x) for x in roots]
    y = [split(product(parts[s], z[s])) for s in slots]
    excess = [add_diagonal(product(y[s], z[s]), -0.5, diagonal) for s in slots]
    rest = [later_factors(x) for x in excess]
    inverses = [roots[s] + rest[s] + dot(rest[s].astype(BF16), add_diagonal(roots[s], -1.0, diagonal).astype(BF16)) for s in slots]
    for slot in slots:
        projected, scaling, _ = state[slot]
        inverse = inverses[slot]
        once = jnp.sum(inverse * projected, axis=1, keepdims=True)
        twice = jnp.sum(inverse * once, axis=0, keepdims=True) / scaling
        spread = jnp.sqrt((members - 1.0) / scaling) * inverse
        out_ref[slot] = (spread + twice).astype(BF16)
        yield slot, spread, twice


def pack(target, slot, spread, twice):
    members = spread.shape[0]
    half = members // 2
    small_row = lax.broadcasted_iota(jnp.int32, (half, half), 0)
    small_col = lax.broadcasted_iota(jnp.int32, (half, half), 1)
    tail_row = lax.broadcasted_iota(jnp.int32, (16, members), 0)
    corner = spread[half:, half:]
    target[slot, :half, :half] = jnp.where(small_row >= small_col, spread[:half, :half], corner).astype(BF16)
    target[slot, :half, half:] = spread[:half, half:].astype(BF16)
    on_diagonal = jnp.sum(jnp.where(small_row == small_col, corner, 0.0), axis=0, keepdims=True)
    high, low = split(twice)
    rows = jnp.where(tail_row == 1, high.astype(F32), jnp.where(tail_row == 2, low.astype(F32), 0.0))
    first = jnp.concatenate([on_diagonal, jnp.zeros_like(on_diagonal)], axis=1)
    target[slot, half:, :] = jnp.where(tail_row == 0, first, rows).astype(BF16)


def unpack(source, slot, target, place):
    half = source.shape[1] - 16
    row = lax.broadcasted_iota(jnp.int32, (half, half), 0)
    col = lax.broadcasted_iota(jnp.int32, (half, half), 1)
    mixed = source[slot, :half, :half].astype(F32)
    across = source[slot, :half, half:].astype(F32)
    tail = source[slot, half:, :].astype(F32)
    mean = tail[1:2] + tail[2:3]
    left, right = mean[:, :half], mean[:, half:]
    turned = mixed.T
    target[place, :half, :half] = (jnp.where(row >= col, mixed, turned) + left).astype(BF16)
    target[place, :half, half:] = (across + right).astype(BF16)
    target[place, half:, :half] = (across.T + left).astype(BF16)
    corner = jnp.where(row < col, mixed, jnp.where(row == col, tail[0:1, :half], turned))
    target[place, half:, half:] = (corner + right).astype(BF16)


def first_kernel(
    ensemble_ref, dense_ref, value_ref, out_ref, beside_ref, corner_ref, below_ref, x_ref, pert_ref, high_ref, centre_ref, wide_ref, left_high, left_low
):
    members, patches, fields = ensemble_ref.shape
    total = jnp.zeros((patches, fields), F32)
    chunk = 32
    for k in range(0, members, chunk):
        part = ensemble_ref[k : k + chunk].astype(F32)
        total = total + jnp.sum(part, axis=0)
        wide_ref[k * patches : (k + chunk) * patches] = part.reshape(chunk * patches, fields)
    centre = total * (1.0 / members)
    centre_ref[...] = centre
    for p in range(patches):
        lanes = slice(p * fields, (p + 1) * fields)
        part = wide_ref[pl.ds(p, members, stride=patches), :]
        x_ref[:, lanes] = part.astype(BF16)
        pert = part - centre[p : p + 1, :]
        pert_ref[:, lanes] = pert
        high_ref[:, lanes] = pert.astype(BF16)
    shares((0, 1, 2), pert_ref, centre, dense_ref, value_ref, left_high, left_low)
    for slot, spread, twice in weights_of(3, x_ref, left_high, left_low, out_ref):
        if slot == 0:
            pack(corner_ref, 0, spread, twice)
            beside_ref[0] = corner_ref[0]
            below_ref[0] = corner_ref[0]
        else:
            pack(below_ref if slot == 1 else beside_ref, 1, spread, twice)


def second_kernel(x_ref, pert_ref, centre_ref, dense_ref, value_ref, one_ref, high_ref, mix_ref, out_ref, left_high, left_low, two_ref):
    patches, fields = centre_ref.shape
    shares((3,), pert_ref, centre_ref[...], dense_ref, value_ref, left_high, left_low)
    parts = ((0, one_ref, 0), (1, one_ref, 1), (3, one_ref, 2), (4, two_ref, 0))
    for _ in weights_of(1, x_ref, left_high, left_low, two_ref):
        pass
    for p in range(0, patches, 2):
        out_ref[:, p * fields : (p + 2) * fields] = blend(parts, high_ref, mix_ref, p)


def blend(parts, high_ref, mix_ref, p):
    fields = mix_ref.shape[2]
    lanes = slice(p * fields, (p + 2) * fields)
    total = None
    for t, ref, slot in parts:
        share = jnp.concatenate([mix_ref[t, p : p + 1, :], mix_ref[t, p + 1 : p + 2, :]], axis=1)
        moved = dot(ref[slot], high_ref[:, lanes])
        moved = jnp.where(share != 0.0, share * moved, 0.0)
        total = moved if total is None else total + moved
    return total


def arrivals(arrived, whole_ref):
    for place, (_, ref, slot) in enumerate(arrived):
        unpack(ref, slot, whole_ref, place)
    return [(t, whole_ref, place) for place, (t, _, _) in enumerate(arrived)]


def middle_kernel(beside_ref, below_ref, high_ref, mix_ref, partial_ref, out_ref, whole_ref):
    parts = arrivals(((2, beside_ref, 0), (5, beside_ref, 1), (6, below_ref, 0), (7, below_ref, 1)), whole_ref)
    fields = mix_ref.shape[2]
    for p in range(0, mix_ref.shape[1], 2):
        lanes = slice(p * fields, (p + 2) * fields)
        out_ref[:, lanes] = partial_ref[:, lanes] + blend(parts, high_ref, mix_ref, p)


def last_kernel(diagonal_ref, high_ref, mix_ref, partial_ref, centre_ref, out_ref, all_ref, whole_ref):
    parts = arrivals(((8, diagonal_ref, 0),), whole_ref)
    members, patches, fields = out_ref.shape
    for p in range(0, patches, 2):
        lanes = slice(p * fields, (p + 2) * fields)
        total = partial_ref[:, lanes] + blend(parts, high_ref, mix_ref, p)
        for q in range(2):
            part = total[:, q * fields : (q + 1) * fields] + centre_ref[p + q : p + q + 1, :]
            all_ref[pl.ds(p + q, members, stride=patches), :] = part
    chunk = 32
    for k in range(0, members, chunk):
        part = all_ref[k * patches : (k + chunk) * patches, :]
        out_ref[k : k + chunk] = part.reshape(chunk, patches, fields).astype(BF16)


def outgoing_kernel(source_ref, target_ref, held_ref, turned_ref, read, written):
    own, devices = source_ref.shape[:2]
    half = devices // 2
    spans = [slice(h * half, (h + 1) * half) for h in range(2)]
    inward = [pltpu.make_async_copy(source_ref.at[:, s], held_ref.at[:, s], read.at[h]) for h, s in enumerate(spans)]
    outward = [pltpu.make_async_copy(turned_ref.at[s], target_ref.at[s], written.at[h]) for h, s in enumerate(spans)]
    for copy in inward:
        copy.start()
    for copy, out, s in zip(inward, outward, spans):
        copy.wait()
        for m in range(own):
            turned_ref[s, m] = held_ref[m, s]
        out.start()
    for out in outward:
        out.wait()


def returned_kernel(source_ref, target_ref, done):
    copies = [pltpu.make_async_copy(source_ref.at[:, m], target_ref.at[m], done.at[m]) for m in range(target_ref.shape[0])]
    for copy in copies:
        copy.start()
    for copy in copies:
        copy.wait()


def call(kernel, outs, specs, scratch=(), to=VMEM):
    return pl.pallas_call(
        kernel,
        out_shape=outs,
        in_specs=specs,
        out_specs=jax.tree.map(lambda _: to, outs),
        scratch_shapes=list(scratch),
        compiler_params=pltpu.CompilerParams(vmem_limit_bytes=48 << 20),
    )


def per_device(background, obs_value, obs_error, obs_patch, obs_variable, obs_count, patch_corners, interp_weights):
    shape = jax.ShapeDtypeStruct
    devices = lax.axis_size("mem")
    regions = lax.axis_size("reg")
    own, _, all_patches, fields = background.shape
    patches = all_patches // devices
    members = own * devices
    points = obs_value.shape[0] * obs_value.shape[1]
    columns = patches * fields
    copies = [pltpu.SemaphoreType.DMA((own,))]

    blocks = (devices, own, patches, fields)
    outgoing = call(
        outgoing_kernel,
        shape(blocks, BF16),
        [HBM],
        [pltpu.VMEM((own,) + (devices,) + blocks[2:], BF16), pltpu.VMEM(blocks, BF16)] + [pltpu.SemaphoreType.DMA((2,))] * 2,
        HBM,
    )(pltpu.with_memory_space_constraint(background.reshape(own, devices, patches, fields), pltpu.HBM))
    ensemble = lax.all_to_all(outgoing, "mem", split_axis=0, concat_axis=0, tiled=True).reshape(members, patches, fields)
    dense, values, mix = call(
        prepare_kernel,
        (shape((points, patches, fields), F32), shape((points, patches, fields), F32), shape((9, patches, fields), F32)),
        [SMEM] + [VMEM] * 6,
    )(obs_count, obs_value, obs_error, obs_patch, obs_variable, patch_corners[0], interp_weights[0])

    packed = (members // 2 + 16, members)
    left = (members + 16, columns)
    flat = (members, columns)
    wide = pltpu.VMEM((members * patches, fields), F32)
    down = [((d + 1) % devices, d) for d in range(devices)]
    across = [(r + 1, r) for r in range(regions - 1)]
    both = [(d * regions + r, e * regions + t) for d, e in down for r, t in across]
    one, to_beside, to_corner, to_below, x, pert, high, centre = call(
        first_kernel,
        (
            shape((3, members, members), BF16),
            shape((2,) + packed, BF16),
            shape((1,) + packed, BF16),
            shape((2,) + packed, BF16),
            shape(flat, BF16),
            shape(flat, F32),
            shape(flat, BF16),
            shape((patches, fields), F32),
        ),
        [VMEM] * 3,
        [wide] + [pltpu.VMEM((3,) + left, BF16)] * 2,
    )(ensemble, dense, values)
    beside = lax.ppermute(to_beside, "reg", across)
    diagonal = lax.ppermute(to_corner, ("mem", "reg"), both)
    below = lax.ppermute(to_below, "mem", down)
    partial = call(
        second_kernel,
        shape(flat, F32),
        [VMEM] * 8,
        [pltpu.VMEM((1,) + left, BF16)] * 2 + [pltpu.VMEM((1, members, members), BF16)],
    )(x, pert, centre, dense, values, one, high, mix)
    partial = call(middle_kernel, shape(flat, F32), [VMEM] * 5, [pltpu.VMEM((4, members, members), BF16)])(
        beside, below, high, mix, partial
    )
    analysis = call(
        last_kernel,
        shape((members, patches, fields), BF16),
        [VMEM] * 5,
        [wide, pltpu.VMEM((1, members, members), BF16)],
    )(diagonal, high, mix, partial, centre)
    returned = lax.all_to_all(analysis.reshape(devices, own, patches, fields), "mem", split_axis=0, concat_axis=0, tiled=True)
    result = call(returned_kernel, shape((own, devices, patches, fields), BF16), [VMEM], copies, HBM)(returned)
    return result.reshape(own, 1, all_patches, fields)


def solution(mesh):
    placed = (
        P("mem", "reg", None, None),
        P("mem", "reg", None),
        P("mem", "reg", None),
        P("mem", "reg", None),
        P("mem", "reg", None),
        P("mem", "reg"),
        P("reg", "mem", None),
        P("reg", "mem", None),
    )
    return jax.shard_map(
        per_device,
        mesh=mesh,
        in_specs=placed,
        out_specs=P("mem", "reg", None, None),
        check_vma=False,
    )
```

```python
import jax
import jax.numpy as jnp
from jax import lax
from jax.experimental import pallas as pl
from jax.experimental.pallas import tpu as pltpu
from jax.sharding import PartitionSpec as P


F32 = jnp.float32
BF16 = jnp.bfloat16
VMEM = pl.BlockSpec(memory_space=pltpu.VMEM)
SMEM = pl.BlockSpec(memory_space=pltpu.SMEM)
HBM = pl.BlockSpec(memory_space=pltpu.HBM)
NN = (((1,), (0,)), ((), ()))
NT = (((1,), (1,)), ((), ()))


def dot(a, b, dims=NN):
    return lax.dot_general(a, b, dims, preferred_element_type=F32)


def split(x):
    high = x.astype(BF16)
    return high, (x - high.astype(F32)).astype(BF16)


def thirds(x):
    high = x.astype(BF16)
    rest = x - high.astype(F32)
    middle = rest.astype(BF16)
    return high, middle, (rest - middle.astype(F32)).astype(BF16)


def product(a, b):
    return dot(a[0], b[0]) + (dot(a[0], b[1]) + dot(a[1], b[0]))


def prepare_kernel(count_ref, value_ref, error_ref, patch_ref, var_ref, corner_ref, coeff_ref, dense_ref, value_out_ref, mix_ref):
    rows, cols, slots = value_ref.shape
    patches, fields = dense_ref.shape[1:]
    slot_index = lax.broadcasted_iota(jnp.int32, (1, slots), 1)
    field_index = lax.broadcasted_iota(jnp.int32, (fields, slots), 0)
    patch_index = lax.broadcasted_iota(jnp.int32, (patches, slots), 0)
    for a in range(rows):
        for b in range(cols):
            weight = jnp.where(slot_index < count_ref[a, b], 1.0 / error_ref[a, b : b + 1, :], 0.0)
            weighted = weight * value_ref[a, b : b + 1, :]
            chosen = (field_index == var_ref[a, b : b + 1, :]).astype(F32).astype(BF16)
            at_patch = patch_index == patch_ref[a, b : b + 1, :]
            left = jnp.concatenate([jnp.where(at_patch, x, 0.0) for x in (weight, weighted)], axis=0)
            high, middle, low = (dot(x, chosen, NT) for x in thirds(left))
            sums = high + (middle + low)
            dense_ref[a * cols + b] = sums[:patches]
            value_out_ref[a * cols + b] = sums[patches:]
    corners, coeffs = corner_ref[...], coeff_ref[...]
    for t in range(mix_ref.shape[0]):
        used = jnp.sum(jnp.where(corners == t, coeffs, 0.0), axis=1, keepdims=True)
        mix_ref[t] = jnp.broadcast_to(used, (patches, fields))


def shares(points, pert_ref, centre, dense_ref, value_ref, left_high, left_low):
    members = pert_ref.shape[0]
    patches, fields = centre.shape
    pulls = [value_ref[n] - dense_ref[n] * centre for n in points]
    for p in range(patches):
        lanes = slice(p * fields, (p + 1) * fields)
        pert = pert_ref[:, lanes]
        for slot, n in enumerate(points):
            left_high[slot, :members, lanes], left_low[slot, :members, lanes] = split(pert * dense_ref[n, p : p + 1, :])
            tail = jnp.broadcast_to(pulls[slot][p : p + 1, :], (left_high.shape[1] - members, fields))
            left_high[slot, members:, lanes], left_low[slot, members:, lanes] = split(tail)


def add_diagonal(x, value, diagonal):
    half = diagonal.shape[0]
    step = jnp.where(diagonal, value, 0.0)
    top = jnp.concatenate([x[:half, :half] + step, x[:half, half:]], axis=1)
    bottom = jnp.concatenate([x[half:, :half], x[half:, half:] + step], axis=1)
    return jnp.concatenate([top, bottom], axis=0)


def two_factors(x, parts, diagonal):
    square = product(parts, parts)
    inner = add_diagonal(square - 4.5 * x, 6.75, diagonal)
    return add_diagonal(product(split(square), split(inner)) - 4.875 * x, 2.25, diagonal)


def later_factors(x):
    rounded = x.astype(BF16)
    square = dot(rounded, rounded)
    return 1.5 * square - x + dot(square.astype(BF16), (square - 2.5 * x).astype(BF16))


def weights_of(count, x_ref, left_high, left_low, out_ref, fill=lambda: None):
    members = x_ref.shape[0]
    half = members // 2
    row = lax.broadcasted_iota(jnp.int32, (half, half), 0)
    col = lax.broadcasted_iota(jnp.int32, (half, half), 1)
    diagonal = row == col
    slots = range(count)
    state = []
    for slot in slots:
        columns = x_ref[...]
        both = dot(left_high[slot], columns, NT) + dot(left_low[slot], columns, NT)
        both = both - jnp.sum(both, axis=1, keepdims=True) * (1.0 / members)
        gram, projected = both[:members], both[members : members + 1]
        on_diagonal = jnp.where(diagonal, gram[:half, :half] + gram[half:, half:], 0.0)
        trace = jnp.sum(jnp.sum(on_diagonal, axis=0, keepdims=True), axis=1, keepdims=True)
        scaling = (members - 1.0) + trace / members
        half_inverse = 0.5 / scaling
        state.append((projected, scaling, add_diagonal(gram * half_inverse, (members - 1.0) * half_inverse, diagonal)))
    parts = [split(x) for _, _, x in state]
    roots = [two_factors(state[s][2], parts[s], diagonal) for s in slots]
    fill()
    z = [split(x) for x in roots]
    y = [split(product(parts[s], z[s])) for s in slots]
    fill()
    excess = [add_diagonal(product(y[s], z[s]), -0.5, diagonal) for s in slots]
    fill()
    rest = [later_factors(x) for x in excess]
    fill()
    inverses = [roots[s] + rest[s] + dot(rest[s].astype(BF16), add_diagonal(roots[s], -1.0, diagonal).astype(BF16)) for s in slots]
    for slot in slots:
        projected, scaling, _ = state[slot]
        inverse = inverses[slot]
        once = jnp.sum(inverse * projected, axis=1, keepdims=True)
        twice = jnp.sum(inverse * once, axis=0, keepdims=True) / scaling
        spread = jnp.sqrt((members - 1.0) / scaling) * inverse
        out_ref[slot] = (spread + twice).astype(BF16)
        yield slot, spread, twice


def pack(target, slot, spread, twice):
    members = spread.shape[0]
    half = members // 2
    small_row = lax.broadcasted_iota(jnp.int32, (half, half), 0)
    small_col = lax.broadcasted_iota(jnp.int32, (half, half), 1)
    tail_row = lax.broadcasted_iota(jnp.int32, (16, members), 0)
    corner = spread[half:, half:]
    target[slot, :half, :half] = jnp.where(small_row >= small_col, spread[:half, :half], corner).astype(BF16)
    target[slot, :half, half:] = spread[:half, half:].astype(BF16)
    on_diagonal = jnp.sum(jnp.where(small_row == small_col, corner, 0.0), axis=0, keepdims=True)
    high, low = split(twice)
    rows = jnp.where(tail_row == 1, high.astype(F32), jnp.where(tail_row == 2, low.astype(F32), 0.0))
    first = jnp.concatenate([on_diagonal, jnp.zeros_like(on_diagonal)], axis=1)
    target[slot, half:, :] = jnp.where(tail_row == 0, first, rows).astype(BF16)


def unpack(source, slot, target, place):
    half = source.shape[1] - 16
    row = lax.broadcasted_iota(jnp.int32, (half, half), 0)
    col = lax.broadcasted_iota(jnp.int32, (half, half), 1)
    mixed = source[slot, :half, :half].astype(F32)
    across = source[slot, :half, half:].astype(F32)
    tail = source[slot, half:, :].astype(F32)
    mean = tail[1:2] + tail[2:3]
    left, right = mean[:, :half], mean[:, half:]
    turned = mixed.T
    target[place, :half, :half] = (jnp.where(row >= col, mixed, turned) + left).astype(BF16)
    target[place, :half, half:] = (across + right).astype(BF16)
    target[place, half:, :half] = (across.T + left).astype(BF16)
    corner = jnp.where(row < col, mixed, jnp.where(row == col, tail[0:1, :half], turned))
    target[place, half:, half:] = (corner + right).astype(BF16)


def first_kernel(
    ensemble_ref, dense_ref, value_ref, out_ref, beside_ref, corner_ref, below_ref, x_ref, pert_ref, high_ref, centre_ref, wide_ref, left_high, left_low
):
    members, patches, fields = ensemble_ref.shape
    total = jnp.zeros((patches, fields), F32)
    chunk = 32
    for k in range(0, members, chunk):
        part = ensemble_ref[k : k + chunk].astype(F32)
        total = total + jnp.sum(part, axis=0)
        wide_ref[k * patches : (k + chunk) * patches] = part.reshape(chunk * patches, fields)
    centre = total * (1.0 / members)
    centre_ref[...] = centre
    for p in range(patches):
        lanes = slice(p * fields, (p + 1) * fields)
        part = wide_ref[pl.ds(p, members, stride=patches), :]
        x_ref[:, lanes] = part.astype(BF16)
        pert = part - centre[p : p + 1, :]
        pert_ref[:, lanes] = pert
        high_ref[:, lanes] = pert.astype(BF16)
    shares((0, 1, 2), pert_ref, centre, dense_ref, value_ref, left_high, left_low)
    for slot, spread, twice in weights_of(3, x_ref, left_high, left_low, out_ref):
        if slot == 0:
            pack(corner_ref, 0, spread, twice)
            beside_ref[0] = corner_ref[0]
            below_ref[0] = corner_ref[0]
        else:
            pack(below_ref if slot == 1 else beside_ref, 1, spread, twice)


def second_kernel(x_ref, pert_ref, centre_ref, dense_ref, value_ref, one_ref, high_ref, mix_ref, out_ref, two_ref, left_high, left_low):
    patches, fields = centre_ref.shape
    tiles = iter(range(0, patches, 2))

    def fill():
        p = next(tiles)
        parts = ((0, one_ref, 0), (1, one_ref, 1), (3, one_ref, 2))
        out_ref[:, p * fields : (p + 2) * fields] = blend(parts, high_ref, mix_ref, p)

    shares((3,), pert_ref, centre_ref[...], dense_ref, value_ref, left_high, left_low)
    for _ in weights_of(1, x_ref, left_high, left_low, two_ref, fill):
        pass


def blend(parts, high_ref, mix_ref, p):
    fields = mix_ref.shape[2]
    lanes = slice(p * fields, (p + 2) * fields)
    total = None
    for t, ref, slot in parts:
        share = jnp.concatenate([mix_ref[t, p : p + 1, :], mix_ref[t, p + 1 : p + 2, :]], axis=1)
        moved = dot(ref[slot], high_ref[:, lanes])
        moved = jnp.where(share != 0.0, share * moved, 0.0)
        total = moved if total is None else total + moved
    return total


def arrivals(arrived, whole_ref):
    for place, (_, ref, slot) in enumerate(arrived):
        unpack(ref, slot, whole_ref, place)
    return [(t, whole_ref, place) for place, (t, _, _) in enumerate(arrived)]


def middle_kernel(beside_ref, below_ref, two_ref, high_ref, mix_ref, partial_ref, out_ref, whole_ref):
    parts = arrivals(((2, beside_ref, 0), (5, beside_ref, 1), (6, below_ref, 0), (7, below_ref, 1)), whole_ref) + [(4, two_ref, 0)]
    fields = mix_ref.shape[2]
    for p in range(0, mix_ref.shape[1], 2):
        lanes = slice(p * fields, (p + 2) * fields)
        out_ref[:, lanes] = partial_ref[:, lanes] + blend(parts, high_ref, mix_ref, p)


def last_kernel(diagonal_ref, high_ref, mix_ref, partial_ref, centre_ref, out_ref, all_ref, whole_ref):
    parts = arrivals(((8, diagonal_ref, 0),), whole_ref)
    members, patches, fields = out_ref.shape
    for p in range(0, patches, 2):
        lanes = slice(p * fields, (p + 2) * fields)
        total = partial_ref[:, lanes] + blend(parts, high_ref, mix_ref, p)
        for q in range(2):
            part = total[:, q * fields : (q + 1) * fields] + centre_ref[p + q : p + q + 1, :]
            all_ref[pl.ds(p + q, members, stride=patches), :] = part
    chunk = 32
    for k in range(0, members, chunk):
        part = all_ref[k * patches : (k + chunk) * patches, :]
        out_ref[k : k + chunk] = part.reshape(chunk, patches, fields).astype(BF16)


def outgoing_kernel(source_ref, target_ref, held_ref, turned_ref, read, written):
    own, devices = source_ref.shape[:2]
    half = devices // 2
    spans = [slice(h * half, (h + 1) * half) for h in range(2)]
    inward = [pltpu.make_async_copy(source_ref.at[:, s], held_ref.at[:, s], read.at[h]) for h, s in enumerate(spans)]
    outward = [pltpu.make_async_copy(turned_ref.at[s], target_ref.at[s], written.at[h]) for h, s in enumerate(spans)]
    for copy in inward:
        copy.start()
    for copy, out, s in zip(inward, outward, spans):
        copy.wait()
        for m in range(own):
            turned_ref[s, m] = held_ref[m, s]
        out.start()
    for out in outward:
        out.wait()


def returned_kernel(source_ref, target_ref, done):
    copies = [pltpu.make_async_copy(source_ref.at[:, m], target_ref.at[m], done.at[m]) for m in range(target_ref.shape[0])]
    for copy in copies:
        copy.start()
    for copy in copies:
        copy.wait()


def call(kernel, outs, specs, scratch=(), to=VMEM):
    return pl.pallas_call(
        kernel,
        out_shape=outs,
        in_specs=specs,
        out_specs=jax.tree.map(lambda _: to, outs),
        scratch_shapes=list(scratch),
        compiler_params=pltpu.CompilerParams(vmem_limit_bytes=48 << 20),
    )


def per_device(background, obs_value, obs_error, obs_patch, obs_variable, obs_count, patch_corners, interp_weights):
    shape = jax.ShapeDtypeStruct
    devices = lax.axis_size("mem")
    regions = lax.axis_size("reg")
    own, _, all_patches, fields = background.shape
    patches = all_patches // devices
    members = own * devices
    points = obs_value.shape[0] * obs_value.shape[1]
    columns = patches * fields
    copies = [pltpu.SemaphoreType.DMA((own,))]

    blocks = (devices, own, patches, fields)
    outgoing = call(
        outgoing_kernel,
        shape(blocks, BF16),
        [HBM],
        [pltpu.VMEM((own,) + (devices,) + blocks[2:], BF16), pltpu.VMEM(blocks, BF16)] + [pltpu.SemaphoreType.DMA((2,))] * 2,
        HBM,
    )(pltpu.with_memory_space_constraint(background.reshape(own, devices, patches, fields), pltpu.HBM))
    ensemble = lax.all_to_all(outgoing, "mem", split_axis=0, concat_axis=0, tiled=True).reshape(members, patches, fields)
    dense, values, mix = call(
        prepare_kernel,
        (shape((points, patches, fields), F32), shape((points, patches, fields), F32), shape((9, patches, fields), F32)),
        [SMEM] + [VMEM] * 6,
    )(obs_count, obs_value, obs_error, obs_patch, obs_variable, patch_corners[0], interp_weights[0])

    packed = (members // 2 + 16, members)
    left = (members + 16, columns)
    flat = (members, columns)
    wide = pltpu.VMEM((members * patches, fields), F32)
    down = [((d + 1) % devices, d) for d in range(devices)]
    across = [(r + 1, r) for r in range(regions - 1)]
    both = [(d * regions + r, e * regions + t) for d, e in down for r, t in across]
    one, to_beside, to_corner, to_below, x, pert, high, centre = call(
        first_kernel,
        (
            shape((3, members, members), BF16),
            shape((2,) + packed, BF16),
            shape((1,) + packed, BF16),
            shape((2,) + packed, BF16),
            shape(flat, BF16),
            shape(flat, F32),
            shape(flat, BF16),
            shape((patches, fields), F32),
        ),
        [VMEM] * 3,
        [wide] + [pltpu.VMEM((3,) + left, BF16)] * 2,
    )(ensemble, dense, values)
    beside = lax.ppermute(to_beside, "reg", across)
    diagonal = lax.ppermute(to_corner, ("mem", "reg"), both)
    below = lax.ppermute(to_below, "mem", down)
    partial, two = call(
        second_kernel,
        (shape(flat, F32), shape((1, members, members), BF16)),
        [VMEM] * 8,
        [pltpu.VMEM((1,) + left, BF16)] * 2,
    )(x, pert, centre, dense, values, one, high, mix)
    partial = call(middle_kernel, shape(flat, F32), [VMEM] * 6, [pltpu.VMEM((4, members, members), BF16)])(
        beside, below, two, high, mix, partial
    )
    analysis = call(
        last_kernel,
        shape((members, patches, fields), BF16),
        [VMEM] * 5,
        [wide, pltpu.VMEM((1, members, members), BF16)],
    )(diagonal, high, mix, partial, centre)
    returned = lax.all_to_all(analysis.reshape(devices, own, patches, fields), "mem", split_axis=0, concat_axis=0, tiled=True)
    result = call(returned_kernel, shape((own, devices, patches, fields), BF16), [VMEM], copies, HBM)(returned)
    return result.reshape(own, 1, all_patches, fields)


def solution(mesh):
    placed = (
        P("mem", "reg", None, None),
        P("mem", "reg", None),
        P("mem", "reg", None),
        P("mem", "reg", None),
        P("mem", "reg", None),
        P("mem", "reg"),
        P("reg", "mem", None),
        P("reg", "mem", None),
    )
    return jax.shard_map(
        per_device,
        mesh=mesh,
        in_specs=placed,
        out_specs=P("mem", "reg", None, None),
        check_vma=False,
    )
```

```python
import jax
import jax.numpy as jnp
from jax import lax
from jax.experimental import pallas as pl
from jax.experimental.pallas import tpu as pltpu
from jax.sharding import PartitionSpec as P


F32 = jnp.float32
BF16 = jnp.bfloat16
VMEM = pl.BlockSpec(memory_space=pltpu.VMEM)
SMEM = pl.BlockSpec(memory_space=pltpu.SMEM)
HBM = pl.BlockSpec(memory_space=pltpu.HBM)
NN = (((1,), (0,)), ((), ()))
NT = (((1,), (1,)), ((), ()))


def dot(a, b, dims=NN):
    return lax.dot_general(a, b, dims, preferred_element_type=F32)


def split(x):
    high = x.astype(BF16)
    return high, (x - high.astype(F32)).astype(BF16)


def thirds(x):
    high = x.astype(BF16)
    rest = x - high.astype(F32)
    middle = rest.astype(BF16)
    return high, middle, (rest - middle.astype(F32)).astype(BF16)


def product(a, b):
    return dot(a[0], b[0]) + (dot(a[0], b[1]) + dot(a[1], b[0]))


def prepare_kernel(count_ref, value_ref, error_ref, patch_ref, var_ref, corner_ref, coeff_ref, dense_ref, value_out_ref, mix_ref):
    rows, cols, slots = value_ref.shape
    patches, fields = dense_ref.shape[1:]
    slot_index = lax.broadcasted_iota(jnp.int32, (1, slots), 1)
    field_index = lax.broadcasted_iota(jnp.int32, (fields, slots), 0)
    patch_index = lax.broadcasted_iota(jnp.int32, (patches, slots), 0)
    for a in range(rows):
        for b in range(cols):
            weight = jnp.where(slot_index < count_ref[a, b], 1.0 / error_ref[a, b : b + 1, :], 0.0)
            weighted = weight * value_ref[a, b : b + 1, :]
            chosen = (field_index == var_ref[a, b : b + 1, :]).astype(F32).astype(BF16)
            at_patch = patch_index == patch_ref[a, b : b + 1, :]
            left = jnp.concatenate([jnp.where(at_patch, x, 0.0) for x in (weight, weighted)], axis=0)
            high, middle, low = (dot(x, chosen, NT) for x in thirds(left))
            sums = high + (middle + low)
            dense_ref[a * cols + b] = sums[:patches]
            value_out_ref[a * cols + b] = sums[patches:]
    corners, coeffs = corner_ref[...], coeff_ref[...]
    for t in range(mix_ref.shape[0]):
        used = jnp.sum(jnp.where(corners == t, coeffs, 0.0), axis=1, keepdims=True)
        mix_ref[t] = jnp.broadcast_to(used, (patches, fields))


def shares(points, pert_ref, centre, dense_ref, value_ref, left_high, left_low):
    members = pert_ref.shape[0]
    patches, fields = centre.shape
    pulls = [value_ref[n] - dense_ref[n] * centre for n in points]
    for p in range(patches):
        lanes = slice(p * fields, (p + 1) * fields)
        pert = pert_ref[:, lanes]
        for slot, n in enumerate(points):
            left_high[slot, :members, lanes], left_low[slot, :members, lanes] = split(pert * dense_ref[n, p : p + 1, :])
            tail = jnp.broadcast_to(pulls[slot][p : p + 1, :], (left_high.shape[1] - members, fields))
            left_high[slot, members:, lanes], left_low[slot, members:, lanes] = split(tail)


def add_diagonal(x, value, diagonal):
    half = diagonal.shape[0]
    step = jnp.where(diagonal, value, 0.0)
    top = jnp.concatenate([x[:half, :half] + step, x[:half, half:]], axis=1)
    bottom = jnp.concatenate([x[half:, :half], x[half:, half:] + step], axis=1)
    return jnp.concatenate([top, bottom], axis=0)


def two_factors(x, parts, diagonal):
    square = product(parts, parts)
    inner = add_diagonal(square - 4.5 * x, 6.75, diagonal)
    return add_diagonal(product(split(square), split(inner)) - 4.875 * x, 2.25, diagonal)


def later_factors(x):
    rounded = x.astype(BF16)
    square = dot(rounded, rounded)
    return 1.5 * square - x + dot(square.astype(BF16), (square - 2.5 * x).astype(BF16))


def weights_of(count, x_ref, left_high, left_low, out_ref, fill=lambda: None):
    members = x_ref.shape[0]
    half = members // 2
    row = lax.broadcasted_iota(jnp.int32, (half, half), 0)
    col = lax.broadcasted_iota(jnp.int32, (half, half), 1)
    diagonal = row == col
    slots = range(count)
    state = []
    for slot in slots:
        columns = x_ref[...]
        both = dot(left_high[slot], columns, NT) + dot(left_low[slot], columns, NT)
        both = both - jnp.sum(both, axis=1, keepdims=True) * (1.0 / members)
        gram, projected = both[:members], both[members : members + 1]
        on_diagonal = jnp.where(diagonal, gram[:half, :half] + gram[half:, half:], 0.0)
        trace = jnp.sum(jnp.sum(on_diagonal, axis=0, keepdims=True), axis=1, keepdims=True)
        scaling = (members - 1.0) + trace / members
        half_inverse = 0.5 / scaling
        state.append((projected, scaling, add_diagonal(gram * half_inverse, (members - 1.0) * half_inverse, diagonal)))
    parts = [split(x) for _, _, x in state]
    roots = [two_factors(state[s][2], parts[s], diagonal) for s in slots]
    fill()
    z = [split(x) for x in roots]
    y = [split(product(parts[s], z[s])) for s in slots]
    fill()
    excess = [add_diagonal(product(y[s], z[s]), -0.5, diagonal) for s in slots]
    fill()
    rest = [later_factors(x) for x in excess]
    fill()
    inverses = [roots[s] + rest[s] + dot(rest[s].astype(BF16), add_diagonal(roots[s], -1.0, diagonal).astype(BF16)) for s in slots]
    for slot in slots:
        projected, scaling, _ = state[slot]
        inverse = inverses[slot]
        once = jnp.sum(inverse * projected, axis=1, keepdims=True)
        twice = jnp.sum(inverse * once, axis=0, keepdims=True) / scaling
        spread = jnp.sqrt((members - 1.0) / scaling) * inverse
        out_ref[slot] = (spread + twice).astype(BF16)
        yield slot, spread, twice


def pack(target, slot, spread, twice):
    members = spread.shape[0]
    half = members // 2
    small_row = lax.broadcasted_iota(jnp.int32, (half, half), 0)
    small_col = lax.broadcasted_iota(jnp.int32, (half, half), 1)
    tail_row = lax.broadcasted_iota(jnp.int32, (16, members), 0)
    corner = spread[half:, half:]
    target[slot, :half, :half] = jnp.where(small_row >= small_col, spread[:half, :half], corner).astype(BF16)
    target[slot, :half, half:] = spread[:half, half:].astype(BF16)
    on_diagonal = jnp.sum(jnp.where(small_row == small_col, corner, 0.0), axis=0, keepdims=True)
    high, low = split(twice)
    rows = jnp.where(tail_row == 1, high.astype(F32), jnp.where(tail_row == 2, low.astype(F32), 0.0))
    first = jnp.concatenate([on_diagonal, jnp.zeros_like(on_diagonal)], axis=1)
    target[slot, half:, :] = jnp.where(tail_row == 0, first, rows).astype(BF16)


def unpack(source, slot, target, place):
    half = source.shape[1] - 16
    row = lax.broadcasted_iota(jnp.int32, (half, half), 0)
    col = lax.broadcasted_iota(jnp.int32, (half, half), 1)
    mixed = source[slot, :half, :half].astype(F32)
    across = source[slot, :half, half:].astype(F32)
    tail = source[slot, half:, :].astype(F32)
    mean = tail[1:2] + tail[2:3]
    left, right = mean[:, :half], mean[:, half:]
    turned = mixed.T
    target[place, :half, :half] = (jnp.where(row >= col, mixed, turned) + left).astype(BF16)
    target[place, :half, half:] = (across + right).astype(BF16)
    target[place, half:, :half] = (across.T + left).astype(BF16)
    corner = jnp.where(row < col, mixed, jnp.where(row == col, tail[0:1, :half], turned))
    target[place, half:, half:] = (corner + right).astype(BF16)


def first_kernel(
    ensemble_ref, dense_ref, value_ref, out_ref, corner_ref, below_ref, x_ref, pert_ref, high_ref, centre_ref, wide_ref, left_high, left_low
):
    members, patches, fields = ensemble_ref.shape
    total = jnp.zeros((patches, fields), F32)
    chunk = 32
    for k in range(0, members, chunk):
        part = ensemble_ref[k : k + chunk].astype(F32)
        total = total + jnp.sum(part, axis=0)
        wide_ref[k * patches : (k + chunk) * patches] = part.reshape(chunk * patches, fields)
    centre = total * (1.0 / members)
    centre_ref[...] = centre
    for p in range(patches):
        lanes = slice(p * fields, (p + 1) * fields)
        part = wide_ref[pl.ds(p, members, stride=patches), :]
        x_ref[:, lanes] = part.astype(BF16)
        pert = part - centre[p : p + 1, :]
        pert_ref[:, lanes] = pert
        high_ref[:, lanes] = pert.astype(BF16)
    shares((0, 1), pert_ref, centre, dense_ref, value_ref, left_high, left_low)
    for slot, spread, twice in weights_of(2, x_ref, left_high, left_low, out_ref):
        pack(below_ref, slot, spread, twice)
        if slot == 0:
            corner_ref[0] = below_ref[0]


def second_kernel(
    x_ref, pert_ref, centre_ref, dense_ref, value_ref, one_ref, corner_ref, high_ref, mix_ref, out_ref, two_ref, beside_ref, left_high, left_low
):
    patches, fields = centre_ref.shape
    tiles = iter(range(0, patches, 2))

    def fill():
        p = next(tiles)
        out_ref[:, p * fields : (p + 2) * fields] = blend(((0, one_ref, 0), (1, one_ref, 1)), high_ref, mix_ref, p)

    beside_ref[0] = corner_ref[0]
    shares((2, 3), pert_ref, centre_ref[...], dense_ref, value_ref, left_high, left_low)
    for slot, spread, twice in weights_of(2, x_ref, left_high, left_low, two_ref, fill):
        if slot == 0:
            pack(beside_ref, 1, spread, twice)


def blend(parts, high_ref, mix_ref, p):
    fields = mix_ref.shape[2]
    lanes = slice(p * fields, (p + 2) * fields)
    total = None
    for t, ref, slot in parts:
        share = jnp.concatenate([mix_ref[t, p : p + 1, :], mix_ref[t, p + 1 : p + 2, :]], axis=1)
        moved = dot(ref[slot], high_ref[:, lanes])
        moved = jnp.where(share != 0.0, share * moved, 0.0)
        total = moved if total is None else total + moved
    return total


def arrivals(arrived, whole_ref):
    for place, (_, ref, slot) in enumerate(arrived):
        unpack(ref, slot, whole_ref, place)
    return [(t, whole_ref, place) for place, (t, _, _) in enumerate(arrived)]


def middle_kernel(below_ref, diagonal_ref, two_ref, high_ref, mix_ref, partial_ref, out_ref, whole_ref):
    parts = arrivals(((6, below_ref, 0), (7, below_ref, 1), (8, diagonal_ref, 0)), whole_ref) + [(3, two_ref, 0), (4, two_ref, 1)]
    fields = mix_ref.shape[2]
    for p in range(0, mix_ref.shape[1], 2):
        lanes = slice(p * fields, (p + 2) * fields)
        out_ref[:, lanes] = partial_ref[:, lanes] + blend(parts, high_ref, mix_ref, p)


def last_kernel(beside_ref, high_ref, mix_ref, partial_ref, centre_ref, out_ref, all_ref, whole_ref):
    parts = arrivals(((2, beside_ref, 0), (5, beside_ref, 1)), whole_ref)
    members, patches, fields = out_ref.shape
    for p in range(0, patches, 2):
        lanes = slice(p * fields, (p + 2) * fields)
        total = partial_ref[:, lanes] + blend(parts, high_ref, mix_ref, p)
        for q in range(2):
            part = total[:, q * fields : (q + 1) * fields] + centre_ref[p + q : p + q + 1, :]
            all_ref[pl.ds(p + q, members, stride=patches), :] = part
    chunk = 32
    for k in range(0, members, chunk):
        part = all_ref[k * patches : (k + chunk) * patches, :]
        out_ref[k : k + chunk] = part.reshape(chunk, patches, fields).astype(BF16)


def outgoing_kernel(source_ref, target_ref, held_ref, turned_ref, read, written):
    own, devices = source_ref.shape[:2]
    half = devices // 2
    spans = [slice(h * half, (h + 1) * half) for h in range(2)]
    inward = [pltpu.make_async_copy(source_ref.at[:, s], held_ref.at[:, s], read.at[h]) for h, s in enumerate(spans)]
    outward = [pltpu.make_async_copy(turned_ref.at[s], target_ref.at[s], written.at[h]) for h, s in enumerate(spans)]
    for copy in inward:
        copy.start()
    for copy, out, s in zip(inward, outward, spans):
        copy.wait()
        for m in range(own):
            turned_ref[s, m] = held_ref[m, s]
        out.start()
    for out in outward:
        out.wait()


def returned_kernel(source_ref, target_ref, done):
    copies = [pltpu.make_async_copy(source_ref.at[:, m], target_ref.at[m], done.at[m]) for m in range(target_ref.shape[0])]
    for copy in copies:
        copy.start()
    for copy in copies:
        copy.wait()


def call(kernel, outs, specs, scratch=(), to=VMEM):
    return pl.pallas_call(
        kernel,
        out_shape=outs,
        in_specs=specs,
        out_specs=jax.tree.map(lambda _: to, outs),
        scratch_shapes=list(scratch),
        compiler_params=pltpu.CompilerParams(vmem_limit_bytes=48 << 20),
    )


def per_device(background, obs_value, obs_error, obs_patch, obs_variable, obs_count, patch_corners, interp_weights):
    shape = jax.ShapeDtypeStruct
    devices = lax.axis_size("mem")
    regions = lax.axis_size("reg")
    own, _, all_patches, fields = background.shape
    patches = all_patches // devices
    members = own * devices
    points = obs_value.shape[0] * obs_value.shape[1]
    columns = patches * fields
    copies = [pltpu.SemaphoreType.DMA((own,))]

    blocks = (devices, own, patches, fields)
    outgoing = call(
        outgoing_kernel,
        shape(blocks, BF16),
        [HBM],
        [pltpu.VMEM((own,) + (devices,) + blocks[2:], BF16), pltpu.VMEM(blocks, BF16)] + [pltpu.SemaphoreType.DMA((2,))] * 2,
        HBM,
    )(pltpu.with_memory_space_constraint(background.reshape(own, devices, patches, fields), pltpu.HBM))
    ensemble = lax.all_to_all(outgoing, "mem", split_axis=0, concat_axis=0, tiled=True).reshape(members, patches, fields)
    dense, values, mix = call(
        prepare_kernel,
        (shape((points, patches, fields), F32), shape((points, patches, fields), F32), shape((9, patches, fields), F32)),
        [SMEM] + [VMEM] * 6,
    )(obs_count, obs_value, obs_error, obs_patch, obs_variable, patch_corners[0], interp_weights[0])

    packed = (members // 2 + 16, members)
    left = (members + 16, columns)
    flat = (members, columns)
    wide = pltpu.VMEM((members * patches, fields), F32)
    down = [((d + 1) % devices, d) for d in range(devices)]
    across = [(r + 1, r) for r in range(regions - 1)]
    both = [(d * regions + r, e * regions + t) for d, e in down for r, t in across]
    pair = shape((2, members, members), BF16)
    lefts = [pltpu.VMEM((2,) + left, BF16)] * 2
    one, to_corner, to_below, x, pert, high, centre = call(
        first_kernel,
        (
            pair,
            shape((1,) + packed, BF16),
            shape((2,) + packed, BF16),
            shape(flat, BF16),
            shape(flat, F32),
            shape(flat, BF16),
            shape((patches, fields), F32),
        ),
        [VMEM] * 3,
        [wide] + lefts,
    )(ensemble, dense, values)
    diagonal = lax.ppermute(to_corner, ("mem", "reg"), both)
    below = lax.ppermute(to_below, "mem", down)
    partial, two, to_beside = call(second_kernel, (shape(flat, F32), pair, shape((2,) + packed, BF16)), [VMEM] * 9, lefts)(
        x, pert, centre, dense, values, one, to_corner, high, mix
    )
    beside = lax.ppermute(to_beside, "reg", across)
    partial = call(middle_kernel, shape(flat, F32), [VMEM] * 6, [pltpu.VMEM((3, members, members), BF16)])(
        below, diagonal, two, high, mix, partial
    )
    analysis = call(
        last_kernel,
        shape((members, patches, fields), BF16),
        [VMEM] * 5,
        [wide, pltpu.VMEM((2, members, members), BF16)],
    )(beside, high, mix, partial, centre)
    returned = lax.all_to_all(analysis.reshape(devices, own, patches, fields), "mem", split_axis=0, concat_axis=0, tiled=True)
    result = call(returned_kernel, shape((own, devices, patches, fields), BF16), [VMEM], copies, HBM)(returned)
    return result.reshape(own, 1, all_patches, fields)


def solution(mesh):
    placed = (
        P("mem", "reg", None, None),
        P("mem", "reg", None),
        P("mem", "reg", None),
        P("mem", "reg", None),
        P("mem", "reg", None),
        P("mem", "reg"),
        P("reg", "mem", None),
        P("reg", "mem", None),
    )
    return jax.shard_map(
        per_device,
        mesh=mesh,
        in_specs=placed,
        out_specs=P("mem", "reg", None, None),
        check_vma=False,
    )
```

```python
import jax
import jax.numpy as jnp
from jax import lax
from jax.experimental import pallas as pl
from jax.experimental.pallas import tpu as pltpu
from jax.sharding import PartitionSpec as P


F32 = jnp.float32
BF16 = jnp.bfloat16
VMEM = pl.BlockSpec(memory_space=pltpu.VMEM)
SMEM = pl.BlockSpec(memory_space=pltpu.SMEM)
HBM = pl.BlockSpec(memory_space=pltpu.HBM)
NN = (((1,), (0,)), ((), ()))
NT = (((1,), (1,)), ((), ()))


def dot(a, b, dims=NN):
    return lax.dot_general(a, b, dims, preferred_element_type=F32)


def split(x):
    high = x.astype(BF16)
    return high, (x - high.astype(F32)).astype(BF16)


def thirds(x):
    high = x.astype(BF16)
    rest = x - high.astype(F32)
    middle = rest.astype(BF16)
    return high, middle, (rest - middle.astype(F32)).astype(BF16)


def product(a, b):
    return dot(a[0], b[0]) + (dot(a[0], b[1]) + dot(a[1], b[0]))


def prepare(count_ref, value_ref, error_ref, patch_ref, var_ref, corner_ref, coeff_ref, dense_ref, value_out_ref, mix_ref):
    rows, cols, slots = value_ref.shape
    patches, fields = dense_ref.shape[1:]
    slot_index = lax.broadcasted_iota(jnp.int32, (1, slots), 1)
    field_index = lax.broadcasted_iota(jnp.int32, (fields, slots), 0)
    patch_index = lax.broadcasted_iota(jnp.int32, (patches, slots), 0)
    for a in range(rows):
        for b in range(cols):
            weight = jnp.where(slot_index < count_ref[a : a + 1, b : b + 1], 1.0 / error_ref[a, b : b + 1, :], 0.0)
            weighted = weight * value_ref[a, b : b + 1, :]
            chosen = (field_index == var_ref[a, b : b + 1, :]).astype(F32).astype(BF16)
            at_patch = patch_index == patch_ref[a, b : b + 1, :]
            left = jnp.concatenate([jnp.where(at_patch, x, 0.0) for x in (weight, weighted)], axis=0)
            high, middle, low = (dot(x, chosen, NT) for x in thirds(left))
            sums = high + (middle + low)
            dense_ref[a * cols + b] = sums[:patches]
            value_out_ref[a * cols + b] = sums[patches:]
    corners, coeffs = corner_ref[...], coeff_ref[...]
    square = (patches, patches)
    own_place = lax.broadcasted_iota(jnp.int32, square, 0) == lax.broadcasted_iota(jnp.int32, square, 1)
    for t in range(mix_ref.shape[0]):
        used = jnp.sum(jnp.where(corners == t, coeffs, 0.0), axis=0, keepdims=True)
        column = jnp.sum(jnp.where(own_place, used, 0.0), axis=1, keepdims=True)
        mix_ref[t] = jnp.broadcast_to(column, (patches, fields))


def shares(points, pert_ref, centre, dense_ref, value_ref, left_high, left_low):
    members = pert_ref.shape[0]
    patches, fields = centre.shape
    pulls = [value_ref[n] - dense_ref[n] * centre for n in points]
    for slot, n in enumerate(points):
        for p in range(patches):
            lanes = slice(p * fields, (p + 1) * fields)
            left_high[slot, :members, lanes], left_low[slot, :members, lanes] = split(pert_ref[:, lanes] * dense_ref[n, p : p + 1, :])
            tail = jnp.broadcast_to(pulls[slot][p : p + 1, :], (left_high.shape[1] - members, fields))
            left_high[slot, members:, lanes], left_low[slot, members:, lanes] = split(tail)


def add_diagonal(x, value, diagonal):
    half = diagonal.shape[0]
    step = jnp.where(diagonal, value, 0.0)
    top = jnp.concatenate([x[:half, :half] + step, x[:half, half:]], axis=1)
    bottom = jnp.concatenate([x[half:, :half], x[half:, half:] + step], axis=1)
    return jnp.concatenate([top, bottom], axis=0)


def two_factors(x, parts, diagonal):
    square = product(parts, parts)
    inner = add_diagonal(square - 4.5 * x, 6.75, diagonal)
    return add_diagonal(product(split(square), split(inner)) - 4.875 * x, 2.25, diagonal)


def later_factors(x):
    rounded = x.astype(BF16)
    square = dot(rounded, rounded)
    return 1.5 * square - x + dot(square.astype(BF16), (square - 2.5 * x).astype(BF16))


def weights_of(count, x_ref, left_high, left_low, out_ref, fill=lambda: None):
    members = x_ref.shape[0]
    half = members // 2
    row = lax.broadcasted_iota(jnp.int32, (half, half), 0)
    col = lax.broadcasted_iota(jnp.int32, (half, half), 1)
    diagonal = row == col
    slots = range(count)
    state = []
    for slot in slots:
        columns = x_ref[...]
        both = dot(left_high[slot], columns, NT) + dot(left_low[slot], columns, NT)
        both = both - jnp.sum(both, axis=1, keepdims=True) * (1.0 / members)
        gram, projected = both[:members], both[members : members + 1]
        on_diagonal = jnp.where(diagonal, gram[:half, :half] + gram[half:, half:], 0.0)
        trace = jnp.sum(jnp.sum(on_diagonal, axis=0, keepdims=True), axis=1, keepdims=True)
        scaling = (members - 1.0) + trace / members
        half_inverse = 0.5 / scaling
        state.append((projected, scaling, add_diagonal(gram * half_inverse, (members - 1.0) * half_inverse, diagonal)))
    parts = [split(x) for _, _, x in state]
    roots = [two_factors(state[s][2], parts[s], diagonal) for s in slots]
    fill()
    z = [split(x) for x in roots]
    y = [split(product(parts[s], z[s])) for s in slots]
    fill()
    excess = [add_diagonal(product(y[s], z[s]), -0.5, diagonal) for s in slots]
    fill()
    rest = [later_factors(x) for x in excess]
    fill()
    inverses = [roots[s] + rest[s] + dot(rest[s].astype(BF16), add_diagonal(roots[s], -1.0, diagonal).astype(BF16)) for s in slots]
    for slot in slots:
        projected, scaling, _ = state[slot]
        inverse = inverses[slot]
        once = jnp.sum(inverse * projected, axis=1, keepdims=True)
        twice = jnp.sum(inverse * once, axis=0, keepdims=True) / scaling
        spread = jnp.sqrt((members - 1.0) / scaling) * inverse
        out_ref[slot] = (spread + twice).astype(BF16)
        yield slot, spread, twice


def pack(target, slot, spread, twice):
    members = spread.shape[0]
    half = members // 2
    small_row = lax.broadcasted_iota(jnp.int32, (half, half), 0)
    small_col = lax.broadcasted_iota(jnp.int32, (half, half), 1)
    tail_row = lax.broadcasted_iota(jnp.int32, (16, members), 0)
    corner = spread[half:, half:]
    target[slot, :half, :half] = jnp.where(small_row >= small_col, spread[:half, :half], corner).astype(BF16)
    target[slot, :half, half:] = spread[:half, half:].astype(BF16)
    on_diagonal = jnp.sum(jnp.where(small_row == small_col, corner, 0.0), axis=0, keepdims=True)
    high, low = split(twice)
    rows = jnp.where(tail_row == 1, high.astype(F32), jnp.where(tail_row == 2, low.astype(F32), 0.0))
    first = jnp.concatenate([on_diagonal, jnp.zeros_like(on_diagonal)], axis=1)
    target[slot, half:, :] = jnp.where(tail_row == 0, first, rows).astype(BF16)


def unpack(source, slot, target, place):
    half = source.shape[1] - 16
    row = lax.broadcasted_iota(jnp.int32, (half, half), 0)
    col = lax.broadcasted_iota(jnp.int32, (half, half), 1)
    mixed = source[slot, :half, :half].astype(F32)
    across = source[slot, :half, half:].astype(F32)
    tail = source[slot, half:, :].astype(F32)
    mean = tail[1:2] + tail[2:3]
    left, right = mean[:, :half], mean[:, half:]
    turned = mixed.T
    target[place, :half, :half] = (jnp.where(row >= col, mixed, turned) + left).astype(BF16)
    target[place, :half, half:] = (across + right).astype(BF16)
    target[place, half:, :half] = (across.T + left).astype(BF16)
    corner = jnp.where(row < col, mixed, jnp.where(row == col, tail[0:1, :half], turned))
    target[place, half:, half:] = (corner + right).astype(BF16)


def first_kernel(
    ensemble_ref, dense_ref, value_ref, out_ref, beside_ref, corner_ref, below_ref, x_ref, pert_ref, high_ref, centre_ref, wide_ref, left_high, left_low
):
    members, patches, fields = ensemble_ref.shape
    total = jnp.zeros((patches, fields), F32)
    chunk = 32
    for k in range(0, members, chunk):
        part = ensemble_ref[k : k + chunk].astype(F32)
        total = total + jnp.sum(part, axis=0)
        wide_ref[k * patches : (k + chunk) * patches] = part.reshape(chunk * patches, fields)
    centre = total * (1.0 / members)
    centre_ref[...] = centre
    for p in range(patches):
        lanes = slice(p * fields, (p + 1) * fields)
        part = wide_ref[pl.ds(p, members, stride=patches), :]
        x_ref[:, lanes] = part.astype(BF16)
        pert = part - centre[p : p + 1, :]
        pert_ref[:, lanes] = pert
        high_ref[:, lanes] = pert.astype(BF16)
    shares((0, 1, 2), pert_ref, centre, dense_ref, value_ref, left_high, left_low)
    for slot, spread, twice in weights_of(3, x_ref, left_high, left_low, out_ref):
        if slot == 0:
            pack(corner_ref, 0, spread, twice)
            beside_ref[0] = corner_ref[0]
            below_ref[0] = corner_ref[0]
        else:
            pack(below_ref if slot == 1 else beside_ref, 1, spread, twice)


def second_kernel(x_ref, pert_ref, centre_ref, dense_ref, value_ref, one_ref, high_ref, mix_ref, out_ref, two_ref, left_high, left_low):
    patches, fields = centre_ref.shape
    tiles = iter(range(0, patches, 2))

    def fill():
        p = next(tiles)
        parts = ((0, one_ref, 0), (1, one_ref, 1), (3, one_ref, 2))
        out_ref[:, p * fields : (p + 2) * fields] = blend(parts, high_ref, mix_ref, p)

    shares((3,), pert_ref, centre_ref[...], dense_ref, value_ref, left_high, left_low)
    for _ in weights_of(1, x_ref, left_high, left_low, two_ref, fill):
        pass


def blend(parts, high_ref, mix_ref, p):
    fields = mix_ref.shape[2]
    lanes = slice(p * fields, (p + 2) * fields)
    total = None
    for t, ref, slot in parts:
        share = jnp.concatenate([mix_ref[t, p : p + 1, :], mix_ref[t, p + 1 : p + 2, :]], axis=1)
        moved = dot(ref[slot], high_ref[:, lanes])
        moved = jnp.where(share != 0.0, share * moved, 0.0)
        total = moved if total is None else total + moved
    return total


def arrivals(arrived, whole_ref):
    for place, (_, ref, slot) in enumerate(arrived):
        unpack(ref, slot, whole_ref, place)
    return [(t, whole_ref, place) for place, (t, _, _) in enumerate(arrived)]


def middle_kernel(beside_ref, below_ref, two_ref, high_ref, mix_ref, partial_ref, out_ref, whole_ref):
    parts = arrivals(((2, beside_ref, 0), (5, beside_ref, 1), (6, below_ref, 0), (7, below_ref, 1)), whole_ref) + [(4, two_ref, 0)]
    fields = mix_ref.shape[2]
    for p in range(0, mix_ref.shape[1], 2):
        lanes = slice(p * fields, (p + 2) * fields)
        out_ref[:, lanes] = partial_ref[:, lanes] + blend(parts, high_ref, mix_ref, p)


def last_kernel(diagonal_ref, high_ref, mix_ref, partial_ref, centre_ref, out_ref, all_ref, whole_ref):
    parts = arrivals(((8, diagonal_ref, 0),), whole_ref)
    members, patches, fields = out_ref.shape
    for p in range(0, patches, 2):
        lanes = slice(p * fields, (p + 2) * fields)
        total = partial_ref[:, lanes] + blend(parts, high_ref, mix_ref, p)
        for q in range(2):
            part = total[:, q * fields : (q + 1) * fields] + centre_ref[p + q : p + q + 1, :]
            all_ref[pl.ds(p + q, members, stride=patches), :] = part
    chunk = 32
    for k in range(0, members, chunk):
        part = all_ref[k * patches : (k + chunk) * patches, :]
        out_ref[k : k + chunk] = part.reshape(chunk, patches, fields).astype(BF16)


def entry_kernel(*refs):
    small, source_ref, target_ref, results = refs[:7], refs[7], refs[8], refs[9:12]
    copied, held_ref, turned_ref, loaded, read, written = refs[12:19], refs[19], refs[20], refs[21], refs[22], refs[23]
    own, devices = source_ref.shape[:2]
    half = devices // 2
    spans = [slice(h * half, (h + 1) * half) for h in range(2)]
    fetch = [pltpu.make_async_copy(a, b, loaded.at[i]) for i, (a, b) in enumerate(zip(small, copied))]
    inward = [pltpu.make_async_copy(source_ref.at[:, s], held_ref.at[:, s], read.at[h]) for h, s in enumerate(spans)]
    outward = [pltpu.make_async_copy(turned_ref.at[s], target_ref.at[s], written.at[h]) for h, s in enumerate(spans)]
    for copy in fetch + inward:
        copy.start()
    for copy in fetch:
        copy.wait()
    prepare(*copied, *results)
    for copy, out, s in zip(inward, outward, spans):
        copy.wait()
        for m in range(own):
            turned_ref[s, m] = held_ref[m, s]
        out.start()
    for out in outward:
        out.wait()


def returned_kernel(source_ref, target_ref, done):
    copies = [pltpu.make_async_copy(source_ref.at[:, m], target_ref.at[m], done.at[m]) for m in range(target_ref.shape[0])]
    for copy in copies:
        copy.start()
    for copy in copies:
        copy.wait()


def call(kernel, outs, specs, scratch=(), to=VMEM):
    return pl.pallas_call(
        kernel,
        out_shape=outs,
        in_specs=specs,
        out_specs=jax.tree.map(lambda _: to, outs),
        scratch_shapes=list(scratch),
        compiler_params=pltpu.CompilerParams(vmem_limit_bytes=32 << 20),
    )


def per_device(background, obs_value, obs_error, obs_patch, obs_variable, obs_count, patch_corners, interp_weights):
    shape = jax.ShapeDtypeStruct
    devices = lax.axis_size("mem")
    regions = lax.axis_size("reg")
    own, _, all_patches, fields = background.shape
    patches = all_patches // devices
    members = own * devices
    points = obs_value.shape[0] * obs_value.shape[1]
    columns = patches * fields
    copies = [pltpu.SemaphoreType.DMA((own,))]

    blocks = (devices, own, patches, fields)
    small = (obs_count, obs_value, obs_error, obs_patch, obs_variable, patch_corners[0].T, interp_weights[0].T)
    given = [pltpu.with_memory_space_constraint(x, pltpu.HBM) for x in small + (background.reshape(own, devices, patches, fields),)]
    sums = (points, patches, fields)
    outgoing, dense, values, mix = pl.pallas_call(
        entry_kernel,
        out_shape=(shape(blocks, BF16), shape(sums, F32), shape(sums, F32), shape((9, patches, fields), F32)),
        in_specs=[HBM] * 8,
        out_specs=(HBM, VMEM, VMEM, VMEM),
        scratch_shapes=[pltpu.VMEM(x.shape, x.dtype) for x in small]
        + [pltpu.VMEM((own, devices) + blocks[2:], BF16), pltpu.VMEM(blocks, BF16)]
        + [pltpu.SemaphoreType.DMA((len(small),))]
        + [pltpu.SemaphoreType.DMA((2,))] * 2,
        compiler_params=pltpu.CompilerParams(vmem_limit_bytes=32 << 20),
    )(*given)
    ensemble = lax.all_to_all(outgoing, "mem", split_axis=0, concat_axis=0, tiled=True).reshape(members, patches, fields)

    packed = (members // 2 + 16, members)
    left = (members + 16, columns)
    flat = (members, columns)
    wide = pltpu.VMEM((members * patches, fields), F32)
    down = [((d + 1) % devices, d) for d in range(devices)]
    across = [(r + 1, r) for r in range(regions - 1)]
    both = [(d * regions + r, e * regions + t) for d, e in down for r, t in across]
    one, to_beside, to_corner, to_below, x, pert, high, centre = call(
        first_kernel,
        (
            shape((3, members, members), BF16),
            shape((2,) + packed, BF16),
            shape((1,) + packed, BF16),
            shape((2,) + packed, BF16),
            shape(flat, BF16),
            shape(flat, F32),
            shape(flat, BF16),
            shape((patches, fields), F32),
        ),
        [VMEM] * 3,
        [wide] + [pltpu.VMEM((3,) + left, BF16)] * 2,
    )(ensemble, dense, values)
    beside = lax.ppermute(to_beside, "reg", across)
    diagonal = lax.ppermute(to_corner, ("mem", "reg"), both)
    below = lax.ppermute(to_below, "mem", down)
    partial, two = call(
        second_kernel,
        (shape(flat, F32), shape((1, members, members), BF16)),
        [VMEM] * 8,
        [pltpu.VMEM((1,) + left, BF16)] * 2,
    )(x, pert, centre, dense, values, one, high, mix)
    partial = call(middle_kernel, shape(flat, F32), [VMEM] * 6, [pltpu.VMEM((4, members, members), BF16)])(
        beside, below, two, high, mix, partial
    )
    analysis = call(
        last_kernel,
        shape((members, patches, fields), BF16),
        [VMEM] * 5,
        [wide, pltpu.VMEM((1, members, members), BF16)],
    )(diagonal, high, mix, partial, centre)
    returned = lax.all_to_all(analysis.reshape(devices, own, patches, fields), "mem", split_axis=0, concat_axis=0, tiled=True)
    result = call(returned_kernel, shape((own, devices, patches, fields), BF16), [VMEM], copies, HBM)(returned)
    return result.reshape(own, 1, all_patches, fields)


def solution(mesh):
    placed = (
        P("mem", "reg", None, None),
        P("mem", "reg", None),
        P("mem", "reg", None),
        P("mem", "reg", None),
        P("mem", "reg", None),
        P("mem", "reg"),
        P("reg", "mem", None),
        P("reg", "mem", None),
    )
    return jax.shard_map(
        per_device,
        mesh=mesh,
        in_specs=placed,
        out_specs=P("mem", "reg", None, None),
        check_vma=False,
    )
```

```python
import jax
import jax.numpy as jnp
from jax import lax
from jax.experimental import pallas as pl
from jax.experimental.pallas import tpu as pltpu
from jax.sharding import PartitionSpec as P


F32 = jnp.float32
BF16 = jnp.bfloat16
VMEM = pl.BlockSpec(memory_space=pltpu.VMEM)
HBM = pl.BlockSpec(memory_space=pltpu.HBM)
NN = (((1,), (0,)), ((), ()))
NT = (((1,), (1,)), ((), ()))


def dot(a, b, dims=NN):
    return lax.dot_general(a, b, dims, preferred_element_type=F32)


def split(x):
    high = x.astype(BF16)
    return high, (x - high.astype(F32)).astype(BF16)


def thirds(x):
    high = x.astype(BF16)
    rest = x - high.astype(F32)
    middle = rest.astype(BF16)
    return high, middle, (rest - middle.astype(F32)).astype(BF16)


def product(a, b):
    return dot(a[0], b[0]) + (dot(a[0], b[1]) + dot(a[1], b[0]))


def prepare(count_ref, value_ref, error_ref, patch_ref, var_ref, corner_ref, coeff_ref, dense_ref, value_out_ref, mix_ref):
    rows, cols, slots = value_ref.shape
    patches, fields = dense_ref.shape[1:]
    slot_index = lax.broadcasted_iota(jnp.int32, (1, slots), 1)
    field_index = lax.broadcasted_iota(jnp.int32, (fields, slots), 0)
    patch_index = lax.broadcasted_iota(jnp.int32, (patches, slots), 0)
    for a in range(rows):
        for b in range(cols):
            weight = jnp.where(slot_index < count_ref[a : a + 1, b : b + 1], 1.0 / error_ref[a, b : b + 1, :], 0.0)
            weighted = weight * value_ref[a, b : b + 1, :]
            chosen = (field_index == var_ref[a, b : b + 1, :]).astype(F32).astype(BF16)
            at_patch = patch_index == patch_ref[a, b : b + 1, :]
            left = jnp.concatenate([jnp.where(at_patch, x, 0.0) for x in (weight, weighted)], axis=0)
            high, middle, low = (dot(x, chosen, NT) for x in thirds(left))
            sums = high + (middle + low)
            dense_ref[a * cols + b] = sums[:patches]
            value_out_ref[a * cols + b] = sums[patches:]
    corners, coeffs = corner_ref[...], coeff_ref[...]
    square = (patches, patches)
    own_place = lax.broadcasted_iota(jnp.int32, square, 0) == lax.broadcasted_iota(jnp.int32, square, 1)
    for t in range(mix_ref.shape[0]):
        used = jnp.sum(jnp.where(corners == t, coeffs, 0.0), axis=0, keepdims=True)
        column = jnp.sum(jnp.where(own_place, used, 0.0), axis=1, keepdims=True)
        mix_ref[t] = jnp.broadcast_to(column, (patches, fields))


def shares(points, pert_ref, centre, dense_ref, value_ref, left_high, left_low):
    members = pert_ref.shape[0]
    patches, fields = centre.shape
    pulls = [value_ref[n] - dense_ref[n] * centre for n in points]
    for slot, n in enumerate(points):
        for p in range(patches):
            lanes = slice(p * fields, (p + 1) * fields)
            left_high[slot, :members, lanes], left_low[slot, :members, lanes] = split(pert_ref[:, lanes] * dense_ref[n, p : p + 1, :])
            tail = jnp.broadcast_to(pulls[slot][p : p + 1, :], (left_high.shape[1] - members, fields))
            left_high[slot, members:, lanes], left_low[slot, members:, lanes] = split(tail)


def add_diagonal(x, value, diagonal):
    half = diagonal.shape[0]
    step = jnp.where(diagonal, value, 0.0)
    top = jnp.concatenate([x[:half, :half] + step, x[:half, half:]], axis=1)
    bottom = jnp.concatenate([x[half:, :half], x[half:, half:] + step], axis=1)
    return jnp.concatenate([top, bottom], axis=0)


def two_factors(x, parts, diagonal):
    square = product(parts, parts)
    inner = add_diagonal(square - 4.5 * x, 6.75, diagonal)
    return add_diagonal(product(split(square), split(inner)) - 4.875 * x, 2.25, diagonal)


def later_factors(x):
    rounded = x.astype(BF16)
    square = dot(rounded, rounded)
    return 1.5 * square - x + dot(square.astype(BF16), (square - 2.5 * x).astype(BF16))


def weights_of(count, x_ref, left_high, left_low, out_ref, fill=lambda: None):
    members = x_ref.shape[0]
    half = members // 2
    row = lax.broadcasted_iota(jnp.int32, (half, half), 0)
    col = lax.broadcasted_iota(jnp.int32, (half, half), 1)
    diagonal = row == col
    slots = range(count)
    state = []
    for slot in slots:
        columns = x_ref[...]
        both = dot(left_high[slot], columns, NT) + dot(left_low[slot], columns, NT)
        both = both - jnp.sum(both, axis=1, keepdims=True) * (1.0 / members)
        gram, projected = both[:members], both[members : members + 1]
        on_diagonal = jnp.where(diagonal, gram[:half, :half] + gram[half:, half:], 0.0)
        trace = jnp.sum(jnp.sum(on_diagonal, axis=0, keepdims=True), axis=1, keepdims=True)
        scaling = (members - 1.0) + trace / members
        half_inverse = 0.5 / scaling
        state.append((projected, scaling, add_diagonal(gram * half_inverse, (members - 1.0) * half_inverse, diagonal)))
    parts = [split(x) for _, _, x in state]
    roots = [two_factors(state[s][2], parts[s], diagonal) for s in slots]
    fill()
    z = [split(x) for x in roots]
    y = [split(product(parts[s], z[s])) for s in slots]
    fill()
    excess = [add_diagonal(product(y[s], z[s]), -0.5, diagonal) for s in slots]
    fill()
    rest = [later_factors(x) for x in excess]
    fill()
    inverses = [roots[s] + rest[s] + dot(rest[s].astype(BF16), add_diagonal(roots[s], -1.0, diagonal).astype(BF16)) for s in slots]
    for slot in slots:
        projected, scaling, _ = state[slot]
        inverse = inverses[slot]
        once = jnp.sum(inverse * projected, axis=1, keepdims=True)
        twice = jnp.sum(inverse * once, axis=0, keepdims=True) / scaling
        spread = jnp.sqrt((members - 1.0) / scaling) * inverse
        out_ref[slot] = (spread + twice).astype(BF16)
        yield slot, spread, twice


def pack(target, slot, spread, twice):
    members = spread.shape[0]
    half = members // 2
    small_row = lax.broadcasted_iota(jnp.int32, (half, half), 0)
    small_col = lax.broadcasted_iota(jnp.int32, (half, half), 1)
    tail_row = lax.broadcasted_iota(jnp.int32, (16, members), 0)
    corner = spread[half:, half:]
    target[slot, :half, :half] = jnp.where(small_row >= small_col, spread[:half, :half], corner).astype(BF16)
    target[slot, :half, half:] = spread[:half, half:].astype(BF16)
    on_diagonal = jnp.sum(jnp.where(small_row == small_col, corner, 0.0), axis=0, keepdims=True)
    high, low = split(twice)
    rows = jnp.where(tail_row == 1, high.astype(F32), jnp.where(tail_row == 2, low.astype(F32), 0.0))
    first = jnp.concatenate([on_diagonal, jnp.zeros_like(on_diagonal)], axis=1)
    target[slot, half:, :] = jnp.where(tail_row == 0, first, rows).astype(BF16)


def unpack(source, slot, target, place):
    half = source.shape[1] - 16
    row = lax.broadcasted_iota(jnp.int32, (half, half), 0)
    col = lax.broadcasted_iota(jnp.int32, (half, half), 1)
    mixed = source[slot, :half, :half].astype(F32)
    across = source[slot, :half, half:].astype(F32)
    tail = source[slot, half:, :].astype(F32)
    mean = tail[1:2] + tail[2:3]
    left, right = mean[:, :half], mean[:, half:]
    turned = mixed.T
    target[place, :half, :half] = (jnp.where(row >= col, mixed, turned) + left).astype(BF16)
    target[place, :half, half:] = (across + right).astype(BF16)
    target[place, half:, :half] = (across.T + left).astype(BF16)
    corner = jnp.where(row < col, mixed, jnp.where(row == col, tail[0:1, :half], turned))
    target[place, half:, half:] = (corner + right).astype(BF16)


def first_kernel(
    ensemble_ref, dense_ref, value_ref, out_ref, beside_ref, corner_ref, below_ref, x_ref, pert_ref, high_ref, centre_ref, wide_ref, left_high, left_low
):
    members, patches, fields = ensemble_ref.shape
    total = jnp.zeros((patches, fields), F32)
    chunk = 32
    for k in range(0, members, chunk):
        part = ensemble_ref[k : k + chunk].astype(F32)
        total = total + jnp.sum(part, axis=0)
        wide_ref[k * patches : (k + chunk) * patches] = part.reshape(chunk * patches, fields)
    centre = total * (1.0 / members)
    centre_ref[...] = centre
    for p in range(patches):
        lanes = slice(p * fields, (p + 1) * fields)
        part = wide_ref[pl.ds(p, members, stride=patches), :]
        x_ref[:, lanes] = part.astype(BF16)
        pert = part - centre[p : p + 1, :]
        pert_ref[:, lanes] = pert
        high_ref[:, lanes] = pert.astype(BF16)
    shares((0, 1, 2), pert_ref, centre, dense_ref, value_ref, left_high, left_low)
    for slot, spread, twice in weights_of(3, x_ref, left_high, left_low, out_ref):
        if slot == 0:
            pack(corner_ref, 0, spread, twice)
            beside_ref[0] = corner_ref[0]
            below_ref[0] = corner_ref[0]
        else:
            pack(below_ref if slot == 1 else beside_ref, 1, spread, twice)


def second_kernel(x_ref, pert_ref, centre_ref, dense_ref, value_ref, one_ref, high_ref, mix_ref, out_ref, two_ref, left_high, left_low):
    patches, fields = centre_ref.shape
    tiles = iter(range(0, patches, 2))

    def fill():
        p = next(tiles)
        parts = ((0, one_ref, 0), (1, one_ref, 1), (3, one_ref, 2))
        out_ref[:, p * fields : (p + 2) * fields] = blend(parts, high_ref, mix_ref, p)

    shares((3,), pert_ref, centre_ref[...], dense_ref, value_ref, left_high, left_low)
    for _ in weights_of(1, x_ref, left_high, left_low, two_ref, fill):
        pass


def blend(parts, high_ref, mix_ref, p):
    fields = mix_ref.shape[2]
    lanes = slice(p * fields, (p + 2) * fields)
    total = None
    for t, ref, slot in parts:
        share = jnp.concatenate([mix_ref[t, p : p + 1, :], mix_ref[t, p + 1 : p + 2, :]], axis=1)
        moved = dot(ref[slot], high_ref[:, lanes])
        moved = jnp.where(share != 0.0, share * moved, 0.0)
        total = moved if total is None else total + moved
    return total


def arrivals(arrived, whole_ref):
    for place, (_, ref, slot) in enumerate(arrived):
        unpack(ref, slot, whole_ref, place)
    return [(t, whole_ref, place) for place, (t, _, _) in enumerate(arrived)]


def middle_kernel(beside_ref, below_ref, two_ref, high_ref, mix_ref, partial_ref, out_ref, whole_ref):
    parts = arrivals(((2, beside_ref, 0), (5, beside_ref, 1), (6, below_ref, 0), (7, below_ref, 1)), whole_ref) + [(4, two_ref, 0)]
    fields = mix_ref.shape[2]
    for p in range(0, mix_ref.shape[1], 2):
        lanes = slice(p * fields, (p + 2) * fields)
        out_ref[:, lanes] = partial_ref[:, lanes] + blend(parts, high_ref, mix_ref, p)


def last_kernel(diagonal_ref, high_ref, mix_ref, partial_ref, centre_ref, out_ref, all_ref, whole_ref):
    parts = arrivals(((8, diagonal_ref, 0),), whole_ref)
    members, patches, fields = out_ref.shape
    for p in range(0, patches, 2):
        lanes = slice(p * fields, (p + 2) * fields)
        total = partial_ref[:, lanes] + blend(parts, high_ref, mix_ref, p)
        for q in range(2):
            part = total[:, q * fields : (q + 1) * fields] + centre_ref[p + q : p + q + 1, :]
            all_ref[pl.ds(p + q, members, stride=patches), :] = part
    chunk = 32
    for k in range(0, members, chunk):
        part = all_ref[k * patches : (k + chunk) * patches, :]
        out_ref[k : k + chunk] = part.reshape(chunk, patches, fields).astype(BF16)


def entry_kernel(*refs):
    small, source_ref, target_ref, results = refs[:7], refs[7], refs[8], refs[9:12]
    copied, loaded, read = refs[12:19], refs[19], refs[20]
    fetch = [pltpu.make_async_copy(a, b, loaded.at[i]) for i, (a, b) in enumerate(zip(small, copied))]
    inward = [pltpu.make_async_copy(source_ref.at[m], target_ref.at[:, m], read.at[m]) for m in range(source_ref.shape[0])]
    for copy in fetch + inward:
        copy.start()
    for copy in fetch:
        copy.wait()
    prepare(*copied, *results)
    for copy in inward:
        copy.wait()


def returned_kernel(source_ref, target_ref, done):
    copies = [pltpu.make_async_copy(source_ref.at[:, m], target_ref.at[m], done.at[m]) for m in range(target_ref.shape[0])]
    for copy in copies:
        copy.start()
    for copy in copies:
        copy.wait()


def call(kernel, outs, specs, scratch=(), to=VMEM):
    return pl.pallas_call(
        kernel,
        out_shape=outs,
        in_specs=specs,
        out_specs=jax.tree.map(lambda _: to, outs),
        scratch_shapes=list(scratch),
        compiler_params=pltpu.CompilerParams(vmem_limit_bytes=32 << 20),
    )


def per_device(background, obs_value, obs_error, obs_patch, obs_variable, obs_count, patch_corners, interp_weights):
    shape = jax.ShapeDtypeStruct
    devices = lax.axis_size("mem")
    regions = lax.axis_size("reg")
    own, _, all_patches, fields = background.shape
    patches = all_patches // devices
    members = own * devices
    points = obs_value.shape[0] * obs_value.shape[1]
    columns = patches * fields
    copies = [pltpu.SemaphoreType.DMA((own,))]

    blocks = (devices, own, patches, fields)
    small = (obs_count, obs_value, obs_error, obs_patch, obs_variable, patch_corners[0].T, interp_weights[0].T)
    given = [pltpu.with_memory_space_constraint(x, pltpu.HBM) for x in small + (background.reshape(own, devices, patches, fields),)]
    sums = (points, patches, fields)
    outgoing, dense, values, mix = pl.pallas_call(
        entry_kernel,
        out_shape=(shape(blocks, BF16), shape(sums, F32), shape(sums, F32), shape((9, patches, fields), F32)),
        in_specs=[HBM] * 8,
        out_specs=(VMEM, VMEM, VMEM, VMEM),
        scratch_shapes=[pltpu.VMEM(x.shape, x.dtype) for x in small]
        + [pltpu.SemaphoreType.DMA((len(small),)), pltpu.SemaphoreType.DMA((own,))],
        compiler_params=pltpu.CompilerParams(vmem_limit_bytes=32 << 20),
    )(*given)
    ensemble = lax.all_to_all(outgoing, "mem", split_axis=0, concat_axis=0, tiled=True).reshape(members, patches, fields)

    packed = (members // 2 + 16, members)
    left = (members + 16, columns)
    flat = (members, columns)
    wide = pltpu.VMEM((members * patches, fields), F32)
    down = [((d + 1) % devices, d) for d in range(devices)]
    across = [(r + 1, r) for r in range(regions - 1)]
    both = [(d * regions + r, e * regions + t) for d, e in down for r, t in across]
    one, to_beside, to_corner, to_below, x, pert, high, centre = call(
        first_kernel,
        (
            shape((3, members, members), BF16),
            shape((2,) + packed, BF16),
            shape((1,) + packed, BF16),
            shape((2,) + packed, BF16),
            shape(flat, BF16),
            shape(flat, F32),
            shape(flat, BF16),
            shape((patches, fields), F32),
        ),
        [VMEM] * 3,
        [wide] + [pltpu.VMEM((3,) + left, BF16)] * 2,
    )(ensemble, dense, values)
    beside = lax.ppermute(to_beside, "reg", across)
    diagonal = lax.ppermute(to_corner, ("mem", "reg"), both)
    below = lax.ppermute(to_below, "mem", down)
    partial, two = call(
        second_kernel,
        (shape(flat, F32), shape((1, members, members), BF16)),
        [VMEM] * 8,
        [pltpu.VMEM((1,) + left, BF16)] * 2,
    )(x, pert, centre, dense, values, one, high, mix)
    partial = call(middle_kernel, shape(flat, F32), [VMEM] * 6, [pltpu.VMEM((4, members, members), BF16)])(
        beside, below, two, high, mix, partial
    )
    analysis = call(
        last_kernel,
        shape((members, patches, fields), BF16),
        [VMEM] * 5,
        [wide, pltpu.VMEM((1, members, members), BF16)],
    )(diagonal, high, mix, partial, centre)
    returned = lax.all_to_all(analysis.reshape(devices, own, patches, fields), "mem", split_axis=0, concat_axis=0, tiled=True)
    result = call(returned_kernel, shape((own, devices, patches, fields), BF16), [VMEM], copies, HBM)(returned)
    return result.reshape(own, 1, all_patches, fields)


def solution(mesh):
    placed = (
        P("mem", "reg", None, None),
        P("mem", "reg", None),
        P("mem", "reg", None),
        P("mem", "reg", None),
        P("mem", "reg", None),
        P("mem", "reg"),
        P("reg", "mem", None),
        P("reg", "mem", None),
    )
    return jax.shard_map(
        per_device,
        mesh=mesh,
        in_specs=placed,
        out_specs=P("mem", "reg", None, None),
        check_vma=False,
    )
```

```python
import jax
import jax.numpy as jnp
from jax import lax
from jax.experimental import pallas as pl
from jax.experimental.pallas import tpu as pltpu
from jax.sharding import PartitionSpec as P


F32 = jnp.float32
BF16 = jnp.bfloat16
VMEM = pl.BlockSpec(memory_space=pltpu.VMEM)
HBM = pl.BlockSpec(memory_space=pltpu.HBM)
NN = (((1,), (0,)), ((), ()))
NT = (((1,), (1,)), ((), ()))


def dot(a, b, dims=NN):
    return lax.dot_general(a, b, dims, preferred_element_type=F32)


def split(x):
    high = x.astype(BF16)
    return high, (x - high.astype(F32)).astype(BF16)


def thirds(x):
    high = x.astype(BF16)
    rest = x - high.astype(F32)
    middle = rest.astype(BF16)
    return high, middle, (rest - middle.astype(F32)).astype(BF16)


def product(a, b):
    return dot(a[0], b[0]) + (dot(a[0], b[1]) + dot(a[1], b[0]))


def prepare(count_ref, value_ref, error_ref, patch_ref, var_ref, corner_ref, coeff_ref, dense_ref, value_out_ref, mix_ref):
    rows, cols, slots = value_ref.shape
    patches, fields = dense_ref.shape[1:]
    slot_index = lax.broadcasted_iota(jnp.int32, (1, slots), 1)
    field_index = lax.broadcasted_iota(jnp.int32, (fields, slots), 0)
    patch_index = lax.broadcasted_iota(jnp.int32, (patches, slots), 0)
    for a in range(rows):
        for b in range(cols):
            weight = jnp.where(slot_index < count_ref[a : a + 1, b : b + 1], 1.0 / error_ref[a, b : b + 1, :], 0.0)
            weighted = weight * value_ref[a, b : b + 1, :]
            chosen = (field_index == var_ref[a, b : b + 1, :]).astype(F32).astype(BF16)
            at_patch = patch_index == patch_ref[a, b : b + 1, :]
            left = jnp.concatenate([jnp.where(at_patch, x, 0.0) for x in (weight, weighted)], axis=0)
            high, middle, low = (dot(x, chosen, NT) for x in thirds(left))
            sums = high + (middle + low)
            dense_ref[a * cols + b] = sums[:patches]
            value_out_ref[a * cols + b] = sums[patches:]
    corners, coeffs = corner_ref[...], coeff_ref[...]
    square = (patches, patches)
    own_place = lax.broadcasted_iota(jnp.int32, square, 0) == lax.broadcasted_iota(jnp.int32, square, 1)
    for t in range(mix_ref.shape[0]):
        used = jnp.sum(jnp.where(corners == t, coeffs, 0.0), axis=0, keepdims=True)
        column = jnp.sum(jnp.where(own_place, used, 0.0), axis=1, keepdims=True)
        mix_ref[t] = jnp.broadcast_to(column, (patches, fields))


def shares(points, pert_ref, centre, dense_ref, value_ref, left_high, left_low):
    members = pert_ref.shape[0]
    patches, fields = centre.shape
    pulls = [value_ref[n] - dense_ref[n] * centre for n in points]
    for slot, n in enumerate(points):
        for p in range(patches):
            lanes = slice(p * fields, (p + 1) * fields)
            left_high[slot, :members, lanes], left_low[slot, :members, lanes] = split(pert_ref[:, lanes] * dense_ref[n, p : p + 1, :])
            tail = jnp.broadcast_to(pulls[slot][p : p + 1, :], (left_high.shape[1] - members, fields))
            left_high[slot, members:, lanes], left_low[slot, members:, lanes] = split(tail)


def add_diagonal(x, value, diagonal):
    half = diagonal.shape[0]
    step = jnp.where(diagonal, value, 0.0)
    top = jnp.concatenate([x[:half, :half] + step, x[:half, half:]], axis=1)
    bottom = jnp.concatenate([x[half:, :half], x[half:, half:] + step], axis=1)
    return jnp.concatenate([top, bottom], axis=0)


def two_factors(x, parts, diagonal):
    square = product(parts, parts)
    inner = add_diagonal(square - 4.5 * x, 6.75, diagonal)
    return add_diagonal(product(split(square), split(inner)) - 4.875 * x, 2.25, diagonal)


def later_factors(x):
    rounded = x.astype(BF16)
    square = dot(rounded, rounded)
    return 1.5 * square - x + dot(square.astype(BF16), (square - 2.5 * x).astype(BF16))


def weights_of(count, x_ref, left_high, left_low, out_ref, fill=lambda: None):
    members = x_ref.shape[0]
    half = members // 2
    row = lax.broadcasted_iota(jnp.int32, (half, half), 0)
    col = lax.broadcasted_iota(jnp.int32, (half, half), 1)
    diagonal = row == col
    slots = range(count)
    state = []
    for slot in slots:
        columns = x_ref[...]
        both = dot(left_high[slot], columns, NT) + dot(left_low[slot], columns, NT)
        both = both - jnp.sum(both, axis=1, keepdims=True) * (1.0 / members)
        gram, projected = both[:members], both[members : members + 1]
        on_diagonal = jnp.where(diagonal, gram[:half, :half] + gram[half:, half:], 0.0)
        trace = jnp.sum(jnp.sum(on_diagonal, axis=0, keepdims=True), axis=1, keepdims=True)
        scaling = (members - 1.0) + trace / members
        half_inverse = 0.5 / scaling
        state.append((projected, scaling, add_diagonal(gram * half_inverse, (members - 1.0) * half_inverse, diagonal)))
    parts = [split(x) for _, _, x in state]
    roots = [two_factors(state[s][2], parts[s], diagonal) for s in slots]
    fill()
    z = [split(x) for x in roots]
    y = [split(product(parts[s], z[s])) for s in slots]
    fill()
    excess = [add_diagonal(product(y[s], z[s]), -0.5, diagonal) for s in slots]
    fill()
    rest = [later_factors(x) for x in excess]
    fill()
    inverses = [roots[s] + rest[s] + dot(rest[s].astype(BF16), add_diagonal(roots[s], -1.0, diagonal).astype(BF16)) for s in slots]
    for slot in slots:
        projected, scaling, _ = state[slot]
        inverse = inverses[slot]
        once = jnp.sum(inverse * projected, axis=1, keepdims=True)
        twice = jnp.sum(inverse * once, axis=0, keepdims=True) / scaling
        spread = jnp.sqrt((members - 1.0) / scaling) * inverse
        out_ref[slot] = (spread + twice).astype(BF16)
        yield slot, spread, twice


def pack(target, slot, spread, twice):
    members = spread.shape[0]
    half = members // 2
    small_row = lax.broadcasted_iota(jnp.int32, (half, half), 0)
    small_col = lax.broadcasted_iota(jnp.int32, (half, half), 1)
    tail_row = lax.broadcasted_iota(jnp.int32, (16, members), 0)
    corner = spread[half:, half:]
    target[slot, :half, :half] = jnp.where(small_row >= small_col, spread[:half, :half], corner).astype(BF16)
    target[slot, :half, half:] = spread[:half, half:].astype(BF16)
    on_diagonal = jnp.sum(jnp.where(small_row == small_col, corner, 0.0), axis=0, keepdims=True)
    high, low = split(twice)
    rows = jnp.where(tail_row == 1, high.astype(F32), jnp.where(tail_row == 2, low.astype(F32), 0.0))
    first = jnp.concatenate([on_diagonal, jnp.zeros_like(on_diagonal)], axis=1)
    target[slot, half:, :] = jnp.where(tail_row == 0, first, rows).astype(BF16)


def unpack(source, slot, target, place):
    half = source.shape[1] - 16
    row = lax.broadcasted_iota(jnp.int32, (half, half), 0)
    col = lax.broadcasted_iota(jnp.int32, (half, half), 1)
    mixed = source[slot, :half, :half].astype(F32)
    across = source[slot, :half, half:].astype(F32)
    tail = source[slot, half:, :].astype(F32)
    mean = tail[1:2] + tail[2:3]
    left, right = mean[:, :half], mean[:, half:]
    turned = mixed.T
    target[place, :half, :half] = (jnp.where(row >= col, mixed, turned) + left).astype(BF16)
    target[place, :half, half:] = (across + right).astype(BF16)
    target[place, half:, :half] = (across.T + left).astype(BF16)
    corner = jnp.where(row < col, mixed, jnp.where(row == col, tail[0:1, :half], turned))
    target[place, half:, half:] = (corner + right).astype(BF16)


def first_kernel(
    ensemble_ref, dense_ref, value_ref, out_ref, beside_ref, corner_ref, below_ref, x_ref, pert_ref, high_ref, centre_ref, wide_ref, left_high, left_low
):
    members, patches, fields = ensemble_ref.shape
    total = jnp.zeros((patches, fields), F32)
    chunk = 32
    for k in range(0, members, chunk):
        part = ensemble_ref[k : k + chunk].astype(F32)
        total = total + jnp.sum(part, axis=0)
        wide_ref[k * patches : (k + chunk) * patches] = part.reshape(chunk * patches, fields)
    centre = total * (1.0 / members)
    centre_ref[...] = centre
    for p in range(patches):
        lanes = slice(p * fields, (p + 1) * fields)
        part = wide_ref[pl.ds(p, members, stride=patches), :]
        x_ref[:, lanes] = part.astype(BF16)
        pert = part - centre[p : p + 1, :]
        pert_ref[:, lanes] = pert
        high_ref[:, lanes] = pert.astype(BF16)
    shares((0, 1, 2), pert_ref, centre, dense_ref, value_ref, left_high, left_low)
    for slot, spread, twice in weights_of(3, x_ref, left_high, left_low, out_ref):
        if slot == 0:
            pack(corner_ref, 0, spread, twice)
            beside_ref[0] = corner_ref[0]
            below_ref[0] = corner_ref[0]
        else:
            pack(below_ref if slot == 1 else beside_ref, 1, spread, twice)


def second_kernel(x_ref, pert_ref, centre_ref, dense_ref, value_ref, one_ref, high_ref, mix_ref, out_ref, two_ref, left_high, left_low):
    patches, fields = centre_ref.shape
    tiles = iter(range(0, patches, 2))

    def fill():
        p = next(tiles)
        parts = ((0, one_ref, 0), (1, one_ref, 1), (3, one_ref, 2))
        out_ref[:, p * fields : (p + 2) * fields] = blend(parts, high_ref, mix_ref, p)

    shares((3,), pert_ref, centre_ref[...], dense_ref, value_ref, left_high, left_low)
    for _ in weights_of(1, x_ref, left_high, left_low, two_ref, fill):
        pass


def blend(parts, high_ref, mix_ref, p):
    fields = mix_ref.shape[2]
    lanes = slice(p * fields, (p + 2) * fields)
    total = None
    for t, ref, slot in parts:
        share = jnp.concatenate([mix_ref[t, p : p + 1, :], mix_ref[t, p + 1 : p + 2, :]], axis=1)
        moved = dot(ref[slot], high_ref[:, lanes])
        moved = jnp.where(share != 0.0, share * moved, 0.0)
        total = moved if total is None else total + moved
    return total


def arrivals(arrived, whole_ref):
    for place, (_, ref, slot) in enumerate(arrived):
        unpack(ref, slot, whole_ref, place)
    return [(t, whole_ref, place) for place, (t, _, _) in enumerate(arrived)]


def middle_kernel(beside_ref, two_ref, high_ref, mix_ref, partial_ref, out_ref, whole_ref):
    parts = arrivals(((2, beside_ref, 0), (5, beside_ref, 1)), whole_ref) + [(4, two_ref, 0)]
    fields = mix_ref.shape[2]
    for p in range(0, mix_ref.shape[1], 2):
        lanes = slice(p * fields, (p + 2) * fields)
        out_ref[:, lanes] = partial_ref[:, lanes] + blend(parts, high_ref, mix_ref, p)


def last_kernel(below_ref, diagonal_ref, high_ref, mix_ref, partial_ref, centre_ref, out_ref, all_ref, whole_ref):
    parts = arrivals(((6, below_ref, 0), (7, below_ref, 1), (8, diagonal_ref, 0)), whole_ref)
    members, patches, fields = out_ref.shape
    for p in range(0, patches, 2):
        lanes = slice(p * fields, (p + 2) * fields)
        total = partial_ref[:, lanes] + blend(parts, high_ref, mix_ref, p)
        for q in range(2):
            part = total[:, q * fields : (q + 1) * fields] + centre_ref[p + q : p + q + 1, :]
            all_ref[pl.ds(p + q, members, stride=patches), :] = part
    chunk = 32
    for k in range(0, members, chunk):
        part = all_ref[k * patches : (k + chunk) * patches, :]
        out_ref[k : k + chunk] = part.reshape(chunk, patches, fields).astype(BF16)


def entry_kernel(*refs):
    small, source_ref, target_ref, results = refs[:7], refs[7], refs[8], refs[9:12]
    copied, loaded, read = refs[12:19], refs[19], refs[20]
    fetch = [pltpu.make_async_copy(a, b, loaded.at[i]) for i, (a, b) in enumerate(zip(small, copied))]
    inward = [pltpu.make_async_copy(source_ref.at[m], target_ref.at[:, m], read.at[m]) for m in range(source_ref.shape[0])]
    for copy in fetch + inward:
        copy.start()
    for copy in fetch:
        copy.wait()
    prepare(*copied, *results)
    for copy in inward:
        copy.wait()


def returned_kernel(source_ref, target_ref, done):
    copies = [pltpu.make_async_copy(source_ref.at[:, m], target_ref.at[m], done.at[m]) for m in range(target_ref.shape[0])]
    for copy in copies:
        copy.start()
    for copy in copies:
        copy.wait()


def call(kernel, outs, specs, scratch=(), to=VMEM):
    return pl.pallas_call(
        kernel,
        out_shape=outs,
        in_specs=specs,
        out_specs=jax.tree.map(lambda _: to, outs),
        scratch_shapes=list(scratch),
        compiler_params=pltpu.CompilerParams(vmem_limit_bytes=32 << 20),
    )


def per_device(background, obs_value, obs_error, obs_patch, obs_variable, obs_count, patch_corners, interp_weights):
    shape = jax.ShapeDtypeStruct
    devices = lax.axis_size("mem")
    regions = lax.axis_size("reg")
    own, _, all_patches, fields = background.shape
    patches = all_patches // devices
    members = own * devices
    points = obs_value.shape[0] * obs_value.shape[1]
    columns = patches * fields
    copies = [pltpu.SemaphoreType.DMA((own,))]

    blocks = (devices, own, patches, fields)
    small = (obs_count, obs_value, obs_error, obs_patch, obs_variable, patch_corners[0].T, interp_weights[0].T)
    given = [pltpu.with_memory_space_constraint(x, pltpu.HBM) for x in small + (background.reshape(own, devices, patches, fields),)]
    sums = (points, patches, fields)
    outgoing, dense, values, mix = pl.pallas_call(
        entry_kernel,
        out_shape=(shape(blocks, BF16), shape(sums, F32), shape(sums, F32), shape((9, patches, fields), F32)),
        in_specs=[HBM] * 8,
        out_specs=(VMEM, VMEM, VMEM, VMEM),
        scratch_shapes=[pltpu.VMEM(x.shape, x.dtype) for x in small]
        + [pltpu.SemaphoreType.DMA((len(small),)), pltpu.SemaphoreType.DMA((own,))],
        compiler_params=pltpu.CompilerParams(vmem_limit_bytes=32 << 20),
    )(*given)
    ensemble = lax.all_to_all(outgoing, "mem", split_axis=0, concat_axis=0, tiled=True).reshape(members, patches, fields)

    packed = (members // 2 + 16, members)
    left = (members + 16, columns)
    flat = (members, columns)
    wide = pltpu.VMEM((members * patches, fields), F32)
    down = [((d + 1) % devices, d) for d in range(devices)]
    across = [(r + 1, r) for r in range(regions - 1)]
    both = [(d * regions + r, e * regions + t) for d, e in down for r, t in across]
    one, to_beside, to_corner, to_below, x, pert, high, centre = call(
        first_kernel,
        (
            shape((3, members, members), BF16),
            shape((2,) + packed, BF16),
            shape((1,) + packed, BF16),
            shape((2,) + packed, BF16),
            shape(flat, BF16),
            shape(flat, F32),
            shape(flat, BF16),
            shape((patches, fields), F32),
        ),
        [VMEM] * 3,
        [wide] + [pltpu.VMEM((3,) + left, BF16)] * 2,
    )(ensemble, dense, values)
    beside = lax.ppermute(to_beside, "reg", across)
    diagonal = lax.ppermute(to_corner, ("mem", "reg"), both)
    below = lax.ppermute(to_below, "mem", down)
    partial, two = call(
        second_kernel,
        (shape(flat, F32), shape((1, members, members), BF16)),
        [VMEM] * 8,
        [pltpu.VMEM((1,) + left, BF16)] * 2,
    )(x, pert, centre, dense, values, one, high, mix)
    partial = call(middle_kernel, shape(flat, F32), [VMEM] * 5, [pltpu.VMEM((2, members, members), BF16)])(
        beside, two, high, mix, partial
    )
    analysis = call(
        last_kernel,
        shape((members, patches, fields), BF16),
        [VMEM] * 6,
        [wide, pltpu.VMEM((3, members, members), BF16)],
    )(below, diagonal, high, mix, partial, centre)
    returned = lax.all_to_all(analysis.reshape(devices, own, patches, fields), "mem", split_axis=0, concat_axis=0, tiled=True)
    result = call(returned_kernel, shape((own, devices, patches, fields), BF16), [VMEM], copies, HBM)(returned)
    return result.reshape(own, 1, all_patches, fields)


def solution(mesh):
    placed = (
        P("mem", "reg", None, None),
        P("mem", "reg", None),
        P("mem", "reg", None),
        P("mem", "reg", None),
        P("mem", "reg", None),
        P("mem", "reg"),
        P("reg", "mem", None),
        P("reg", "mem", None),
    )
    return jax.shard_map(
        per_device,
        mesh=mesh,
        in_specs=placed,
        out_specs=P("mem", "reg", None, None),
        check_vma=False,
    )
```

```python
import jax
import jax.numpy as jnp
from jax import lax
from jax.experimental import pallas as pl
from jax.experimental.pallas import tpu as pltpu
from jax.sharding import PartitionSpec as P


F32 = jnp.float32
BF16 = jnp.bfloat16
VMEM = pl.BlockSpec(memory_space=pltpu.VMEM)
HBM = pl.BlockSpec(memory_space=pltpu.HBM)
NN = (((1,), (0,)), ((), ()))
NT = (((1,), (1,)), ((), ()))


def dot(a, b, dims=NN):
    return lax.dot_general(a, b, dims, preferred_element_type=F32)


def split(x):
    high = x.astype(BF16)
    return high, (x - high.astype(F32)).astype(BF16)


def thirds(x):
    high = x.astype(BF16)
    rest = x - high.astype(F32)
    middle = rest.astype(BF16)
    return high, middle, (rest - middle.astype(F32)).astype(BF16)


def product(a, b):
    return dot(a[0], b[0]) + (dot(a[0], b[1]) + dot(a[1], b[0]))


def prepare(count_ref, value_ref, error_ref, patch_ref, var_ref, corner_ref, coeff_ref, dense_ref, value_out_ref, mix_ref):
    rows, cols, slots = value_ref.shape
    patches, fields = dense_ref.shape[1:]
    slot_index = lax.broadcasted_iota(jnp.int32, (1, slots), 1)
    field_index = lax.broadcasted_iota(jnp.int32, (fields, slots), 0)
    patch_index = lax.broadcasted_iota(jnp.int32, (patches, slots), 0)
    for a in range(rows):
        for b in range(cols):
            weight = jnp.where(slot_index < count_ref[a : a + 1, b : b + 1], 1.0 / error_ref[a, b : b + 1, :], 0.0)
            weighted = weight * value_ref[a, b : b + 1, :]
            chosen = (field_index == var_ref[a, b : b + 1, :]).astype(F32).astype(BF16)
            at_patch = patch_index == patch_ref[a, b : b + 1, :]
            left = jnp.concatenate([jnp.where(at_patch, x, 0.0) for x in (weight, weighted)], axis=0)
            high, middle, low = (dot(x, chosen, NT) for x in thirds(left))
            sums = high + (middle + low)
            dense_ref[a * cols + b] = sums[:patches]
            value_out_ref[a * cols + b] = sums[patches:]
    corners, coeffs = corner_ref[...], coeff_ref[...]
    square = (patches, patches)
    own_place = lax.broadcasted_iota(jnp.int32, square, 0) == lax.broadcasted_iota(jnp.int32, square, 1)
    for t in range(mix_ref.shape[0]):
        used = jnp.sum(jnp.where(corners == t, coeffs, 0.0), axis=0, keepdims=True)
        column = jnp.sum(jnp.where(own_place, used, 0.0), axis=1, keepdims=True)
        mix_ref[t] = jnp.broadcast_to(column, (patches, fields))


def shares(points, pert_ref, centre, dense_ref, value_ref, left_high, left_low):
    members = pert_ref.shape[0]
    patches, fields = centre.shape
    pulls = [value_ref[n] - dense_ref[n] * centre for n in points]
    for slot, n in enumerate(points):
        for p in range(patches):
            lanes = slice(p * fields, (p + 1) * fields)
            left_high[slot, :members, lanes], left_low[slot, :members, lanes] = split(pert_ref[:, lanes] * dense_ref[n, p : p + 1, :])
            tail = jnp.broadcast_to(pulls[slot][p : p + 1, :], (left_high.shape[1] - members, fields))
            left_high[slot, members:, lanes], left_low[slot, members:, lanes] = split(tail)


def add_diagonal(x, value, diagonal):
    half = diagonal.shape[0]
    step = jnp.where(diagonal, value, 0.0)
    top = jnp.concatenate([x[:half, :half] + step, x[:half, half:]], axis=1)
    bottom = jnp.concatenate([x[half:, :half], x[half:, half:] + step], axis=1)
    return jnp.concatenate([top, bottom], axis=0)


def two_factors(x, parts, diagonal):
    square = product(parts, parts)
    inner = add_diagonal(square - 4.5 * x, 6.75, diagonal)
    return add_diagonal(product(split(square), split(inner)) - 4.875 * x, 2.25, diagonal)


def later_factors(x):
    rounded = x.astype(BF16)
    square = dot(rounded, rounded)
    return 1.5 * square - x + dot(square.astype(BF16), (square - 2.5 * x).astype(BF16))


def weights_of(count, x_ref, left_high, left_low, out_ref, fill=lambda: None):
    members = x_ref.shape[0]
    half = members // 2
    row = lax.broadcasted_iota(jnp.int32, (half, half), 0)
    col = lax.broadcasted_iota(jnp.int32, (half, half), 1)
    diagonal = row == col
    slots = range(count)
    state = []
    for slot in slots:
        columns = x_ref[...]
        both = dot(left_high[slot], columns, NT) + dot(left_low[slot], columns, NT)
        both = both - jnp.sum(both, axis=1, keepdims=True) * (1.0 / members)
        gram, projected = both[:members], both[members : members + 1]
        on_diagonal = jnp.where(diagonal, gram[:half, :half] + gram[half:, half:], 0.0)
        trace = jnp.sum(jnp.sum(on_diagonal, axis=0, keepdims=True), axis=1, keepdims=True)
        scaling = (members - 1.0) + trace / members
        half_inverse = 0.5 / scaling
        state.append((projected, scaling, add_diagonal(gram * half_inverse, (members - 1.0) * half_inverse, diagonal)))
    parts = [split(x) for _, _, x in state]
    roots = [two_factors(state[s][2], parts[s], diagonal) for s in slots]
    fill()
    z = [split(x) for x in roots]
    y = [split(product(parts[s], z[s])) for s in slots]
    fill()
    excess = [add_diagonal(product(y[s], z[s]), -0.5, diagonal) for s in slots]
    fill()
    rest = [later_factors(x) for x in excess]
    fill()
    inverses = [roots[s] + rest[s] + dot(rest[s].astype(BF16), add_diagonal(roots[s], -1.0, diagonal).astype(BF16)) for s in slots]
    for slot in slots:
        projected, scaling, _ = state[slot]
        inverse = inverses[slot]
        once = jnp.sum(inverse * projected, axis=1, keepdims=True)
        twice = jnp.sum(inverse * once, axis=0, keepdims=True) / scaling
        spread = jnp.sqrt((members - 1.0) / scaling) * inverse
        out_ref[slot] = (spread + twice).astype(BF16)
        yield slot, spread, twice


def pack(target, slot, spread, twice):
    members = spread.shape[0]
    half = members // 2
    small_row = lax.broadcasted_iota(jnp.int32, (half, half), 0)
    small_col = lax.broadcasted_iota(jnp.int32, (half, half), 1)
    tail_row = lax.broadcasted_iota(jnp.int32, (8, members), 0)
    corner = spread[half:, half:]
    target[slot, :half, :half] = jnp.where(small_row >= small_col, spread[:half, :half], corner).astype(BF16)
    target[slot, :half, half:] = spread[:half, half:].astype(BF16)
    on_diagonal = jnp.sum(jnp.where(small_row == small_col, corner, 0.0), axis=0, keepdims=True)
    high, low = split(twice)
    rows = jnp.where(tail_row == 1, high.astype(F32), jnp.where(tail_row == 2, low.astype(F32), 0.0))
    first = jnp.concatenate([on_diagonal, jnp.zeros_like(on_diagonal)], axis=1)
    target[slot, half:, :] = jnp.where(tail_row == 0, first, rows).astype(BF16)


def unpack(source, slot, target, place):
    half = source.shape[1] - 8
    row = lax.broadcasted_iota(jnp.int32, (half, half), 0)
    col = lax.broadcasted_iota(jnp.int32, (half, half), 1)
    mixed = source[slot, :half, :half].astype(F32)
    across = source[slot, :half, half:].astype(F32)
    tail = source[slot, half:, :].astype(F32)
    mean = tail[1:2] + tail[2:3]
    left, right = mean[:, :half], mean[:, half:]
    turned = mixed.T
    target[place, :half, :half] = (jnp.where(row >= col, mixed, turned) + left).astype(BF16)
    target[place, :half, half:] = (across + right).astype(BF16)
    target[place, half:, :half] = (across.T + left).astype(BF16)
    corner = jnp.where(row < col, mixed, jnp.where(row == col, tail[0:1, :half], turned))
    target[place, half:, half:] = (corner + right).astype(BF16)


def first_kernel(*refs):
    ensemble_ref, small, sums = refs[0], refs[1:8], refs[8:11]
    out_ref, beside_ref, corner_ref, below_ref, x_ref, pert_ref, high_ref, centre_ref, wide_ref, left_high, left_low = refs[11:]
    dense_ref, value_ref, _ = sums
    prepare(*small, *sums)
    members, patches, fields = ensemble_ref.shape
    total = jnp.zeros((patches, fields), F32)
    chunk = 32
    for k in range(0, members, chunk):
        part = ensemble_ref[k : k + chunk].astype(F32)
        total = total + jnp.sum(part, axis=0)
        wide_ref[k * patches : (k + chunk) * patches] = part.reshape(chunk * patches, fields)
    centre = total * (1.0 / members)
    centre_ref[...] = centre
    for p in range(patches):
        lanes = slice(p * fields, (p + 1) * fields)
        part = wide_ref[pl.ds(p, members, stride=patches), :]
        x_ref[:, lanes] = part.astype(BF16)
        pert = part - centre[p : p + 1, :]
        pert_ref[:, lanes] = pert
        high_ref[:, lanes] = pert.astype(BF16)
    shares((0, 1, 2), pert_ref, centre, dense_ref, value_ref, left_high, left_low)
    for slot, spread, twice in weights_of(3, x_ref, left_high, left_low, out_ref):
        if slot == 0:
            pack(corner_ref, 0, spread, twice)
            beside_ref[0] = corner_ref[0]
            below_ref[0] = corner_ref[0]
        else:
            pack(below_ref if slot == 1 else beside_ref, 1, spread, twice)


def second_kernel(x_ref, pert_ref, centre_ref, dense_ref, value_ref, one_ref, high_ref, mix_ref, out_ref, two_ref, left_high, left_low):
    patches, fields = centre_ref.shape
    tiles = iter(range(0, patches, 2))

    def fill():
        p = next(tiles)
        parts = ((0, one_ref, 0), (1, one_ref, 1), (3, one_ref, 2))
        out_ref[:, p * fields : (p + 2) * fields] = blend(parts, high_ref, mix_ref, p)

    shares((3,), pert_ref, centre_ref[...], dense_ref, value_ref, left_high, left_low)
    for _ in weights_of(1, x_ref, left_high, left_low, two_ref, fill):
        pass


def blend(parts, high_ref, mix_ref, p):
    fields = mix_ref.shape[2]
    lanes = slice(p * fields, (p + 2) * fields)
    total = None
    for t, ref, slot in parts:
        share = jnp.concatenate([mix_ref[t, p : p + 1, :], mix_ref[t, p + 1 : p + 2, :]], axis=1)
        moved = dot(ref[slot], high_ref[:, lanes])
        moved = jnp.where(share != 0.0, share * moved, 0.0)
        total = moved if total is None else total + moved
    return total


def arrivals(arrived, whole_ref):
    for place, (_, ref, slot) in enumerate(arrived):
        unpack(ref, slot, whole_ref, place)
    return [(t, whole_ref, place) for place, (t, _, _) in enumerate(arrived)]


def middle_kernel(beside_ref, below_ref, two_ref, high_ref, mix_ref, partial_ref, out_ref, whole_ref):
    parts = arrivals(((2, beside_ref, 0), (5, beside_ref, 1), (6, below_ref, 0), (7, below_ref, 1)), whole_ref) + [(4, two_ref, 0)]
    fields = mix_ref.shape[2]
    for p in range(0, mix_ref.shape[1], 2):
        lanes = slice(p * fields, (p + 2) * fields)
        out_ref[:, lanes] = partial_ref[:, lanes] + blend(parts, high_ref, mix_ref, p)


def last_kernel(diagonal_ref, high_ref, mix_ref, partial_ref, centre_ref, out_ref, all_ref, whole_ref):
    parts = arrivals(((8, diagonal_ref, 0),), whole_ref)
    members, patches, fields = out_ref.shape
    for p in range(0, patches, 2):
        lanes = slice(p * fields, (p + 2) * fields)
        total = partial_ref[:, lanes] + blend(parts, high_ref, mix_ref, p)
        for q in range(2):
            part = total[:, q * fields : (q + 1) * fields] + centre_ref[p + q : p + q + 1, :]
            all_ref[pl.ds(p + q, members, stride=patches), :] = part
    chunk = 32
    for k in range(0, members, chunk):
        part = all_ref[k * patches : (k + chunk) * patches, :]
        out_ref[k : k + chunk] = part.reshape(chunk, patches, fields).astype(BF16)


def entry_kernel(*refs):
    source_ref, small, target_ref, copied, read, loaded = refs[0], refs[1:8], refs[8], refs[9:16], refs[16], refs[17]
    copies = [pltpu.make_async_copy(a, b, loaded.at[i]) for i, (a, b) in enumerate(zip(small, copied))]
    copies += [pltpu.make_async_copy(source_ref.at[m], target_ref.at[:, m], read.at[m]) for m in range(source_ref.shape[0])]
    for copy in copies:
        copy.start()
    for copy in copies:
        copy.wait()


def returned_kernel(source_ref, target_ref, done):
    copies = [pltpu.make_async_copy(source_ref.at[:, m], target_ref.at[m], done.at[m]) for m in range(target_ref.shape[0])]
    for copy in copies:
        copy.start()
    for copy in copies:
        copy.wait()


def call(kernel, outs, specs, scratch=(), to=VMEM):
    return pl.pallas_call(
        kernel,
        out_shape=outs,
        in_specs=specs,
        out_specs=jax.tree.map(lambda _: to, outs),
        scratch_shapes=list(scratch),
        compiler_params=pltpu.CompilerParams(vmem_limit_bytes=32 << 20),
    )


def per_device(background, obs_value, obs_error, obs_patch, obs_variable, obs_count, patch_corners, interp_weights):
    shape = jax.ShapeDtypeStruct
    devices = lax.axis_size("mem")
    regions = lax.axis_size("reg")
    own, _, all_patches, fields = background.shape
    patches = all_patches // devices
    members = own * devices
    points = obs_value.shape[0] * obs_value.shape[1]
    columns = patches * fields
    copies = [pltpu.SemaphoreType.DMA((own,))]

    blocks = (devices, own, patches, fields)
    small = (obs_count, obs_value, obs_error, obs_patch, obs_variable, patch_corners[0].T, interp_weights[0].T)
    sums = (points, patches, fields)
    given = [pltpu.with_memory_space_constraint(x, pltpu.HBM) for x in (background.reshape(own, devices, patches, fields),) + small]
    outgoing, *small = call(
        entry_kernel,
        (shape(blocks, BF16),) + tuple(shape(x.shape, x.dtype) for x in small),
        [HBM] * 8,
        copies + [pltpu.SemaphoreType.DMA((len(small),))],
    )(*given)
    ensemble = lax.all_to_all(outgoing, "mem", split_axis=0, concat_axis=0, tiled=True).reshape(members, patches, fields)

    packed = (members // 2 + 8, members)
    left = (members + 16, columns)
    flat = (members, columns)
    wide = pltpu.VMEM((members * patches, fields), F32)
    down = [((d + 1) % devices, d) for d in range(devices)]
    across = [(r + 1, r) for r in range(regions - 1)]
    both = [(d * regions + r, e * regions + t) for d, e in down for r, t in across]
    dense, values, mix, one, to_beside, to_corner, to_below, x, pert, high, centre = call(
        first_kernel,
        (
            shape(sums, F32),
            shape(sums, F32),
            shape((9, patches, fields), F32),
            shape((3, members, members), BF16),
            shape((2,) + packed, BF16),
            shape((1,) + packed, BF16),
            shape((2,) + packed, BF16),
            shape(flat, BF16),
            shape(flat, F32),
            shape(flat, BF16),
            shape((patches, fields), F32),
        ),
        [VMEM] * 8,
        [wide] + [pltpu.VMEM((3,) + left, BF16)] * 2,
    )(ensemble, *small)
    beside = lax.ppermute(to_beside, "reg", across)
    diagonal = lax.ppermute(to_corner, ("mem", "reg"), both)
    below = lax.ppermute(to_below, "mem", down)
    partial, two = call(
        second_kernel,
        (shape(flat, F32), shape((1, members, members), BF16)),
        [VMEM] * 8,
        [pltpu.VMEM((1,) + left, BF16)] * 2,
    )(x, pert, centre, dense, values, one, high, mix)
    partial = call(middle_kernel, shape(flat, F32), [VMEM] * 6, [pltpu.VMEM((4, members, members), BF16)])(
        beside, below, two, high, mix, partial
    )
    analysis = call(
        last_kernel,
        shape((members, patches, fields), BF16),
        [VMEM] * 5,
        [wide, pltpu.VMEM((1, members, members), BF16)],
    )(diagonal, high, mix, partial, centre)
    returned = lax.all_to_all(analysis.reshape(devices, own, patches, fields), "mem", split_axis=0, concat_axis=0, tiled=True)
    result = call(returned_kernel, shape((own, devices, patches, fields), BF16), [VMEM], copies, HBM)(returned)
    return result.reshape(own, 1, all_patches, fields)


def solution(mesh):
    placed = (
        P("mem", "reg", None, None),
        P("mem", "reg", None),
        P("mem", "reg", None),
        P("mem", "reg", None),
        P("mem", "reg", None),
        P("mem", "reg"),
        P("reg", "mem", None),
        P("reg", "mem", None),
    )
    return jax.shard_map(
        per_device,
        mesh=mesh,
        in_specs=placed,
        out_specs=P("mem", "reg", None, None),
        check_vma=False,
    )
```

```python
import jax
import jax.numpy as jnp
from jax import lax
from jax.experimental import pallas as pl
from jax.experimental.pallas import tpu as pltpu
from jax.sharding import PartitionSpec as P


F32 = jnp.float32
BF16 = jnp.bfloat16
VMEM = pl.BlockSpec(memory_space=pltpu.VMEM)
HBM = pl.BlockSpec(memory_space=pltpu.HBM)
NN = (((1,), (0,)), ((), ()))
NT = (((1,), (1,)), ((), ()))


def dot(a, b, dims=NN):
    return lax.dot_general(a, b, dims, preferred_element_type=F32)


def split(x):
    high = x.astype(BF16)
    return high, (x - high.astype(F32)).astype(BF16)


def thirds(x):
    high = x.astype(BF16)
    rest = x - high.astype(F32)
    middle = rest.astype(BF16)
    return high, middle, (rest - middle.astype(F32)).astype(BF16)


def product(a, b):
    return dot(a[0], b[0]) + (dot(a[0], b[1]) + dot(a[1], b[0]))


def prepare(chosen_points, count_ref, value_ref, error_ref, patch_ref, var_ref, dense_ref, value_out_ref):
    rows, cols, slots = value_ref.shape
    patches, fields = dense_ref.shape[1:]
    slot_index = lax.broadcasted_iota(jnp.int32, (1, slots), 1)
    field_index = lax.broadcasted_iota(jnp.int32, (fields, slots), 0)
    patch_index = lax.broadcasted_iota(jnp.int32, (patches, slots), 0)
    for a in range(rows):
        for b in range(cols):
            if a * cols + b not in chosen_points:
                continue
            weight = jnp.where(slot_index < count_ref[a : a + 1, b : b + 1], 1.0 / error_ref[a, b : b + 1, :], 0.0)
            weighted = weight * value_ref[a, b : b + 1, :]
            chosen = (field_index == var_ref[a, b : b + 1, :]).astype(F32).astype(BF16)
            at_patch = patch_index == patch_ref[a, b : b + 1, :]
            left = jnp.concatenate([jnp.where(at_patch, x, 0.0) for x in (weight, weighted)], axis=0)
            high, middle, low = (dot(x, chosen, NT) for x in thirds(left))
            sums = high + (middle + low)
            dense_ref[a * cols + b] = sums[:patches]
            value_out_ref[a * cols + b] = sums[patches:]


def mix(corner_ref, coeff_ref, mix_ref):
    patches, fields = mix_ref.shape[1:]
    corners, coeffs = corner_ref[...], coeff_ref[...]
    square = (patches, patches)
    own_place = lax.broadcasted_iota(jnp.int32, square, 0) == lax.broadcasted_iota(jnp.int32, square, 1)
    for t in range(mix_ref.shape[0]):
        used = jnp.sum(jnp.where(corners == t, coeffs, 0.0), axis=0, keepdims=True)
        column = jnp.sum(jnp.where(own_place, used, 0.0), axis=1, keepdims=True)
        mix_ref[t] = jnp.broadcast_to(column, (patches, fields))


def shares(points, pert_ref, centre, dense_ref, value_ref, left_high, left_low):
    members = pert_ref.shape[0]
    patches, fields = centre.shape
    pulls = [value_ref[n] - dense_ref[n] * centre for n in points]
    for slot, n in enumerate(points):
        for p in range(patches):
            lanes = slice(p * fields, (p + 1) * fields)
            left_high[slot, :members, lanes], left_low[slot, :members, lanes] = split(pert_ref[:, lanes] * dense_ref[n, p : p + 1, :])
            tail = jnp.broadcast_to(pulls[slot][p : p + 1, :], (left_high.shape[1] - members, fields))
            left_high[slot, members:, lanes], left_low[slot, members:, lanes] = split(tail)


def add_diagonal(x, value, diagonal):
    half = diagonal.shape[0]
    step = jnp.where(diagonal, value, 0.0)
    top = jnp.concatenate([x[:half, :half] + step, x[:half, half:]], axis=1)
    bottom = jnp.concatenate([x[half:, :half], x[half:, half:] + step], axis=1)
    return jnp.concatenate([top, bottom], axis=0)


def two_factors(x, parts, diagonal):
    square = product(parts, parts)
    inner = add_diagonal(square - 4.5 * x, 6.75, diagonal)
    return add_diagonal(product(split(square), split(inner)) - 4.875 * x, 2.25, diagonal)


def later_factors(x):
    rounded = x.astype(BF16)
    square = dot(rounded, rounded)
    return 1.5 * square - x + dot(square.astype(BF16), (square - 2.5 * x).astype(BF16))


def weights_of(count, x_ref, left_high, left_low, out_ref, fill=lambda: None):
    members = x_ref.shape[0]
    half = members // 2
    row = lax.broadcasted_iota(jnp.int32, (half, half), 0)
    col = lax.broadcasted_iota(jnp.int32, (half, half), 1)
    diagonal = row == col
    slots = range(count)
    state = []
    for slot in slots:
        columns = x_ref[...]
        both = dot(left_high[slot], columns, NT) + dot(left_low[slot], columns, NT)
        both = both - jnp.sum(both, axis=1, keepdims=True) * (1.0 / members)
        gram, projected = both[:members], both[members : members + 1]
        on_diagonal = jnp.where(diagonal, gram[:half, :half] + gram[half:, half:], 0.0)
        trace = jnp.sum(jnp.sum(on_diagonal, axis=0, keepdims=True), axis=1, keepdims=True)
        scaling = (members - 1.0) + trace / members
        half_inverse = 0.5 / scaling
        state.append((projected, scaling, add_diagonal(gram * half_inverse, (members - 1.0) * half_inverse, diagonal)))
    parts = [split(x) for _, _, x in state]
    roots = [two_factors(state[s][2], parts[s], diagonal) for s in slots]
    fill()
    z = [split(x) for x in roots]
    y = [split(product(parts[s], z[s])) for s in slots]
    fill()
    excess = [add_diagonal(product(y[s], z[s]), -0.5, diagonal) for s in slots]
    fill()
    rest = [later_factors(x) for x in excess]
    fill()
    inverses = [roots[s] + rest[s] + dot(rest[s].astype(BF16), add_diagonal(roots[s], -1.0, diagonal).astype(BF16)) for s in slots]
    for slot in slots:
        projected, scaling, _ = state[slot]
        inverse = inverses[slot]
        once = jnp.sum(inverse * projected, axis=1, keepdims=True)
        twice = jnp.sum(inverse * once, axis=0, keepdims=True) / scaling
        spread = jnp.sqrt((members - 1.0) / scaling) * inverse
        out_ref[slot] = (spread + twice).astype(BF16)
        yield slot, spread, twice


def pack(target, slot, spread, twice):
    members = spread.shape[0]
    half = members // 2
    small_row = lax.broadcasted_iota(jnp.int32, (half, half), 0)
    small_col = lax.broadcasted_iota(jnp.int32, (half, half), 1)
    tail_row = lax.broadcasted_iota(jnp.int32, (8, members), 0)
    corner = spread[half:, half:]
    target[slot, :half, :half] = jnp.where(small_row >= small_col, spread[:half, :half], corner).astype(BF16)
    target[slot, :half, half:] = spread[:half, half:].astype(BF16)
    on_diagonal = jnp.sum(jnp.where(small_row == small_col, corner, 0.0), axis=0, keepdims=True)
    high, low = split(twice)
    rows = jnp.where(tail_row == 1, high.astype(F32), jnp.where(tail_row == 2, low.astype(F32), 0.0))
    first = jnp.concatenate([on_diagonal, jnp.zeros_like(on_diagonal)], axis=1)
    target[slot, half:, :] = jnp.where(tail_row == 0, first, rows).astype(BF16)


def unpack(source, slot, target, place):
    half = source.shape[1] - 8
    row = lax.broadcasted_iota(jnp.int32, (half, half), 0)
    col = lax.broadcasted_iota(jnp.int32, (half, half), 1)
    mixed = source[slot, :half, :half].astype(F32)
    across = source[slot, :half, half:].astype(F32)
    tail = source[slot, half:, :].astype(F32)
    mean = tail[1:2] + tail[2:3]
    left, right = mean[:, :half], mean[:, half:]
    turned = mixed.T
    target[place, :half, :half] = (jnp.where(row >= col, mixed, turned) + left).astype(BF16)
    target[place, :half, half:] = (across + right).astype(BF16)
    target[place, half:, :half] = (across.T + left).astype(BF16)
    corner = jnp.where(row < col, mixed, jnp.where(row == col, tail[0:1, :half], turned))
    target[place, half:, half:] = (corner + right).astype(BF16)


def first_kernel(*refs):
    ensemble_ref, small = refs[0], refs[1:6]
    out_ref, beside_ref, corner_ref, below_ref, x_ref, pert_ref, high_ref, centre_ref, dense_ref, value_ref, wide_ref, left_high, left_low = refs[6:]
    prepare((0, 1, 2), *small, dense_ref, value_ref)
    members, patches, fields = ensemble_ref.shape
    total = jnp.zeros((patches, fields), F32)
    chunk = 32
    for k in range(0, members, chunk):
        part = ensemble_ref[k : k + chunk].astype(F32)
        total = total + jnp.sum(part, axis=0)
        wide_ref[k * patches : (k + chunk) * patches] = part.reshape(chunk * patches, fields)
    centre = total * (1.0 / members)
    centre_ref[...] = centre
    for p in range(patches):
        lanes = slice(p * fields, (p + 1) * fields)
        part = wide_ref[pl.ds(p, members, stride=patches), :]
        x_ref[:, lanes] = part.astype(BF16)
        pert = part - centre[p : p + 1, :]
        pert_ref[:, lanes] = pert
        high_ref[:, lanes] = pert.astype(BF16)
    shares((0, 1, 2), pert_ref, centre, dense_ref, value_ref, left_high, left_low)
    for slot, spread, twice in weights_of(3, x_ref, left_high, left_low, out_ref):
        if slot == 0:
            pack(corner_ref, 0, spread, twice)
            beside_ref[0] = corner_ref[0]
            below_ref[0] = corner_ref[0]
        else:
            pack(below_ref if slot == 1 else beside_ref, 1, spread, twice)


def second_kernel(*refs):
    x_ref, pert_ref, centre_ref, one_ref, high_ref = refs[:5]
    small, out_ref, two_ref, mix_ref, dense_ref, value_ref, left_high, left_low = refs[5:12], *refs[12:]
    prepare((3,), *small[:5], dense_ref, value_ref)
    mix(*small[5:], mix_ref)
    patches, fields = centre_ref.shape
    tiles = iter(range(0, patches, 2))

    def fill():
        p = next(tiles)
        parts = ((0, one_ref, 0), (1, one_ref, 1), (3, one_ref, 2))
        out_ref[:, p * fields : (p + 2) * fields] = blend(parts, high_ref, mix_ref, p)

    shares((3,), pert_ref, centre_ref[...], dense_ref, value_ref, left_high, left_low)
    for _ in weights_of(1, x_ref, left_high, left_low, two_ref, fill):
        pass


def blend(parts, high_ref, mix_ref, p):
    fields = mix_ref.shape[2]
    lanes = slice(p * fields, (p + 2) * fields)
    total = None
    for t, ref, slot in parts:
        share = jnp.concatenate([mix_ref[t, p : p + 1, :], mix_ref[t, p + 1 : p + 2, :]], axis=1)
        moved = dot(ref[slot], high_ref[:, lanes])
        moved = jnp.where(share != 0.0, share * moved, 0.0)
        total = moved if total is None else total + moved
    return total


def arrivals(arrived, whole_ref):
    for place, (_, ref, slot) in enumerate(arrived):
        unpack(ref, slot, whole_ref, place)
    return [(t, whole_ref, place) for place, (t, _, _) in enumerate(arrived)]


def middle_kernel(beside_ref, below_ref, two_ref, high_ref, mix_ref, partial_ref, out_ref, whole_ref):
    parts = arrivals(((2, beside_ref, 0), (5, beside_ref, 1), (6, below_ref, 0), (7, below_ref, 1)), whole_ref) + [(4, two_ref, 0)]
    fields = mix_ref.shape[2]
    for p in range(0, mix_ref.shape[1], 2):
        lanes = slice(p * fields, (p + 2) * fields)
        out_ref[:, lanes] = partial_ref[:, lanes] + blend(parts, high_ref, mix_ref, p)


def last_kernel(diagonal_ref, high_ref, mix_ref, partial_ref, centre_ref, out_ref, all_ref, whole_ref):
    parts = arrivals(((8, diagonal_ref, 0),), whole_ref)
    members, patches, fields = out_ref.shape
    for p in range(0, patches, 2):
        lanes = slice(p * fields, (p + 2) * fields)
        total = partial_ref[:, lanes] + blend(parts, high_ref, mix_ref, p)
        for q in range(2):
            part = total[:, q * fields : (q + 1) * fields] + centre_ref[p + q : p + q + 1, :]
            all_ref[pl.ds(p + q, members, stride=patches), :] = part
    chunk = 32
    for k in range(0, members, chunk):
        part = all_ref[k * patches : (k + chunk) * patches, :]
        out_ref[k : k + chunk] = part.reshape(chunk, patches, fields).astype(BF16)


def entry_kernel(*refs):
    source_ref, small, target_ref, copied, read, loaded = refs[0], refs[1:8], refs[8], refs[9:16], refs[16], refs[17]
    copies = [pltpu.make_async_copy(a, b, loaded.at[i]) for i, (a, b) in enumerate(zip(small, copied))]
    copies += [pltpu.make_async_copy(source_ref.at[m], target_ref.at[:, m], read.at[m]) for m in range(source_ref.shape[0])]
    for copy in copies:
        copy.start()
    for copy in copies:
        copy.wait()


def returned_kernel(source_ref, target_ref, done):
    copies = [pltpu.make_async_copy(source_ref.at[:, m], target_ref.at[m], done.at[m]) for m in range(target_ref.shape[0])]
    for copy in copies:
        copy.start()
    for copy in copies:
        copy.wait()


def call(kernel, outs, specs, scratch=(), to=VMEM):
    return pl.pallas_call(
        kernel,
        out_shape=outs,
        in_specs=specs,
        out_specs=jax.tree.map(lambda _: to, outs),
        scratch_shapes=list(scratch),
        compiler_params=pltpu.CompilerParams(vmem_limit_bytes=32 << 20),
    )


def per_device(background, obs_value, obs_error, obs_patch, obs_variable, obs_count, patch_corners, interp_weights):
    shape = jax.ShapeDtypeStruct
    devices = lax.axis_size("mem")
    regions = lax.axis_size("reg")
    own, _, all_patches, fields = background.shape
    patches = all_patches // devices
    members = own * devices
    points = obs_value.shape[0] * obs_value.shape[1]
    columns = patches * fields
    copies = [pltpu.SemaphoreType.DMA((own,))]

    blocks = (devices, own, patches, fields)
    small = (obs_count, obs_value, obs_error, obs_patch, obs_variable, patch_corners[0].T, interp_weights[0].T)
    sums = (points, patches, fields)
    given = [pltpu.with_memory_space_constraint(x, pltpu.HBM) for x in (background.reshape(own, devices, patches, fields),) + small]
    outgoing, *small = call(
        entry_kernel,
        (shape(blocks, BF16),) + tuple(shape(x.shape, x.dtype) for x in small),
        [HBM] * 8,
        copies + [pltpu.SemaphoreType.DMA((len(small),))],
    )(*given)
    ensemble = lax.all_to_all(outgoing, "mem", split_axis=0, concat_axis=0, tiled=True).reshape(members, patches, fields)

    packed = (members // 2 + 8, members)
    left = (members + 16, columns)
    flat = (members, columns)
    wide = pltpu.VMEM((members * patches, fields), F32)
    down = [((d + 1) % devices, d) for d in range(devices)]
    across = [(r + 1, r) for r in range(regions - 1)]
    both = [(d * regions + r, e * regions + t) for d, e in down for r, t in across]
    one, to_beside, to_corner, to_below, x, pert, high, centre = call(
        first_kernel,
        (
            shape((3, members, members), BF16),
            shape((2,) + packed, BF16),
            shape((1,) + packed, BF16),
            shape((2,) + packed, BF16),
            shape(flat, BF16),
            shape(flat, F32),
            shape(flat, BF16),
            shape((patches, fields), F32),
        ),
        [VMEM] * 6,
        [pltpu.VMEM(sums, F32)] * 2 + [wide] + [pltpu.VMEM((3,) + left, BF16)] * 2,
    )(ensemble, *small[:5])
    beside = lax.ppermute(to_beside, "reg", across)
    diagonal = lax.ppermute(to_corner, ("mem", "reg"), both)
    below = lax.ppermute(to_below, "mem", down)
    partial, two, shared = call(
        second_kernel,
        (shape(flat, F32), shape((1, members, members), BF16), shape((9, patches, fields), F32)),
        [VMEM] * 12,
        [pltpu.VMEM(sums, F32)] * 2 + [pltpu.VMEM((1,) + left, BF16)] * 2,
    )(x, pert, centre, one, high, *small)
    partial = call(middle_kernel, shape(flat, F32), [VMEM] * 6, [pltpu.VMEM((4, members, members), BF16)])(
        beside, below, two, high, shared, partial
    )
    analysis = call(
        last_kernel,
        shape((members, patches, fields), BF16),
        [VMEM] * 5,
        [wide, pltpu.VMEM((1, members, members), BF16)],
    )(diagonal, high, shared, partial, centre)
    returned = lax.all_to_all(analysis.reshape(devices, own, patches, fields), "mem", split_axis=0, concat_axis=0, tiled=True)
    result = call(returned_kernel, shape((own, devices, patches, fields), BF16), [VMEM], copies, HBM)(returned)
    return result.reshape(own, 1, all_patches, fields)


def solution(mesh):
    placed = (
        P("mem", "reg", None, None),
        P("mem", "reg", None),
        P("mem", "reg", None),
        P("mem", "reg", None),
        P("mem", "reg", None),
        P("mem", "reg"),
        P("reg", "mem", None),
        P("reg", "mem", None),
    )
    return jax.shard_map(
        per_device,
        mesh=mesh,
        in_specs=placed,
        out_specs=P("mem", "reg", None, None),
        check_vma=False,
    )
```
